32 devices in a mesh: dp: 4 (over z), seq: 4 (over y, x), head: 2 (over core).
Axes of the slice: x: 2, y: 2, z: 4, core: 2. Of those that a mesh axis runs over, the one named last changes fastest.
Arguments:
- block_input: float32 [8, 1024, 1024], P('dp', 'seq', 'head'), may hold values from -6 to 6
- segment_ids: int32 [8, 1024], P('dp', 'seq'), may hold values from 0 to 3, never falling along the last dimension, each value on 1 to 512 neighbouring positions
- mixer_gain: float32 [1024], replicated, may hold values from 0.5 to 1.5
- query_weight: bfloat16 [1024, 1024], P(None, 'head'), may hold values from -0.1875 to 0.1875
- key_weight: bfloat16 [1024, 1024], P(None, 'head'), may hold values from -0.1875 to 0.1875
- value_weight: bfloat16 [1024, 1024], P(None, 'head'), may hold values from -0.1875 to 0.1875
- gate_weight: bfloat16 [1024, 1024], P(None, 'head'), may hold values from -0.1875 to 0.1875
- beta_weight: bfloat16 [1024, 8], P(None, 'head'), may hold values from -0.1875 to 0.1875
- conv_weight: float32 [3, 4, 8, 128], P(None, None, 'head'), may hold values from -3 to 3
- head_gain: float32 [128], replicated, may hold values from 0.5 to 1.5
- out_weight: bfloat16 [1024, 1024], P('head'), may hold values from -0.375 to 0.375
- feed_gain: float32 [1024], replicated, may hold values from 0.5 to 1.5
- feed_gate: bfloat16 [1024, 2816], P(None, 'head'), may hold values from -0.1875 to 0.1875
- feed_up: bfloat16 [1024, 2816], P(None, 'head'), may hold values from -0.1875 to 0.1875
- feed_down: bfloat16 [2816, 1024], P('head'), may hold values from -0.21875 to 0.21875
- grad_output: float32 [8, 1024, 1024], P('dp', 'seq', 'head'), may hold values from -6 to 6
Outputs:
- block_output: float32 [8, 1024, 1024], P('dp', 'seq', 'head')
- input_grad: float32 [8, 1024, 1024], P('dp', 'seq', 'head')
- grad_mixer_gain: float32 [1024], P(('dp', 'seq'))
- grad_query: float32 [1024, 1024], P(('dp', 'seq'), 'head')
- grad_key: float32 [1024, 1024], P(('dp', 'seq'), 'head')
- grad_value: float32 [1024, 1024], P(('dp', 'seq'), 'head')
- grad_gate: float32 [1024, 1024], P(('dp', 'seq'), 'head')
- grad_beta: float32 [1024, 8], P(('dp', 'seq'), 'head')
- grad_conv: float32 [3, 4, 8, 128], P(None, None, 'head', ('dp', 'seq'))
- grad_head_gain: float32 [128], P(('dp', 'seq'))
- grad_out_weight: float32 [1024, 1024], P('head', ('dp', 'seq'))
- grad_feed_gain: float32 [1024], P(('dp', 'seq'))
- grad_feed_gate: float32 [1024, 2816], P(('dp', 'seq'), 'head')
- grad_feed_up: float32 [1024, 2816], P(('dp', 'seq'), 'head')
- grad_feed_down: float32 [2816, 1024], P('head', ('dp', 'seq'))
The draws below stay inside these ranges and needn't reach their ends.
Inputs may be any that keep to these rules, and one draw needn't show every extreme that they name: `segment_ids`: in each sequence the ids never fall; a document is a run of equal ids, and the first token of a sequence starts one.
All inputs are finite; a program needn't handle non-finite values.
Results may differ from the reference program's by a relative error of at most 0.012.
Values sent between devices are 32-bit elements; how exact they have to be, the bound alone decides.
No kernel may reach another device: no remote copies, remote signals or barrier semaphores. Data moves between devices by JAX's collectives and lax.ppermute only.
A program may use at most 192 MiB of HBM per device.

```python
import math
import jax
import jax.numpy as jnp
import numpy as np
from jax import lax

D = 1024
H = 8
DK = 128
FF = 2816
CONV = 4
GROUP = 64
SEQ_LEN = 1024
DOCS = 4
SEQS = 8


def strengthened(values, own_key, source, target, shards_of, factor):
    owner, partner = [(jnp.arange(values.shape[position]) // (values.shape[position] // shards_of)).reshape([-1 if axis == position else 1 for axis in range(values.ndim)]) for position in (source, target)]
    chosen = jax.random.permutation(own_key, shards_of)[partner]
    strong = (owner == chosen) | (owner == (partner + shards_of // 2) % shards_of)
    return jnp.where(strong, factor * values, values)


def level_of(own_key, extent, cuts, low, top_value):
    level = 1.0
    for axis_at, parts in cuts:
        heights = jax.random.uniform(jax.random.fold_in(jax.random.fold_in(own_key, 6), axis_at), (parts,), jnp.float32, low / len(cuts), top_value / len(cuts))
        level = level * jnp.repeat(jnp.exp(heights), extent[axis_at] // parts).reshape((-1,) + (1,) * (len(extent) - 1 - axis_at))
    return level


def split_up(count, total, limit, skew):
    weights = [(1 << 20) // math.isqrt(standing ** skew) + 1 for standing in range(2, count + 1)]
    surplus, holding = total - limit - (count - 1), [1] * (count - 1)
    while surplus > 0:
        movable = [i for i in range(count - 1) if holding[i] < limit]
        mass, remaining = sum([weights[i] for i in movable]), surplus
        for i in movable:
            extra = min(limit - holding[i], max(1, remaining * weights[i] // mass), surplus)
            holding[i] = holding[i] + extra
            surplus = surplus - extra
    return np.array([limit] + holding)


def ragged_sizes(key, count, total, reach, slope):
    if count == 2:
        one = jax.random.randint(key, (), max(1, total - reach), min(reach, total - 1) + 1)
        return jnp.stack([one, total - one])
    lengths = jnp.asarray(split_up(count, total, reach, slope), jnp.int32)
    twos = (count - 1) // 2
    source_of, taker = lengths[1:1 + 2 * twos:2], lengths[2:2 + 2 * twos:2]
    slack = jnp.minimum(source_of - 1, reach - taker)
    passed = jax.random.randint(jax.random.fold_in(key, 1), (twos,), 0, 1 << 20) % (slack + 1)
    lengths = lengths.at[1:1 + 2 * twos:2].set(source_of - passed).at[2:2 + 2 * twos:2].set(taker + passed)
    return lengths[jax.random.permutation(jax.random.fold_in(key, 2), count)]


def gaussian(key, dims, deviation, bound, split=(), kind=jnp.bfloat16):
    values = deviation * jax.random.normal(key, dims, jnp.float32)
    if split:
        values = values * level_of(key, dims, split, -0.22, 0.18)
    return jnp.clip(values, -bound, bound).astype(kind)


def heavy_noise(key, shape, scale, most, cuts, heavy, kind=jnp.bfloat16):
    values = scale * jax.random.normal(key, shape, jnp.float32)
    if cuts:
        values = values * level_of(key, shape, cuts, -0.22, 0.18)
    return jnp.clip(strengthened(values, jax.random.fold_in(key, 3), *heavy), -most, most).astype(kind)


def setup_inputs(seed: int = 0) -> dict:
    seeds = jax.random.split(jax.random.key(seed), 17)
    block_input = gaussian(seeds[0], (SEQS, SEQ_LEN, D), 1.0, 6.0, ((0, 4), (1, 4), (2, 2)), jnp.float32)
    segment_ids = jax.vmap(lambda own: jnp.searchsorted(jnp.cumsum(ragged_sizes(own, DOCS, SEQ_LEN, SEQ_LEN // 2, 2)), jnp.arange(SEQ_LEN), side="right"))(jax.random.split(seeds[1], SEQS)).reshape((SEQS, SEQ_LEN)).astype(jnp.int32)
    mixer_gain = jnp.clip(1.0 + 0.1 * jax.random.normal(seeds[2], (D,), jnp.float32), 0.5, 1.5)
    query_weight = gaussian(seeds[3], (D, H * DK), D ** -0.5, 0.1875, ((1, 2),))
    key_weight = gaussian(seeds[4], (D, H * DK), D ** -0.5, 0.1875, ((1, 2),))
    value_weight = gaussian(seeds[5], (D, H * DK), D ** -0.5, 0.1875, ((1, 2),))
    gate_weight = gaussian(seeds[6], (D, H * DK), D ** -0.5, 0.1875, ((1, 2),))
    beta_weight = gaussian(seeds[7], (D, H), D ** -0.5, 0.1875, ((1, 2),))
    conv_weight = gaussian(seeds[8], (3, CONV, H, DK), CONV ** -0.5, 3.0, ((2, 2),), jnp.float32)
    head_gain = jnp.clip(1.0 + 0.1 * jax.random.normal(seeds[9], (DK,), jnp.float32), 0.5, 1.5)
    out_weight = gaussian(seeds[10], (H * DK, D), (D // 4) ** -0.5, 0.375, ((0, 2),))
    feed_gain = jnp.clip(1.0 + 0.1 * jax.random.normal(seeds[11], (D,), jnp.float32), 0.5, 1.5)
    feed_gate = gaussian(seeds[12], (D, FF), D ** -0.5, 0.1875, ((1, 2),))
    feed_up = gaussian(seeds[13], (D, FF), D ** -0.5, 0.1875, ((1, 2),))
    feed_down = gaussian(seeds[14], (FF, D), (FF // 4) ** -0.5, 0.21875, ((0, 2),))
    grad_output = heavy_noise(seeds[15], (SEQS, SEQ_LEN, D), 1.0, 6.0, ((0, 4), (1, 4), (2, 2)), (1, 2, 4, 2.0), jnp.float32)
    return {"block_input": block_input, "segment_ids": segment_ids, "mixer_gain": mixer_gain, "query_weight": query_weight, "key_weight": key_weight, "value_weight": value_weight, "gate_weight": gate_weight, "beta_weight": beta_weight, "conv_weight": conv_weight, "head_gain": head_gain, "out_weight": out_weight, "feed_gain": feed_gain, "feed_gate": feed_gate, "feed_up": feed_up, "feed_down": feed_down, "grad_output": grad_output}


norm_eps = 1e-05
unit_eps = 1e-06
top_precision = lax.Precision.HIGHEST

@jax.custom_vjp
def low(v):
    return lax.optimization_barrier(v.astype(jnp.bfloat16)).astype(jnp.float32)

@jax.custom_vjp
def low_back(v):
    return v

def low_keep(v):
    return (low(v), None)

def low_pass(kept, grad):
    return (grad,)

def back_keep(v):
    return (v, None)

def back_low(kept, grad):
    return (low(grad),)
low.defvjp(low_keep, low_pass)
low_back.defvjp(back_keep, back_low)

def product(first_op, second_op):
    return jnp.dot(first_op, second_op, precision=top_precision, preferred_element_type=jnp.float32)

def rms_scale(values):
    return lax.rsqrt(lax.optimization_barrier(jnp.mean(values * values, axis=-1, keepdims=True)) + norm_eps)

def unit_rows(values):
    return values * lax.rsqrt(lax.optimization_barrier(jnp.sum(values * values, axis=-1, keepdims=True)) + unit_eps)

def delta_rule(query_heads, key_heads, value_heads, beta_heads, keep_flags):
    length = query_heads.shape[0]

    def token_step(state_now, pieces):
        query_one, key_one, value_one, beta_one, keep_one = pieces
        state_now = state_now * keep_one
        recalled = jnp.einsum('hvk,hk->hv', state_now, key_one, precision=top_precision)
        state_now = state_now + beta_one[:, None, None] * jnp.einsum('hv,hk->hvk', value_one - recalled, key_one, precision=top_precision)
        return (state_now, jnp.einsum('hvk,hk->hv', state_now, query_one, precision=top_precision))

    def block_step(state_now, pieces):
        return lax.scan(token_step, state_now, pieces)
    blocks = length // GROUP
    pieces = tuple((array_item.reshape((blocks, GROUP) + array_item.shape[1:]) for array_item in (query_heads, key_heads, value_heads, beta_heads, keep_flags)))
    start_state = jnp.zeros((H, DK, DK), jnp.float32)
    final_state, outputs = lax.scan(jax.checkpoint(block_step), start_state, pieces)
    return outputs.reshape(length, H, DK)

def block(params, block_input, segment_row):
    mixer_gain, query_weight, key_weight, value_weight, gate_weight, beta_weight, conv_weight, head_gain, out_weight, feed_gain, feed_gate, feed_up, feed_down = params
    length = block_input.shape[0]
    normed_in = low(block_input * rms_scale(block_input) * mixer_gain)
    query_proj = low_back(product(normed_in, query_weight))
    key_proj = low_back(product(normed_in, key_weight))
    value_proj = low_back(product(normed_in, value_weight))
    gate_proj = low_back(product(normed_in, gate_weight))
    beta_logits = low_back(product(normed_in, beta_weight))
    segment_float = segment_row.astype(jnp.float32)
    stacked = jnp.stack([query_proj, key_proj, value_proj])
    conv_taps = conv_weight.reshape(3, CONV, H * DK)
    mixed_sum = jnp.zeros_like(stacked)
    for tap_index in range(CONV):
        delay_rows = CONV - 1 - tap_index
        moved_rows = jnp.pad(stacked, ((0, 0), (delay_rows, 0), (0, 0)))[:, :length]
        moved_ids = jnp.pad(segment_float, (delay_rows, 0), constant_values=-1.0)[:length]
        same_doc = (moved_ids == segment_float).astype(jnp.float32)
        mixed_sum = mixed_sum + conv_taps[:, tap_index, None, :] * moved_rows * same_doc[None, :, None]
    active = jax.nn.silu(mixed_sum).reshape(3, length, H, DK)
    query_heads = low(unit_rows(active[0]) * (1.0 / math.sqrt(DK)))
    key_heads = low(unit_rows(active[1]))
    value_heads = low(active[2])
    beta_heads = jax.nn.sigmoid(beta_logits)
    keep_flags = jnp.concatenate([jnp.zeros((1,), jnp.float32), (segment_float[1:] == segment_float[:-1]).astype(jnp.float32)])
    mix_heads = delta_rule(query_heads, key_heads, value_heads, beta_heads, keep_flags)
    gate_heads = gate_proj.reshape(length, H, DK)
    gated_rows = (mix_heads * rms_scale(mix_heads) * head_gain * jax.nn.silu(gate_heads)).reshape(length, H * DK)
    mixer_out = low_back(product(low(gated_rows), out_weight))
    middle = block_input + mixer_out
    normed_mid = low(middle * rms_scale(middle) * feed_gain)
    gate_act = low_back(product(normed_mid, feed_gate))
    up_act = low_back(product(normed_mid, feed_up))
    inner_low = low(jax.nn.silu(gate_act) * up_act)
    return middle + low_back(product(inner_low, feed_down))

def reference(block_input, segment_ids, mixer_gain, query_weight, key_weight, value_weight, gate_weight, beta_weight, conv_weight, head_gain, out_weight, feed_gain, feed_gate, feed_up, feed_down, grad_output):
    params = tuple((array_item.astype(jnp.float32) for array_item in (mixer_gain, query_weight, key_weight, value_weight, gate_weight, beta_weight, conv_weight, head_gain, out_weight, feed_gain, feed_gate, feed_up, feed_down)))

    def one_sequence(totals, pieces):
        input_row, segment_row, grad_row = pieces
        result, back_fn = jax.vjp(lambda weights, values: block(weights, values, segment_row), params, input_row)
        weight_grads, input_grad = back_fn(grad_row)
        return (tuple((first_op + second_op for first_op, second_op in zip(totals, weight_grads))), (result, input_grad))
    zero_grads = tuple((jnp.zeros_like(array_item) for array_item in params))
    totals, (outputs, input_grads) = lax.scan(one_sequence, zero_grads, (block_input, segment_ids, grad_output))
    return (outputs, input_grads, totals[0], totals[1], totals[2], totals[3], totals[4], totals[5], totals[6], totals[7], totals[8], totals[9], totals[10], totals[11], totals[12])
```

```python
import functools
import math

import jax
import jax.numpy as jnp
from jax import lax
from jax.experimental import pallas as pl
from jax.experimental.pallas import tpu as pltpu
from jax.sharding import PartitionSpec as P

HALO = 16
LONGEST = 512

norm_eps = 1e-05
unit_eps = 1e-06
f32 = jnp.float32
bf16 = jnp.bfloat16
VMEM_LIMIT = 48 * 1024 * 1024


def nn(a, b):
    return lax.dot_general(a, b, (((1,), (0,)), ((), ())), preferred_element_type=f32)


def nt(a, b):
    return lax.dot_general(a, b, (((1,), (1,)), ((), ())), preferred_element_type=f32)


def tn(a, b):
    return lax.dot_general(a, b, (((0,), (0,)), ((), ())), preferred_element_type=f32)


def split(value):
    high = value.astype(bf16)
    return high, (value - high.astype(f32)).astype(bf16)


def nn3(a, b):
    a_high, a_low = a
    b_high, b_low = b
    return nn(a_high, b_high) + nn(a_high, b_low) + nn(a_low, b_high)


def sigmoid(value):
    return 1.0 / (1.0 + jnp.exp(-value))


def rms_scale(values):
    return lax.rsqrt(jnp.mean(values * values, axis=-1, keepdims=True) + norm_eps)


def norm_back(grad_rows, normed, row_scale, gain_vec):
    grad_hat = grad_rows * gain_vec
    return row_scale * (grad_hat - normed * jnp.mean(grad_hat * normed, axis=-1, keepdims=True))


def grid_of(size):
    row = lax.broadcasted_iota(jnp.int32, (size, size), 0)
    return row, lax.broadcasted_iota(jnp.int32, (size, size), 1)


def unit_inverse(lower, size):
    row, col = grid_of(size)
    apart = row ^ col
    inverse = jnp.where(apart == 0, 1.0, 0.0) - jnp.where(apart == 1, lower, 0.0)
    level = 1
    while (1 << level) < size:
        below = jnp.where((apart >> level) == 1, lower, 0.0)
        inverse_parts = split(inverse)
        inverse = inverse - nn3(inverse_parts, split(nn3(split(below), inverse_parts)))
        level += 1
    return inverse


def conv_taps(proj, seq, taps, kind, info, count):
    rows = []
    for tap in range(4):
        moved = proj[seq, HALO - 3 + tap : HALO - 3 + tap + count, :]
        rows.append(moved if tap == 3 else moved * info[seq, :, tap : tap + 1])
    mixed = rows[0] * taps[kind, 0:1, :]
    for tap in range(1, 4):
        mixed = mixed + rows[tap] * taps[kind, tap : tap + 1, :]
    return rows, mixed


def head_column(table, seq, head):
    lane = lax.broadcasted_iota(jnp.int32, table.shape[1:], 1)
    return jnp.sum(jnp.where(lane == head, table[seq], 0.0), axis=1, keepdims=True)


def forward_kernel(
    seqs, count, size,
    query_in, key_in, value_in, taps, info, seg_row, beta,
    query_out, key_out, value_out, inverse_out, fresh_out, carry_out, local_out, reach_out, state_out, transit_out,
):
    head = pl.program_id(0)
    row, col = grid_of(count)
    scale = 1.0 / math.sqrt(size)
    for seq in range(seqs):
        parts = []
        for kind, proj in enumerate((query_in, key_in, value_in)):
            mixed = conv_taps(proj, seq, taps, kind, info, count)[1]
            parts.append(mixed * sigmoid(mixed))
        query, key, value = parts
        query = query * (lax.rsqrt(jnp.sum(query * query, axis=1, keepdims=True) + unit_eps) * scale)
        key = key * lax.rsqrt(jnp.sum(key * key, axis=1, keepdims=True) + unit_eps)
        query, key, value = query.astype(bf16), key.astype(bf16), value.astype(bf16)
        query_out[seq], key_out[seq], value_out[seq] = query, key, value
        enter, last = info[seq, :, 3:4], info[seq, :, 4:5]
        same = info[seq, :, 5:6] == seg_row[seq]
        beta_col = head_column(beta, seq, head)
        key_full = key.astype(f32)
        lower = jnp.where(same & (row > col), nt(key, key) * beta_col, 0.0)
        inverse = unit_inverse(lower, count)
        inverse_parts = split(inverse)
        inverse_out[0, seq] = inverse_parts[0]
        right = jnp.concatenate([key_full * (beta_col * enter), value.astype(f32) * beta_col], axis=1)
        solved = nn3(inverse_parts, split(right))
        solved_high, solved_low = split(solved)
        key_last = (key_full * last).astype(bf16)
        ends = tn(key_last, solved_high) + tn(key_last, solved_low)
        state_out[seq, 0] = ends[:, size:]
        transit_row, transit_col = grid_of(size)
        eye = jnp.where(transit_row == transit_col, 1.0, 0.0)
        transit_out[seq, 0] = eye * info[seq, count - 1 : count, 3:4] - ends[:, :size]
        attend = jnp.where(same & (row >= col), nt(query, key), 0.0).astype(bf16)
        reads = nn(attend, solved_high)
        local_out[seq] = reads[:, size:]
        reach_out[seq] = (query.astype(f32) * enter - reads[:, :size]).astype(bf16)
        carry_out[seq] = solved_high[:, :size]
        fresh_out[seq] = solved[:, size:]


def pl_forward(proj, taps, info, seg_row, beta, first, heads, seqs, count, size, channels):
    def rows(dtype):
        return jax.ShapeDtypeStruct((seqs, count, heads * size), dtype)

    row_spec = pl.BlockSpec((seqs, count, size), lambda h: (0, 0, h))
    proj_spec = pl.BlockSpec((seqs, count + HALO, size), lambda h: (0, 0, h + first))
    state = jax.ShapeDtypeStruct((seqs, heads, size, size), f32)
    state_spec = pl.BlockSpec((seqs, 1, size, size), lambda h: (0, h, 0, 0))
    flops = heads * seqs * (6 * 14 * count**3 + 16 * count * count * size)
    return pl.pallas_call(
        functools.partial(forward_kernel, seqs, count, size),
        grid=(heads,),
        in_specs=[proj_spec] * 3
        + [
            pl.BlockSpec((3, 4, size), lambda h: (0, 0, h + first)),
            pl.BlockSpec(info.shape, lambda h: (0, 0, 0)),
            pl.BlockSpec(seg_row.shape, lambda h: (0, 0, 0)),
            pl.BlockSpec(beta.shape, lambda h: (0, 0, 0)),
        ],
        out_specs=[row_spec] * 3
        + [pl.BlockSpec((1, seqs, count, count), lambda h: (h, 0, 0, 0))]
        + [row_spec] * 4
        + [state_spec] * 2,
        out_shape=[rows(bf16)] * 3
        + [jax.ShapeDtypeStruct((heads, seqs, count, count), bf16)]
        + [rows(f32), rows(bf16), rows(f32), rows(bf16)]
        + [state] * 2,
        compiler_params=pltpu.CompilerParams(vmem_limit_bytes=VMEM_LIMIT),
        cost_estimate=pl.CostEstimate(flops=flops, bytes_accessed=12 << 20, transcendentals=0),
    )(*proj, taps, info, seg_row, beta)


def arrived(hop_refs, seq):
    states, transits = hop_refs
    total = states[-1][seq, 0]
    for state, transit in zip(states[-2::-1], transits[::-1]):
        total = state[seq, 0] + nn3(split(transit[seq, 0]), split(total))
    return total


def read_kernel(seqs, count, size, heads, hops, *refs):
    states, transits = refs[:hops], refs[hops : 2 * hops - 1]
    local, reach, gate, gain, out_weight, state_out, mix_out, gated_out, part_out, held = refs[2 * hops - 1 :]
    head = pl.program_id(0)
    for seq in range(seqs):
        state = arrived((states, transits), seq)
        state_out[seq, 0] = state
        state_high, state_low = split(state)
        moved = reach[seq]
        mix = local[seq] + nn(moved, state_high) + nn(moved, state_low)
        mix_out[seq] = mix
        gate_now = gate[seq]
        gated = (mix * rms_scale(mix) * gain[...] * (gate_now * sigmoid(gate_now))).astype(bf16)
        gated_out[seq] = gated
        held[head, seq * count : (seq + 1) * count, :] = gated

    @pl.when(head == heads - 1)
    def _():
        rows = jnp.concatenate([held[h] for h in range(heads)], axis=1)
        part_out[...] = nn(rows, out_weight[...])


def pl_read(states, transits, local, reach, gate, gain, out_weight, heads, seqs, count, size, width):
    row_spec = pl.BlockSpec((seqs, count, size), lambda h: (0, 0, h))
    state_spec = pl.BlockSpec((seqs, 1, size, size), lambda h: (0, h, 0, 0))
    hops = len(states)
    return pl.pallas_call(
        functools.partial(read_kernel, seqs, count, size, heads, hops),
        grid=(heads,),
        in_specs=[state_spec] * (2 * hops - 1)
        + [row_spec] * 3
        + [pl.BlockSpec((1, size), lambda h: (0, 0)), pl.BlockSpec((heads * size, width), lambda h: (0, 0))],
        out_specs=[state_spec, row_spec, row_spec, pl.BlockSpec((seqs * count, width), lambda h: (0, 0))],
        out_shape=[
            jax.ShapeDtypeStruct((seqs, heads, size, size), f32),
            jax.ShapeDtypeStruct((seqs, count, heads * size), f32),
            jax.ShapeDtypeStruct((seqs, count, heads * size), bf16),
            jax.ShapeDtypeStruct((seqs * count, width), f32),
        ],
        scratch_shapes=[pltpu.VMEM((heads, seqs * count, size), bf16)],
        compiler_params=pltpu.CompilerParams(vmem_limit_bytes=VMEM_LIMIT),
        cost_estimate=pl.CostEstimate(
            flops=2 * seqs * count * heads * size * (width + 2 * size), bytes_accessed=12 << 20, transcendentals=0
        ),
    )(*states, *transits, local, reach, gate, gain, out_weight)


def gate_back_kernel(seqs, count, size, mixer_grad, out_weight, mix, gate, gain, reach, mix_grad, gate_grad, gain_grad, pull):
    head = pl.program_id(0)

    @pl.when(head == 0)
    def _():
        gain_grad[...] = jnp.zeros_like(gain_grad)

    grads = nt(mixer_grad[...], out_weight[...])
    for seq in range(seqs):
        grad = grads[seq * count : (seq + 1) * count]
        mix_now, gate_now = mix[seq], gate[seq]
        scale = rms_scale(mix_now)
        normed = mix_now * scale
        sig = sigmoid(gate_now)
        gate_silu = gate_now * sig
        with_norm = grad * normed
        gain_grad[...] += jnp.sum((with_norm * gate_silu).reshape(count // 8, 8, size), axis=0)
        gate_grad[seq] = (with_norm * gain[...] * (sig * (1.0 + gate_now * (1.0 - sig)))).astype(bf16)
        normed_grad = grad * gain[...] * gate_silu
        mix_grad_now = scale * (normed_grad - normed * jnp.mean(normed_grad * normed, axis=1, keepdims=True))
        low = mix_grad_now.astype(bf16)
        mix_grad[seq] = low
        pull[seq, 0] = tn(reach[seq], low)


def pl_gate_back(mixer_grad, out_weight, mix, gate, gain, reach, heads, seqs, count, size, width):
    row_spec = pl.BlockSpec((seqs, count, size), lambda h: (0, 0, h))
    return pl.pallas_call(
        functools.partial(gate_back_kernel, seqs, count, size),
        grid=(heads,),
        in_specs=[
            pl.BlockSpec((seqs * count, width), lambda h: (0, 0)),
            pl.BlockSpec((size, width), lambda h: (h, 0)),
            row_spec,
            row_spec,
            pl.BlockSpec((1, size), lambda h: (0, 0)),
            row_spec,
        ],
        out_specs=[
            row_spec,
            row_spec,
            pl.BlockSpec((8, size), lambda h: (0, 0)),
            pl.BlockSpec((seqs, 1, size, size), lambda h: (0, h, 0, 0)),
        ],
        out_shape=[
            jax.ShapeDtypeStruct((seqs, count, heads * size), bf16),
            jax.ShapeDtypeStruct((seqs, count, heads * size), bf16),
            jax.ShapeDtypeStruct((8, size), f32),
            jax.ShapeDtypeStruct((seqs, heads, size, size), f32),
        ],
        compiler_params=pltpu.CompilerParams(vmem_limit_bytes=VMEM_LIMIT),
        cost_estimate=pl.CostEstimate(
            flops=2 * seqs * count * heads * size * (width + size), bytes_accessed=8 << 20, transcendentals=0
        ),
    )(mixer_grad, out_weight, mix, gate, gain, reach)


def backward_kernel(seqs, count, size, hops, *refs):
    pulls, transits = refs[:hops], refs[hops : 2 * hops - 1]
    (
        query_in, key_in, value_in, taps, info, seg_row, beta,
        query_ref, key_ref, value_ref, inverse_ref, fresh_ref, carry_ref, mix_grad_ref, state_ref,
        query_grad_out, key_grad_out, value_grad_out, edge_out, taps_grad_out, logit_grad_out,
    ) = refs[2 * hops - 1 :]
    head = pl.program_id(0)
    row, col = grid_of(count)
    scale = 1.0 / math.sqrt(size)

    @pl.when(head == 0)
    def _():
        logit_grad_out[...] = jnp.zeros_like(logit_grad_out)

    taps_totals = None
    for seq in range(seqs):
        total = pulls[-1][seq, 0]
        for pull, transit in zip(pulls[-2::-1], transits[::-1]):
            transit_high, transit_low = split(transit[seq, 0])
            total_high, total_low = split(total)
            total = pull[seq, 0] + (
                tn(transit_high, total_high) + tn(transit_high, total_low) + tn(transit_low, total_high)
            )
        out_state_grad = total.astype(bf16)
        state = state_ref[seq, 0].astype(bf16)
        query, key, value = query_ref[seq], key_ref[seq], value_ref[seq]
        mix_grad = mix_grad_ref[seq]
        enter, last = info[seq, :, 3:4], info[seq, :, 4:5]
        same = info[seq, :, 5:6] == seg_row[seq]
        causal = same & (row >= col)
        strict = same & (row > col)
        beta_col = head_column(beta, seq, head)
        key_full = key.astype(f32)
        key_last = (key_full * last).astype(bf16)
        update = (fresh_ref[seq] - nn(carry_ref[seq], state)).astype(bf16)
        attend = jnp.where(causal, nt(query, key), 0.0).astype(bf16)
        update_grad = tn(attend, mix_grad) + nn(key_last, out_state_grad)
        right_grad = tn(inverse_ref[0, seq], update_grad.astype(bf16))
        right_low = right_grad.astype(bf16)
        both = nt(jnp.concatenate([mix_grad, right_low], axis=0), update)
        attend_grad = jnp.where(causal, both[:count], 0.0).astype(bf16)
        lower_grad = jnp.where(strict, -both[count:], 0.0)
        gram = nt(key, key)
        surprise = value.astype(f32) - enter * nn(key, state)
        beta_grad = jnp.sum(right_grad * surprise, axis=1, keepdims=True) + jnp.sum(
            lower_grad * gram, axis=1, keepdims=True
        )
        logit_grad = beta_grad * beta_col * (1.0 - beta_col)
        lane = lax.broadcasted_iota(jnp.int32, logit_grad_out.shape[1:], 1)
        logit_grad_out[seq] += jnp.where(lane == head, logit_grad, 0.0)
        value_grad = right_grad * beta_col
        gram_grad = (lower_grad * beta_col).astype(bf16)
        stacked = jnp.concatenate([gram_grad, attend_grad], axis=0)
        forth = nn(stacked, key)
        back = tn(stacked, jnp.concatenate([key, query], axis=0))
        through = nt(
            jnp.concatenate([(value_grad * enter).astype(bf16), mix_grad], axis=0), state
        )
        key_grad = forth[:count] + back - through[:count] + last * nt(update, out_state_grad)
        query_grad = forth[count:] + enter * through[count:]
        for kind, (proj, grad, out) in enumerate(
            (
                (query_in, query_grad, query_grad_out),
                (key_in, key_grad, key_grad_out),
                (value_in, value_grad, value_grad_out),
            )
        ):
            rows, mixed = conv_taps(proj, seq, taps, kind, info, count)
            sig = sigmoid(mixed)
            if kind < 2:
                active = mixed * sig
                norm = lax.rsqrt(jnp.sum(active * active, axis=1, keepdims=True) + unit_eps)
                unit = active * norm
                grad = grad - unit * jnp.sum(grad * unit, axis=1, keepdims=True)
                grad = grad * (norm * scale if kind == 0 else norm)
            mixed_grad = grad * (sig * (1.0 + mixed * (1.0 - sig)))
            sums = [jnp.sum((mixed_grad * rows[tap]).reshape(count // 8, 8, size), axis=0) for tap in range(4)]
            blank = jnp.zeros((8, size), f32)
            proj_grad = mixed_grad * taps[kind, 3:4, :]
            edge = blank
            for tap in range(3):
                delay = 3 - tap
                masked = mixed_grad * (info[seq, :, tap : tap + 1] * taps[kind, tap : tap + 1, :])
                moved = pltpu.roll(masked, count - delay, 0)
                at = lax.broadcasted_iota(jnp.int32, (count, size), 0)
                proj_grad = proj_grad + jnp.where(at < count - delay, moved, 0.0)
                first = pltpu.roll(masked[:8], 8 - delay, 0)
                at_edge = lax.broadcasted_iota(jnp.int32, (8, size), 0)
                edge = edge + jnp.where(at_edge >= 8 - delay, first, 0.0)
            out[seq] = proj_grad
            edge_out[kind, seq] = edge
            sums = jnp.stack([jnp.sum(part, axis=0) for part in sums])
            if seq == 0:
                taps_grad_out[kind] = sums
            else:
                taps_grad_out[kind] += sums


def pl_backward(pulls, transits, proj, taps, info, seg_row, beta, saved, mix_grad, state, heads, seqs, count, size):
    hops = len(pulls)
    row_spec = pl.BlockSpec((seqs, count, size), lambda h: (0, 0, h))
    state_spec = pl.BlockSpec((seqs, 1, size, size), lambda h: (0, h, 0, 0))
    proj_spec = pl.BlockSpec((seqs, count + HALO, size), lambda h: (0, 0, h))
    flops = heads * seqs * 2 * count * count * size * 16
    return pl.pallas_call(
        functools.partial(backward_kernel, seqs, count, size, hops),
        grid=(heads,),
        in_specs=[state_spec] * (2 * hops - 1)
        + [proj_spec] * 3
        + [
            pl.BlockSpec((3, 4, size), lambda h: (0, 0, h)),
            pl.BlockSpec(info.shape, lambda h: (0, 0, 0)),
            pl.BlockSpec(seg_row.shape, lambda h: (0, 0, 0)),
            pl.BlockSpec(beta.shape, lambda h: (0, 0, 0)),
        ]
        + [row_spec] * 3
        + [pl.BlockSpec((1, seqs, count, count), lambda h: (h, 0, 0, 0))]
        + [row_spec] * 3
        + [state_spec],
        out_specs=[row_spec] * 3
        + [
            pl.BlockSpec((3, seqs, 8, size), lambda h: (0, 0, 0, h)),
            pl.BlockSpec((3, 4, size), lambda h: (0, 0, h)),
            pl.BlockSpec((seqs, count, heads), lambda h: (0, 0, 0)),
        ],
        out_shape=[jax.ShapeDtypeStruct((seqs, count, heads * size), f32)] * 3
        + [
            jax.ShapeDtypeStruct((3, seqs, 8, heads * size), f32),
            jax.ShapeDtypeStruct((3, 4, heads * size), f32),
            jax.ShapeDtypeStruct((seqs, count, heads), f32),
        ],
        compiler_params=pltpu.CompilerParams(vmem_limit_bytes=VMEM_LIMIT),
        cost_estimate=pl.CostEstimate(flops=flops, bytes_accessed=16 << 20, transcendentals=0),
    )(*pulls, *transits, *proj, taps, info, seg_row, beta, *saved, mix_grad, state)


def shifted(value, axis, steps):
    count = lax.axis_size(axis)
    initial, last = (max(0, -steps), min(count, count - steps))
    return lax.ppermute(value, axis, [(source, source + steps) for source in range(initial, last)])


def swapped(value):
    return lax.ppermute(value, "head", [(0, 1), (1, 0)])


def in_order(own, other, axis):
    mine = lax.axis_index("head") == 0
    return jnp.where(
        mine, jnp.concatenate([own, other], axis=axis), jnp.concatenate([other, own], axis=axis)
    )


def own_half(value, half):
    return lax.dynamic_slice_in_dim(value, lax.axis_index("head") * half, half, value.ndim - 1)


def pick(value, index, axis):
    return lax.dynamic_index_in_dim(value, index, axis, keepdims=False)


def scatter_sum(first, second):
    dp, seq = lax.axis_size("dp"), lax.axis_size("seq")
    rows = first.shape[0]
    if seq != 4:
        return tuple(
            lax.psum_scatter(part, ("dp", "seq"), scatter_dimension=0, tiled=True) for part in (first, second)
        )
    place = lax.axis_index("seq")
    low, high = place % 2, place // 2
    across_low = [(source, source ^ 1) for source in range(4)]
    across_high = [(source, source ^ 2) for source in range(4)]
    first = first.reshape(dp, 2, 2, rows // (4 * dp), first.shape[1])
    second = second.reshape(dp, 2, 2, rows // (4 * dp), second.shape[1])
    first_in = lax.ppermute(pick(first, 1 - low, 2), "seq", across_low)
    second_in = lax.ppermute(pick(second, 1 - high, 1), "seq", across_high)
    first = pick(first, low, 2) + first_in
    second = pick(second, high, 1) + second_in
    first_in = lax.ppermute(pick(first, 1 - high, 1), "seq", across_high)
    second_in = lax.ppermute(pick(second, 1 - low, 1), "seq", across_low)
    first = pick(first, high, 1) + first_in
    second = pick(second, low, 1) + second_in
    cut = first.shape[-1]
    joined = jnp.concatenate([first, second], axis=-1).reshape(rows // 4, -1)
    joined = lax.psum_scatter(joined, "dp", scatter_dimension=0, tiled=True)
    return joined[:, :cut], joined[:, cut:]


def local(
    block_input,
    segment_ids,
    mixer_gain,
    query_weight,
    key_weight,
    value_weight,
    gate_weight,
    beta_weight,
    conv_weight,
    head_gain,
    out_weight,
    feed_gain,
    feed_gate,
    feed_up,
    feed_down,
    grad_output,
):
    seqs, count, half = block_input.shape
    rows = seqs * count
    size = head_gain.shape[0]
    heads = beta_weight.shape[1]
    channels = heads * size
    width = query_weight.shape[0]
    hops = -(-(LONGEST - 1) // count)
    hops = min(hops, lax.axis_size("seq") - 1)

    other_input = swapped(block_input)
    before = shifted(block_input[:, count - 3 :], "seq", 1)
    other_before = swapped(before)
    full_input = in_order(block_input, other_input, 2)
    full_before = in_order(before, other_before, 2)
    segments = segment_ids.astype(f32)
    edge_ids = shifted(segments[:, count - 3 :], "seq", 1)
    other_grad = swapped(grad_output)

    extended = jnp.concatenate(
        [jnp.zeros((seqs, HALO - 3, width), f32), full_before, full_input], axis=1
    )
    extended_low = (extended * rms_scale(extended) * mixer_gain).astype(bf16)
    flat = extended_low.reshape(seqs * (count + HALO), width)
    proj = [
        nn(flat, weight).reshape(seqs, count + HALO, channels)
        for weight in (query_weight, key_weight, value_weight)
    ]
    normed_in = extended_low[:, HALO:].reshape(rows, width)
    beta = jax.nn.sigmoid(nn(normed_in, beta_weight)).reshape(seqs, count, heads)
    gate_proj = nn(normed_in, gate_weight).reshape(seqs, count, channels)

    extended_ids = jnp.concatenate([edge_ids, segments], axis=1)
    masks = [(extended_ids[:, tap : tap + count] == segments) for tap in range(3)]
    enter = segments == edge_ids[:, 2:3]
    last = segments == segments[:, count - 1 :]
    zero = jnp.zeros_like(segments)
    info = jnp.stack(
        [mask.astype(f32) for mask in masks] + [enter.astype(f32), last.astype(f32), segments, zero, zero], axis=-1
    )
    seg_row = segments[:, None, :]
    taps = conv_weight.reshape(3, 4, channels)
    gain = head_gain[None, :]

    (query, key, value, inverse, fresh, carry, local_mix, reach, state_end, transit) = pl_forward(
        proj, taps, info, seg_row, beta, 0, heads, seqs, count, size, channels
    )
    states = [shifted(state_end, "seq", hop) for hop in range(1, hops + 1)]
    transits = [shifted(transit, "seq", hop) for hop in range(1, hops)]
    state, mix, gated, part = pl_read(
        states, transits, local_mix, reach, gate_proj, gain, out_weight, heads, seqs, count, size, width
    )
    gated = gated.reshape(rows, channels)

    flat_input = full_input.reshape(rows, width)
    middle = flat_input + (part + swapped(part))
    middle_scale = rms_scale(middle)
    middle_normed = middle * middle_scale
    normed_mid = (middle_normed * feed_gain).astype(bf16)
    gate_act = nn(normed_mid, feed_gate)
    up_act = nn(normed_mid, feed_up)
    gate_sig = jax.nn.sigmoid(gate_act)
    gate_silu = gate_act * gate_sig
    inner = (gate_silu * up_act).astype(bf16)
    full_grad = in_order(grad_output, other_grad, 2).reshape(rows, width)
    down_grad = full_grad.astype(bf16)
    cut = feed_down.shape[0] // 256 * 128
    sums_down = scatter_sum(tn(down_grad, inner[:, :cut]), tn(down_grad, inner[:, cut:]))
    inner_grad = nt(down_grad, feed_down)
    gate_grad = (inner_grad * up_act * (gate_sig * (1.0 + gate_act * (1.0 - gate_sig)))).astype(bf16)
    up_grad = (inner_grad * gate_silu).astype(bf16)
    sums_feed = scatter_sum(tn(normed_mid, gate_grad), tn(normed_mid, up_grad))
    mid_part = nt(gate_grad, feed_gate) + nt(up_grad, feed_up)
    mid_grad = mid_part + swapped(mid_part)
    grad_feed_gain = jnp.sum(mid_grad * middle_normed, axis=0)
    middle_grad = full_grad + norm_back(mid_grad, middle_normed, middle_scale, feed_gain)
    mixer_grad = middle_grad.astype(bf16)

    down_part = nn(inner, feed_down)
    mine = lax.axis_index("head")
    down_out = lax.dynamic_slice_in_dim(down_part, (1 - mine) * half, half, 1)
    block_output = own_half(middle, half) + (own_half(down_part, half) + swapped(down_out))

    mix_grad, gate_low, gain_grad, pull = pl_gate_back(
        mixer_grad, out_weight, mix, gate_proj, gain, reach, heads, seqs, count, size, width
    )
    gate_low = gate_low.reshape(rows, channels)
    pulls = [shifted(pull, "seq", -hop) for hop in range(1, hops + 1)]
    back_transits = [shifted(transit, "seq", -hop) for hop in range(1, hops)]
    sums_out = scatter_sum(tn(mixer_grad, gated), tn(normed_in, gate_low))
    query_grad, key_grad, value_grad, edge, taps_grad, logit_grad = pl_backward(
        pulls, back_transits, proj, taps, info, seg_row, beta,
        (query, key, value, inverse, fresh, carry), mix_grad, state, heads, seqs, count, size,
    )
    edge = shifted(edge, "seq", -1)
    lows = [
        (grad + jnp.pad(edge[kind], ((0, 0), (count - 8, 0), (0, 0)))).astype(bf16).reshape(rows, channels)
        for kind, grad in enumerate((query_grad, key_grad, value_grad))
    ]
    beta_low = logit_grad.astype(bf16).reshape(rows, heads)
    sums_query = scatter_sum(tn(normed_in, lows[0]), tn(normed_in, lows[1]))
    last_sums = tn(normed_in, lows[2])
    sums_value = scatter_sum(last_sums[:, : channels // 2], last_sums[:, channels // 2 :])
    in_part = (
        nt(lows[0], query_weight)
        + nt(lows[1], key_weight)
        + nt(lows[2], value_weight)
        + nt(gate_low, gate_weight)
        + nt(beta_low, beta_weight)
    )
    in_grad = in_part + swapped(in_part)
    input_scale = rms_scale(flat_input)
    input_normed = flat_input * input_scale
    grad_mixer_gain = jnp.sum(in_grad * input_normed, axis=0)
    input_grad = own_half(middle_grad + norm_back(in_grad, input_normed, input_scale, mixer_gain), half)
    grad_beta = tn(normed_in, beta_low)

    blocks = lax.axis_size("dp") * lax.axis_size("seq")
    head_part = jnp.sum(gain_grad, axis=0)
    head_part = head_part + swapped(head_part)
    pieces = [
        grad_mixer_gain.reshape(blocks, -1),
        grad_feed_gain.reshape(blocks, -1),
        grad_beta.reshape(blocks, -1),
        taps_grad.reshape(12 * heads, blocks, size // blocks).transpose(1, 0, 2).reshape(blocks, -1),
        head_part.reshape(blocks, -1),
    ]
    small = jnp.concatenate(pieces, axis=1)
    small = jnp.pad(small, ((0, 0), (0, -small.shape[1] % 1024)))
    small = lax.psum_scatter(small.reshape(-1, 128), ("dp", "seq"), scatter_dimension=0, tiled=True).reshape(-1)
    cuts, at = [], 0
    for piece in pieces:
        cuts.append(small[at : at + piece.shape[1]])
        at += piece.shape[1]
    shape = (seqs, count, half)
    return (
        block_output.reshape(shape),
        input_grad.reshape(shape),
        cuts[0],
        sums_query[0],
        sums_query[1],
        jnp.concatenate(sums_value, axis=1),
        sums_out[1],
        cuts[2].reshape(-1, heads),
        cuts[3].reshape(3, 4, heads, size // blocks),
        cuts[4],
        sums_out[0].T,
        cuts[1],
        sums_feed[0],
        sums_feed[1],
        jnp.concatenate(sums_down, axis=1).T,
    )


def solution(mesh):
    return jax.shard_map(
        local,
        mesh=mesh,
        in_specs=(
            P("dp", "seq", "head"),
            P("dp", "seq"),
            P(),
            P(None, "head"),
            P(None, "head"),
            P(None, "head"),
            P(None, "head"),
            P(None, "head"),
            P(None, None, "head", None),
            P(),
            P("head", None),
            P(),
            P(None, "head"),
            P(None, "head"),
            P("head", None),
            P("dp", "seq", "head"),
        ),
        out_specs=(
            P("dp", "seq", "head"),
            P("dp", "seq", "head"),
            P(("dp", "seq")),
            P(("dp", "seq"), "head"),
            P(("dp", "seq"), "head"),
            P(("dp", "seq"), "head"),
            P(("dp", "seq"), "head"),
            P(("dp", "seq"), "head"),
            P(None, None, "head", ("dp", "seq")),
            P(("dp", "seq")),
            P("head", ("dp", "seq")),
            P(("dp", "seq")),
            P(("dp", "seq"), "head"),
            P(("dp", "seq"), "head"),
            P("head", ("dp", "seq")),
        ),
        check_vma=False,
    )
```

```python
import functools
import math

import jax
import jax.numpy as jnp
from jax import lax
from jax.experimental import pallas as pl
from jax.experimental.pallas import tpu as pltpu
from jax.sharding import PartitionSpec as P

HALO = 16
LONGEST = 512

norm_eps = 1e-05
unit_eps = 1e-06
f32 = jnp.float32
bf16 = jnp.bfloat16
VMEM_LIMIT = 48 * 1024 * 1024


def nn(a, b):
    return lax.dot_general(a, b, (((1,), (0,)), ((), ())), preferred_element_type=f32)


def nt(a, b):
    return lax.dot_general(a, b, (((1,), (1,)), ((), ())), preferred_element_type=f32)


def tn(a, b):
    return lax.dot_general(a, b, (((0,), (0,)), ((), ())), preferred_element_type=f32)


def split(value):
    high = value.astype(bf16)
    return high, (value - high.astype(f32)).astype(bf16)


def nn3(a, b):
    a_high, a_low = a
    b_high, b_low = b
    return nn(a_high, b_high) + nn(a_high, b_low) + nn(a_low, b_high)


def sigmoid(value):
    return 1.0 / (1.0 + jnp.exp(-value))


def rms_scale(values):
    return lax.rsqrt(jnp.mean(values * values, axis=-1, keepdims=True) + norm_eps)


def norm_back(grad_rows, normed, row_scale, gain_vec):
    grad_hat = grad_rows * gain_vec
    return row_scale * (grad_hat - normed * jnp.mean(grad_hat * normed, axis=-1, keepdims=True))


def grid_of(size):
    row = lax.broadcasted_iota(jnp.int32, (size, size), 0)
    return row, lax.broadcasted_iota(jnp.int32, (size, size), 1)


def unit_inverses(lowers, size):
    row, col = grid_of(size)
    apart = row ^ col
    eye = jnp.where(apart == 0, 1.0, 0.0)
    inverses = [eye - jnp.where(apart == 1, lower, 0.0) for lower in lowers]
    lows = [lower.astype(bf16) for lower in lowers]
    level = 1
    while (1 << level) < size:
        here = (apart >> level) == 1
        rounded = [inverse.astype(bf16) for inverse in inverses]
        right = [nn(jnp.where(here, low, 0.0), near).astype(bf16) for low, near in zip(lows, rounded)]
        inverses = [inverse - nn(near, far) for inverse, near, far in zip(inverses, rounded, right)]
        level += 1
    parts = [split(inverse) for inverse in inverses]
    wholes = [split(lower) for lower in lowers]
    left = [
        (eye - inverse - nn3(whole, part)).astype(bf16)
        for inverse, whole, part in zip(inverses, wholes, parts)
    ]
    return [inverse + nn(part[0], rest) for inverse, part, rest in zip(inverses, parts, left)]


def conv_taps(proj, seq, taps, kind, info, count, lanes=slice(None)):
    rows = []
    for tap in range(4):
        moved = proj[seq, HALO - 3 + tap : HALO - 3 + tap + count, lanes]
        rows.append(moved if tap == 3 else moved * info[:, tap : tap + 1])
    mixed = rows[0] * taps[kind, 0:1, lanes]
    for tap in range(1, 4):
        mixed = mixed + rows[tap] * taps[kind, tap : tap + 1, lanes]
    return rows, mixed


def turned(info, seq):
    row, col = grid_of(8)
    return tn(info[seq].astype(bf16), jnp.where(row == col, 1.0, 0.0).astype(bf16))


def head_column(table, seq, head):
    lane = lax.broadcasted_iota(jnp.int32, table.shape[1:], 1)
    return jnp.sum(jnp.where(lane == head, table[seq], 0.0), axis=1, keepdims=True)


def forward_kernel(
    seqs, count, size, group,
    query_in, key_in, value_in, taps, info, beta,
    query_out, key_out, value_out, inverse_out, fresh_out, carry_out, local_out, reach_out, state_out, transit_out, both_out,
):
    row, col = grid_of(count)
    scale = 1.0 / math.sqrt(size)
    infos = [turned(info, seq) for seq in range(seqs)]
    sames = [infos[seq][:, 5:6] == info[seq, 5:6, :] for seq in range(seqs)]
    every = [(seq, part, slice(part * size, (part + 1) * size)) for part in range(group) for seq in range(seqs)]
    queries, keys, lowers, betas = [], [], [], []
    for seq, part, lanes in every:
        parts = []
        for kind, proj in enumerate((query_in, key_in, value_in)):
            mixed = conv_taps(proj, seq, taps, kind, infos[seq], count, lanes)[1]
            parts.append(mixed * sigmoid(mixed))
        query, key, value = parts
        query = query * (lax.rsqrt(jnp.sum(query * query, axis=1, keepdims=True) + unit_eps) * scale)
        key = key * lax.rsqrt(jnp.sum(key * key, axis=1, keepdims=True) + unit_eps)
        query, key, value = query.astype(bf16), key.astype(bf16), value.astype(bf16)
        query_out[seq, :, lanes], key_out[seq, :, lanes], value_out[seq, :, lanes] = query, key, value
        beta_col = head_column(beta, seq, pl.program_id(0) * group + part)
        queries.append(query)
        keys.append(key)
        betas.append(beta_col)
        lowers.append(jnp.where(sames[seq] & (row > col), nt(key, key) * beta_col, 0.0))
    inverses = unit_inverses(lowers, count)
    for (seq, part, lanes), query, key, beta_col, inverse in zip(every, queries, keys, betas, inverses):
        enter, last = infos[seq][:, 3:4], infos[seq][:, 4:5]
        key_full = key.astype(f32)
        inverse_parts = split(inverse)
        inverse_out[part, seq] = inverse_parts[0]
        right = jnp.concatenate(
            [key_full * (beta_col * enter), value_out[seq, :, lanes].astype(f32) * beta_col], axis=1
        )
        solved = nn3(inverse_parts, split(right))
        solved_high, solved_low = split(solved)
        key_last = (key_full * last).astype(bf16)
        ends = tn(key_last, solved_high) + tn(key_last, solved_low)
        transit_row, transit_col = grid_of(size)
        eye = jnp.where(transit_row == transit_col, 1.0, 0.0)
        transit = eye * info[seq, 3:4, count - 1 :] - ends[:, :size]
        state_out[seq, part] = ends[:, size:]
        transit_out[seq, part] = transit
        both_out[seq, part, 0] = ends[:, size:]
        both_out[seq, part, 1] = transit
        attend = jnp.where(sames[seq] & (row >= col), nt(query, key), 0.0).astype(bf16)
        reads = nn(attend, solved_high)
        local_out[seq, :, lanes] = reads[:, size:]
        reach_out[seq, :, lanes] = (query.astype(f32) * enter - reads[:, :size]).astype(bf16)
        carry_out[seq, :, lanes] = solved_high[:, :size]
        fresh_out[seq, :, lanes] = solved[:, size:]


def pl_forward(proj, taps, info, beta, group, heads, seqs, count, size, channels):
    def rows(dtype):
        return jax.ShapeDtypeStruct((seqs, count, heads * size), dtype)

    row_spec = pl.BlockSpec((seqs, count, group * size), lambda h: (0, 0, h))
    proj_spec = pl.BlockSpec((seqs, count + HALO, group * size), lambda h: (0, 0, h))
    state = jax.ShapeDtypeStruct((seqs, heads, size, size), f32)
    state_spec = pl.BlockSpec((seqs, group, size, size), lambda h: (0, h, 0, 0))
    flops = heads * seqs * (40 * count**3 + 16 * count * count * size)
    return pl.pallas_call(
        functools.partial(forward_kernel, seqs, count, size, group),
        grid=(heads // group,),
        in_specs=[proj_spec] * 3
        + [
            pl.BlockSpec((3, 4, group * size), lambda h: (0, 0, h)),
            pl.BlockSpec(info.shape, lambda h: (0, 0, 0)),
            pl.BlockSpec(beta.shape, lambda h: (0, 0, 0)),
        ],
        out_specs=[row_spec] * 3
        + [pl.BlockSpec((group, seqs, count, count), lambda h: (h, 0, 0, 0))]
        + [row_spec] * 4
        + [state_spec] * 2
        + [pl.BlockSpec((seqs, group, 2, size, size), lambda h: (0, h, 0, 0, 0))],
        out_shape=[rows(bf16)] * 3
        + [jax.ShapeDtypeStruct((heads, seqs, count, count), bf16)]
        + [rows(f32), rows(bf16), rows(f32), rows(bf16)]
        + [state] * 2
        + [jax.ShapeDtypeStruct((seqs, heads, 2, size, size), f32)],
        compiler_params=pltpu.CompilerParams(vmem_limit_bytes=VMEM_LIMIT),
        cost_estimate=pl.CostEstimate(flops=flops, bytes_accessed=12 << 20, transcendentals=0),
    )(*proj, taps, info, beta)


def arrived(boths, farthest, seq):
    total = farthest[seq, 0]
    for both in boths[::-1]:
        total = both[seq, 0, 0] + nn3(split(both[seq, 0, 1]), split(total))
    return total


def read_kernel(seqs, count, size, heads, hops, *refs):
    boths, farthest = refs[: hops - 1], refs[hops - 1]
    local, reach, gate, gain, out_weight, state_out, mix_out, gated_out, part_out, held = refs[hops:]
    head = pl.program_id(0)
    for seq in range(seqs):
        state = arrived(boths, farthest, seq)
        state_out[seq, 0] = state
        state_high, state_low = split(state)
        moved = reach[seq]
        mix = local[seq] + nn(moved, state_high) + nn(moved, state_low)
        mix_out[seq] = mix
        gate_now = gate[seq]
        gated = (mix * rms_scale(mix) * gain[...] * (gate_now * sigmoid(gate_now))).astype(bf16)
        gated_out[seq] = gated
        held[head, seq * count : (seq + 1) * count, :] = gated

    @pl.when(head == heads - 1)
    def _():
        rows = jnp.concatenate([held[h] for h in range(heads)], axis=1)
        part_out[...] = nn(rows, out_weight[...])


def pl_read(boths, farthest, local, reach, gate, gain, out_weight, heads, seqs, count, size, width):
    row_spec = pl.BlockSpec((seqs, count, size), lambda h: (0, 0, h))
    state_spec = pl.BlockSpec((seqs, 1, size, size), lambda h: (0, h, 0, 0))
    both_spec = pl.BlockSpec((seqs, 1, 2, size, size), lambda h: (0, h, 0, 0, 0))
    hops = len(boths) + 1
    return pl.pallas_call(
        functools.partial(read_kernel, seqs, count, size, heads, hops),
        grid=(heads,),
        in_specs=[both_spec] * (hops - 1)
        + [state_spec]
        + [row_spec] * 3
        + [pl.BlockSpec((1, size), lambda h: (0, 0)), pl.BlockSpec((heads * size, width), lambda h: (0, 0))],
        out_specs=[state_spec, row_spec, row_spec, pl.BlockSpec((seqs * count, width), lambda h: (0, 0))],
        out_shape=[
            jax.ShapeDtypeStruct((seqs, heads, size, size), f32),
            jax.ShapeDtypeStruct((seqs, count, heads * size), f32),
            jax.ShapeDtypeStruct((seqs, count, heads * size), bf16),
            jax.ShapeDtypeStruct((seqs * count, width), f32),
        ],
        scratch_shapes=[pltpu.VMEM((heads, seqs * count, size), bf16)],
        compiler_params=pltpu.CompilerParams(vmem_limit_bytes=VMEM_LIMIT),
        cost_estimate=pl.CostEstimate(
            flops=2 * seqs * count * heads * size * (width + 2 * size), bytes_accessed=12 << 20, transcendentals=0
        ),
    )(*boths, farthest, local, reach, gate, gain, out_weight)


def gate_back_kernel(seqs, count, size, mixer_grad, out_weight, mix, gate, gain, reach, mix_grad, gate_grad, gain_grad, pull):
    head = pl.program_id(0)

    @pl.when(head == 0)
    def _():
        gain_grad[...] = jnp.zeros_like(gain_grad)

    grads = nt(mixer_grad[...], out_weight[...])
    for seq in range(seqs):
        grad = grads[seq * count : (seq + 1) * count]
        mix_now, gate_now = mix[seq], gate[seq]
        scale = rms_scale(mix_now)
        normed = mix_now * scale
        sig = sigmoid(gate_now)
        gate_silu = gate_now * sig
        with_norm = grad * normed
        gain_grad[...] += jnp.sum((with_norm * gate_silu).reshape(count // 8, 8, size), axis=0)
        gate_grad[seq] = (with_norm * gain[...] * (sig * (1.0 + gate_now * (1.0 - sig)))).astype(bf16)
        normed_grad = grad * gain[...] * gate_silu
        mix_grad_now = scale * (normed_grad - normed * jnp.mean(normed_grad * normed, axis=1, keepdims=True))
        low = mix_grad_now.astype(bf16)
        mix_grad[seq] = low
        pull[seq, 0] = tn(reach[seq], low)


def pl_gate_back(mixer_grad, out_weight, mix, gate, gain, reach, heads, seqs, count, size, width):
    row_spec = pl.BlockSpec((seqs, count, size), lambda h: (0, 0, h))
    return pl.pallas_call(
        functools.partial(gate_back_kernel, seqs, count, size),
        grid=(heads,),
        in_specs=[
            pl.BlockSpec((seqs * count, width), lambda h: (0, 0)),
            pl.BlockSpec((size, width), lambda h: (h, 0)),
            row_spec,
            row_spec,
            pl.BlockSpec((1, size), lambda h: (0, 0)),
            row_spec,
        ],
        out_specs=[
            row_spec,
            row_spec,
            pl.BlockSpec((8, size), lambda h: (0, 0)),
            pl.BlockSpec((seqs, 1, size, size), lambda h: (0, h, 0, 0)),
        ],
        out_shape=[
            jax.ShapeDtypeStruct((seqs, count, heads * size), bf16),
            jax.ShapeDtypeStruct((seqs, count, heads * size), bf16),
            jax.ShapeDtypeStruct((8, size), f32),
            jax.ShapeDtypeStruct((seqs, heads, size, size), f32),
        ],
        compiler_params=pltpu.CompilerParams(vmem_limit_bytes=VMEM_LIMIT),
        cost_estimate=pl.CostEstimate(
            flops=2 * seqs * count * heads * size * (width + size), bytes_accessed=8 << 20, transcendentals=0
        ),
    )(mixer_grad, out_weight, mix, gate, gain, reach)


def backward_kernel(seqs, count, size, hops, *refs):
    pulls, transits = refs[:hops], refs[hops : 2 * hops - 1]
    (
        query_in, key_in, value_in, taps, info_rows, beta,
        query_ref, key_ref, value_ref, inverse_ref, fresh_ref, carry_ref, mix_grad_ref, state_ref,
        query_grad_out, key_grad_out, value_grad_out, edge_out, taps_grad_out, logit_grad_out,
    ) = refs[2 * hops - 1 :]
    head = pl.program_id(0)
    row, col = grid_of(count)
    scale = 1.0 / math.sqrt(size)

    @pl.when(head == 0)
    def _():
        logit_grad_out[...] = jnp.zeros_like(logit_grad_out)

    taps_totals = None
    for seq in range(seqs):
        total = pulls[-1][seq, 0]
        for pull, transit in zip(pulls[-2::-1], transits[::-1]):
            transit_high, transit_low = split(transit[seq, 0])
            total_high, total_low = split(total)
            total = pull[seq, 0] + (
                tn(transit_high, total_high) + tn(transit_high, total_low) + tn(transit_low, total_high)
            )
        out_state_grad = total.astype(bf16)
        state = state_ref[seq, 0].astype(bf16)
        query, key, value = query_ref[seq], key_ref[seq], value_ref[seq]
        mix_grad = mix_grad_ref[seq]
        info = turned(info_rows, seq)
        enter, last = info[:, 3:4], info[:, 4:5]
        same = info[:, 5:6] == info_rows[seq, 5:6, :]
        causal = same & (row >= col)
        strict = same & (row > col)
        beta_col = head_column(beta, seq, head)
        key_full = key.astype(f32)
        key_last = (key_full * last).astype(bf16)
        update = (fresh_ref[seq] - nn(carry_ref[seq], state)).astype(bf16)
        attend = jnp.where(causal, nt(query, key), 0.0).astype(bf16)
        update_grad = tn(attend, mix_grad) + nn(key_last, out_state_grad)
        right_grad = tn(inverse_ref[0, seq], update_grad.astype(bf16))
        right_low = right_grad.astype(bf16)
        both = nt(jnp.concatenate([mix_grad, right_low], axis=0), update)
        attend_grad = jnp.where(causal, both[:count], 0.0).astype(bf16)
        lower_grad = jnp.where(strict, -both[count:], 0.0)
        gram = nt(key, key)
        surprise = value.astype(f32) - enter * nn(key, state)
        beta_grad = jnp.sum(right_grad * surprise, axis=1, keepdims=True) + jnp.sum(
            lower_grad * gram, axis=1, keepdims=True
        )
        logit_grad = beta_grad * beta_col * (1.0 - beta_col)
        lane = lax.broadcasted_iota(jnp.int32, logit_grad_out.shape[1:], 1)
        logit_grad_out[seq] += jnp.where(lane == head, logit_grad, 0.0)
        value_grad = right_grad * beta_col
        gram_grad = (lower_grad * beta_col).astype(bf16)
        stacked = jnp.concatenate([gram_grad, attend_grad], axis=0)
        forth = nn(stacked, key)
        back = tn(stacked, jnp.concatenate([key, query], axis=0))
        through = nt(
            jnp.concatenate([(value_grad * enter).astype(bf16), mix_grad], axis=0), state
        )
        key_grad = forth[:count] + back - through[:count] + last * nt(update, out_state_grad)
        query_grad = forth[count:] + enter * through[count:]
        for kind, (proj, grad, out) in enumerate(
            (
                (query_in, query_grad, query_grad_out),
                (key_in, key_grad, key_grad_out),
                (value_in, value_grad, value_grad_out),
            )
        ):
            rows, mixed = conv_taps(proj, seq, taps, kind, info, count)
            sig = sigmoid(mixed)
            if kind < 2:
                active = mixed * sig
                norm = lax.rsqrt(jnp.sum(active * active, axis=1, keepdims=True) + unit_eps)
                unit = active * norm
                grad = grad - unit * jnp.sum(grad * unit, axis=1, keepdims=True)
                grad = grad * (norm * scale if kind == 0 else norm)
            mixed_grad = grad * (sig * (1.0 + mixed * (1.0 - sig)))
            sums = [jnp.sum((mixed_grad * rows[tap]).reshape(count // 8, 8, size), axis=0) for tap in range(4)]
            blank = jnp.zeros((8, size), f32)
            proj_grad = mixed_grad * taps[kind, 3:4, :]
            edge = blank
            for tap in range(3):
                delay = 3 - tap
                masked = mixed_grad * (info[:, tap : tap + 1] * taps[kind, tap : tap + 1, :])
                moved = pltpu.roll(masked, count - delay, 0)
                at = lax.broadcasted_iota(jnp.int32, (count, size), 0)
                proj_grad = proj_grad + jnp.where(at < count - delay, moved, 0.0)
                first = pltpu.roll(masked[:8], 8 - delay, 0)
                at_edge = lax.broadcasted_iota(jnp.int32, (8, size), 0)
                edge = edge + jnp.where(at_edge >= 8 - delay, first, 0.0)
            out[seq] = proj_grad
            edge_out[kind, seq] = edge
            sums = jnp.stack([jnp.sum(part, axis=0) for part in sums])
            if seq == 0:
                taps_grad_out[kind] = sums
            else:
                taps_grad_out[kind] += sums


def pl_backward(pulls, transits, proj, taps, info, beta, saved, mix_grad, state, heads, seqs, count, size):
    hops = len(pulls)
    row_spec = pl.BlockSpec((seqs, count, size), lambda h: (0, 0, h))
    state_spec = pl.BlockSpec((seqs, 1, size, size), lambda h: (0, h, 0, 0))
    proj_spec = pl.BlockSpec((seqs, count + HALO, size), lambda h: (0, 0, h))
    flops = heads * seqs * 2 * count * count * size * 160
    return pl.pallas_call(
        functools.partial(backward_kernel, seqs, count, size, hops),
        grid=(heads,),
        in_specs=[state_spec] * (2 * hops - 1)
        + [proj_spec] * 3
        + [
            pl.BlockSpec((3, 4, size), lambda h: (0, 0, h)),
            pl.BlockSpec(info.shape, lambda h: (0, 0, 0)),
            pl.BlockSpec(beta.shape, lambda h: (0, 0, 0)),
        ]
        + [row_spec] * 3
        + [pl.BlockSpec((1, seqs, count, count), lambda h: (h, 0, 0, 0))]
        + [row_spec] * 3
        + [state_spec],
        out_specs=[row_spec] * 3
        + [
            pl.BlockSpec((3, seqs, 8, size), lambda h: (0, 0, 0, h)),
            pl.BlockSpec((3, 4, size), lambda h: (0, 0, h)),
            pl.BlockSpec((seqs, count, heads), lambda h: (0, 0, 0)),
        ],
        out_shape=[jax.ShapeDtypeStruct((seqs, count, heads * size), f32)] * 3
        + [
            jax.ShapeDtypeStruct((3, seqs, 8, heads * size), f32),
            jax.ShapeDtypeStruct((3, 4, heads * size), f32),
            jax.ShapeDtypeStruct((seqs, count, heads), f32),
        ],
        compiler_params=pltpu.CompilerParams(vmem_limit_bytes=VMEM_LIMIT),
        cost_estimate=pl.CostEstimate(flops=flops, bytes_accessed=16 << 20, transcendentals=0),
    )(*pulls, *transits, *proj, taps, info, beta, *saved, mix_grad, state)


def shifted(value, axis, steps):
    count = lax.axis_size(axis)
    initial, last = (max(0, -steps), min(count, count - steps))
    return lax.ppermute(value, axis, [(source, source + steps) for source in range(initial, last)])


def swapped(value):
    return lax.ppermute(value, "head", [(0, 1), (1, 0)])


def in_order(own, other, axis):
    mine = lax.axis_index("head") == 0
    return jnp.where(
        mine, jnp.concatenate([own, other], axis=axis), jnp.concatenate([other, own], axis=axis)
    )


def own_half(value, half):
    return lax.dynamic_slice_in_dim(value, lax.axis_index("head") * half, half, value.ndim - 1)


def pick(value, index, axis):
    return lax.dynamic_index_in_dim(value, index, axis, keepdims=False)


def together(*values):
    return lax.optimization_barrier(values)


def weight_kernel(block, first_window, second_window, bits, first_left, first_right, second_left, second_right, *refs):
    first_leaves, first_stays, second_leaves, second_stays, held, held_second = refs
    low, high = bits[0], bits[1]
    held[...] = tn(first_left[...], first_right[:, first_window])
    for part in range(2):
        base = part * 2 * block
        first_leaves[0, part] = held[pl.ds(pl.multiple_of(base + (1 - low) * block, 8), block), :]
        first_stays[0, part] = held[pl.ds(pl.multiple_of(base + low * block, 8), block), :]
    held_second[...] = tn(second_left[...], second_right[:, second_window])
    second_leaves[0] = held_second[pl.ds(pl.multiple_of((1 - high) * 2 * block, 8), 2 * block), :]
    second_stays[0] = held_second[pl.ds(pl.multiple_of(high * 2 * block, 8), 2 * block), :]


def fold_kernel(block, bits, first_stays, first_comes, second_stays, second_comes, *refs):
    first_leaves, first_keeps, second_leaves, second_keeps = refs
    low, high = bits[0], bits[1]
    first_leaves[0] = first_stays[0, 1 - high] + first_comes[0, 1 - high]
    first_keeps[0] = first_stays[0, high] + first_comes[0, high]
    away = pl.ds(pl.multiple_of((1 - low) * block, 8), block)
    here = pl.ds(pl.multiple_of(low * block, 8), block)
    second_leaves[0] = second_stays[0, away] + second_comes[0, away]
    second_keeps[0] = second_stays[0, here] + second_comes[0, here]


def join_kernel(bits, first_keeps, first_comes, second_keeps, second_comes, out):
    cut = first_keeps.shape[-1]
    out[:, :cut] = first_keeps[0] + first_comes[0]
    out[:, cut:] = second_keeps[0] + second_comes[0]


def per_block(kernel, bits, steps, args, in_specs, out_specs, out_shape, scratch, flops, bytes_accessed):
    return pl.pallas_call(
        kernel,
        grid_spec=pltpu.PrefetchScalarGridSpec(
            num_scalar_prefetch=1, grid=(steps,), in_specs=in_specs, out_specs=out_specs, scratch_shapes=scratch
        ),
        out_shape=out_shape,
        compiler_params=pltpu.CompilerParams(vmem_limit_bytes=VMEM_LIMIT),
        cost_estimate=pl.CostEstimate(flops=flops, bytes_accessed=bytes_accessed, transcendentals=0),
    )(bits, *args)


def four_block(dims):
    return pl.BlockSpec((1,) + dims, lambda z, bits: (z,) + (0,) * len(dims))


def swap_bit(value, bit):
    return lax.ppermute(value, "seq", [(source, source ^ (1 << bit)) for source in range(4)])


def by_bits():
    return lax.axis_size("seq") == 4


def weight_grads(bits, first_left, first_right, second_left, second_right, first_window=None, second_window=None):
    first_window = first_window or slice(0, first_right.shape[1])
    second_window = second_window or slice(0, second_right.shape[1])
    if not by_bits():
        return tn(first_left, first_right[:, first_window]), tn(second_left, second_right[:, second_window])
    dp = lax.axis_size("dp")
    tokens, rows = first_left.shape
    first_cols = first_window.stop - first_window.start
    second_cols = second_window.stop - second_window.start
    block = rows // (4 * dp)
    left_spec = pl.BlockSpec((tokens, 4 * block), lambda z, bits: (0, z))

    def whole(cols):
        return pl.BlockSpec((tokens, cols), lambda z, bits: (0, 0))

    first, second = (2, block, first_cols), (2 * block, second_cols)
    return per_block(
        functools.partial(weight_kernel, block, first_window, second_window),
        bits,
        dp,
        (first_left, first_right, second_left, second_right),
        [left_spec, whole(first_right.shape[1]), left_spec, whole(second_right.shape[1])],
        [four_block(dims) for dims in (first, first, second, second)],
        [jax.ShapeDtypeStruct((dp,) + dims, f32) for dims in (first, first, second, second)],
        [pltpu.VMEM((4 * block, first_cols), f32), pltpu.VMEM((4 * block, second_cols), f32)],
        2 * tokens * rows * (first_cols + second_cols),
        4 * rows * (first_cols + second_cols) + 2 * tokens * (2 * rows + first_cols + second_cols),
    )


def paired_kernel(first_left, first_right, second_left, second_right, out):
    cut = first_right.shape[1]
    out[:, :cut] = tn(first_left[...], first_right[...])
    out[:, cut:] = tn(second_left[...], second_right[...])


def paired_grads(first_left, first_right, second_left, second_right):
    tokens, rows = first_left.shape
    cols = first_right.shape[1] + second_right.shape[1]
    step = rows // 4
    left_spec = pl.BlockSpec((tokens, step), lambda i: (0, i))
    whole = [pl.BlockSpec(right.shape, lambda i: (0, 0)) for right in (first_right, second_right)]
    return pl.pallas_call(
        paired_kernel,
        grid=(4,),
        in_specs=[left_spec, whole[0], left_spec, whole[1]],
        out_specs=pl.BlockSpec((step, cols), lambda i: (i, 0)),
        out_shape=jax.ShapeDtypeStruct((rows, cols), f32),
        compiler_params=pltpu.CompilerParams(vmem_limit_bytes=VMEM_LIMIT),
        cost_estimate=pl.CostEstimate(
            flops=2 * tokens * rows * cols, bytes_accessed=4 * rows * cols + 4 * tokens * rows, transcendentals=0
        ),
    )(first_left, first_right, second_left, second_right)


def first_swap(parts):
    if not by_bits():
        return parts
    first_leaves, first_stays, second_leaves, second_stays = parts
    return first_stays, swap_bit(first_leaves, 0), second_stays, swap_bit(second_leaves, 1)


def fold(bits, parts):
    if not by_bits():
        return parts
    dp = lax.axis_size("dp")
    block, first_cols, second_cols = parts[0].shape[2], parts[0].shape[3], parts[2].shape[2]
    ins = [(2, block, first_cols)] * 2 + [(2 * block, second_cols)] * 2
    outs = [(block, first_cols)] * 2 + [(block, second_cols)] * 2
    return per_block(
        functools.partial(fold_kernel, block),
        bits,
        dp,
        parts,
        [four_block(dims) for dims in ins],
        [four_block(dims) for dims in outs],
        [jax.ShapeDtypeStruct((dp,) + dims, f32) for dims in outs],
        [],
        0,
        24 * dp * block * (first_cols + second_cols),
    )


def second_swap(parts):
    if not by_bits():
        return parts
    first_leaves, first_keeps, second_leaves, second_keeps = parts
    return first_keeps, swap_bit(first_leaves, 1), second_keeps, swap_bit(second_leaves, 0)


def join(bits, parts):
    if not by_bits():
        return tuple(
            lax.psum_scatter(part, ("dp", "seq"), scatter_dimension=0, tiled=True) for part in parts
        )
    dp = lax.axis_size("dp")
    block, first_cols, second_cols = parts[0].shape[1], parts[0].shape[2], parts[2].shape[2]
    return per_block(
        join_kernel,
        bits,
        dp,
        parts,
        [four_block((block, cols)) for cols in (first_cols, first_cols, second_cols, second_cols)],
        pl.BlockSpec((block, first_cols + second_cols), lambda z, bits: (z, 0)),
        jax.ShapeDtypeStruct((dp * block, first_cols + second_cols), f32),
        [],
        0,
        12 * dp * block * (first_cols + second_cols),
    )


def last_sum(joined, cut):
    if not by_bits():
        return joined
    joined = lax.psum_scatter(joined, "dp", scatter_dimension=0, tiled=True)
    return joined[:, :cut], joined[:, cut:]


def swap_add(value, bit):
    if not by_bits():
        return value
    value = value.reshape(2 - bit, 2, -1, value.shape[-1])
    mine = (lax.axis_index("seq") >> bit) & 1
    return pick(value, mine, 1) + swap_bit(pick(value, 1 - mine, 1), bit)


def small_sum(value, names):
    if not by_bits():
        return lax.psum_scatter(value, names, scatter_dimension=0, tiled=True)
    if names == "dp" and lax.axis_size("dp") != 4:
        return lax.psum_scatter(value, "dp", scatter_dimension=0, tiled=True)
    value = value.reshape((2, 2) + (value.shape[0] // 4,) + value.shape[1:])
    for bit in range(2):
        mine = (lax.axis_index(names) >> bit) & 1
        perm = [(source, source ^ (1 << bit)) for source in range(4)]
        value = pick(value, mine, 1 - bit) + lax.ppermute(pick(value, 1 - mine, 1 - bit), names, perm)
    return value


def local(
    block_input,
    segment_ids,
    mixer_gain,
    query_weight,
    key_weight,
    value_weight,
    gate_weight,
    beta_weight,
    conv_weight,
    head_gain,
    out_weight,
    feed_gain,
    feed_gate,
    feed_up,
    feed_down,
    grad_output,
):
    seqs, count, half = block_input.shape
    rows = seqs * count
    size = head_gain.shape[0]
    heads = beta_weight.shape[1]
    channels = heads * size
    width = query_weight.shape[0]
    hops = -(-(LONGEST - 1) // count)
    hops = min(hops, lax.axis_size("seq") - 1)

    other_input = swapped(block_input)
    segments = segment_ids.astype(f32)
    before = shifted(
        jnp.concatenate([block_input[:, count - 3 :], segments[:, count - 3 :, None]], axis=2), "seq", 1
    )
    edge_ids = before[:, :, half]
    before = before[:, :, :half]
    other_before = swapped(before)
    full_input = in_order(block_input, other_input, 2)
    full_before = in_order(before, other_before, 2)
    other_grad = swapped(grad_output)

    extended = jnp.concatenate(
        [jnp.zeros((seqs, HALO - 3, width), f32), full_before, full_input], axis=1
    )
    extended_low = (extended * rms_scale(extended) * mixer_gain).astype(bf16)
    flat = extended_low.reshape(seqs * (count + HALO), width)
    proj = [
        nn(flat, weight).reshape(seqs, count + HALO, channels)
        for weight in (query_weight, key_weight, value_weight)
    ]
    normed_in = extended_low[:, HALO:].reshape(rows, width)
    beta = jax.nn.sigmoid(nn(normed_in, beta_weight)).reshape(seqs, count, heads)
    gate_proj = nn(normed_in, gate_weight).reshape(seqs, count, channels)

    extended_ids = jnp.concatenate([edge_ids, segments], axis=1)
    masks = [(extended_ids[:, tap : tap + count] == segments) for tap in range(3)]
    enter = segments == edge_ids[:, 2:3]
    last = segments == segments[:, count - 1 :]
    zero = jnp.zeros_like(segments)
    info = jnp.stack(
        [mask.astype(f32) for mask in masks] + [enter.astype(f32), last.astype(f32), segments, zero, zero], axis=1
    )
    taps = conv_weight.reshape(3, 4, channels)
    gain = head_gain[None, :]

    (query, key, value, inverse, fresh, carry, local_mix, reach, state_end, transit, both) = pl_forward(
        proj, taps, info, beta, 2 if heads % 2 == 0 else 1, heads, seqs, count, size, channels
    )
    boths = [shifted(both, "seq", hop) for hop in range(1, hops)]
    farthest = shifted(state_end, "seq", hops)
    back_transits = [shifted(transit, "seq", -hop) for hop in range(1, hops)]
    boths, farthest, back_transits = lax.optimization_barrier((boths, farthest, back_transits))
    state, mix, gated, part = pl_read(
        boths, farthest, local_mix, reach, gate_proj, gain, out_weight, heads, seqs, count, size, width
    )
    gated = gated.reshape(rows, channels)
    flat_input = full_input.reshape(rows, width)
    middle = flat_input + (part + swapped(part))
    middle_scale = rms_scale(middle)
    middle_normed = middle * middle_scale
    normed_mid = (middle_normed * feed_gain).astype(bf16)
    gate_act = nn(normed_mid, feed_gate)
    up_act = nn(normed_mid, feed_up)
    gate_sig = jax.nn.sigmoid(gate_act)
    gate_silu = gate_act * gate_sig
    inner = (gate_silu * up_act).astype(bf16)
    full_grad = in_order(grad_output, other_grad, 2).reshape(rows, width)
    down_grad = full_grad.astype(bf16)
    cut = feed_down.shape[0] // 256 * 128
    inner_grad = nt(down_grad, feed_down)
    gate_grad = (inner_grad * up_act * (gate_sig * (1.0 + gate_act * (1.0 - gate_sig)))).astype(bf16)
    up_grad = (inner_grad * gate_silu).astype(bf16)
    place = lax.axis_index("seq")
    bits = jnp.stack([place & 1, (place >> 1) & 1]).astype(jnp.int32)
    down_sums = weight_grads(
        bits, down_grad, inner, down_grad, inner, slice(0, cut), slice(cut, inner.shape[1])
    )
    down_sums, mid_gate, mid_up = together(down_sums, gate_grad, up_grad)
    down_sums = first_swap(down_sums)
    mid_part = nt(mid_gate, feed_gate) + nt(mid_up, feed_up)
    mid_grad = mid_part + swapped(mid_part)
    grad_feed_gain = jnp.sum(mid_grad * middle_normed, axis=0)
    middle_grad = full_grad + norm_back(mid_grad, middle_normed, middle_scale, feed_gain)
    mixer_grad = middle_grad.astype(bf16)

    down_part = nn(inner, feed_down)
    mine = lax.axis_index("head")
    down_out = lax.dynamic_slice_in_dim(down_part, (1 - mine) * half, half, 1)
    block_output = own_half(middle, half) + (own_half(down_part, half) + swapped(down_out))

    mix_grad, gate_low, gain_grad, pull = pl_gate_back(
        mixer_grad, out_weight, mix, gate_proj, gain, reach, heads, seqs, count, size, width
    )
    gate_low = gate_low.reshape(rows, channels)

    pull, late_gate, late_up = together(pull, gate_grad, up_grad)
    pulls = [shifted(pull, "seq", -hop) for hop in range(1, hops + 1)]
    feed_sums = weight_grads(bits, normed_mid, late_gate, normed_mid, late_up)
    down_sums, feed_sums, late_gated, late_low = together(down_sums, feed_sums, gated, gate_low)
    down_half = fold(bits, down_sums)
    down_half = list(down_half)
    down_half[0], late_gated, late_low = together(down_half[0], late_gated, late_low)
    down_sums = second_swap(down_half)
    out_joined = paired_grads(mixer_grad, late_gated, normed_in, late_low)
    if by_bits():
        out_joined = lax.psum_scatter(out_joined, "dp", scatter_dimension=0, tiled=True)
    pulls, feed_sums, mix_grad = together(pulls, feed_sums, mix_grad)
    feed_sums = first_swap(feed_sums)
    query_grad, key_grad, value_grad, edge, taps_grad, logit_grad = pl_backward(
        pulls, back_transits, proj, taps, info, beta,
        (query, key, value, inverse, fresh, carry), mix_grad, state, heads, seqs, count, size,
    )
    down_joined = join(bits, down_sums)
    edge = shifted(edge, "seq", -1)
    query_grad, out_joined = together(query_grad, out_joined)
    out_joined = swap_add(out_joined, 0)

    feed_sums, edge, out_joined, down_joined, query_grad, key_grad, value_grad, logit_grad = lax.optimization_barrier(
        (feed_sums, edge, out_joined, down_joined, query_grad, key_grad, value_grad, logit_grad)
    )
    sums_down = last_sum(down_joined, cut)
    feed_half = fold(bits, feed_sums)
    feed_half, query_grad, key_grad, value_grad = together(feed_half, query_grad, key_grad, value_grad)
    feed_sums = second_swap(feed_half)
    out_joined = swap_add(out_joined, 1)
    lows = [
        (grad + jnp.pad(edge[kind], ((0, 0), (count - 8, 0), (0, 0)))).astype(bf16).reshape(rows, channels)
        for kind, grad in enumerate((query_grad, key_grad, value_grad))
    ]
    beta_low = logit_grad.astype(bf16).reshape(rows, heads)
    third = channels // 2
    mixed_sums = weight_grads(
        bits,
        normed_in,
        jnp.concatenate([lows[0], lows[2][:, :third]], axis=1),
        normed_in,
        jnp.concatenate([lows[1], lows[2][:, third:]], axis=1),
    )
    mixed_sums, late = together(mixed_sums, lows)
    mixed_sums = first_swap(mixed_sums)
    in_part = (
        nt(late[0], query_weight)
        + nt(late[1], key_weight)
        + nt(late[2], value_weight)
        + nt(gate_low, gate_weight)
        + nt(beta_low, beta_weight)
    )
    grad_beta = tn(normed_in, beta_low)
    in_grad = in_part + swapped(in_part)
    head_part = jnp.sum(gain_grad, axis=0)
    head_part = head_part + swapped(head_part)
    feed_joined = join(bits, feed_sums)
    input_scale = rms_scale(flat_input)
    input_normed = flat_input * input_scale
    grad_mixer_gain = jnp.sum(in_grad * input_normed, axis=0)
    input_grad = own_half(middle_grad + norm_back(in_grad, input_normed, input_scale, mixer_gain), half)

    blocks = lax.axis_size("dp") * lax.axis_size("seq")
    pieces = [
        grad_mixer_gain.reshape(blocks, -1),
        grad_feed_gain.reshape(blocks, -1),
        grad_beta.reshape(blocks, -1),
        taps_grad.reshape(12 * heads, blocks, size // blocks).transpose(1, 0, 2).reshape(blocks, -1),
        head_part.reshape(blocks, -1),
    ]
    small = jnp.concatenate(pieces, axis=1)
    small = jnp.pad(small, ((0, 0), (0, -small.shape[1] % 1024)))
    small = small.reshape(blocks, -1, 128)
    if by_bits():
        small = small_sum(small, "dp")

    sums_feed = last_sum(feed_joined, feed_gate.shape[1])
    mixed_sums, out_joined, small, input_grad, sums_down = lax.optimization_barrier(
        (mixed_sums, out_joined, small, input_grad, sums_down, feed_joined)
    )[:5]
    mixed_sums = second_swap(fold(bits, mixed_sums))
    small = small_sum(small, "seq" if by_bits() else ("dp", "seq")).reshape(-1)
    sums_feed, mixed_sums, small = lax.optimization_barrier((sums_feed, mixed_sums, small))
    sums_mixed = last_sum(join(bits, mixed_sums), channels + third)
    if by_bits():
        out_joined = out_joined.reshape(-1, out_joined.shape[-1])
    else:
        out_joined = lax.psum_scatter(out_joined, ("dp", "seq"), scatter_dimension=0, tiled=True)
    cuts, at = [], 0
    for piece in pieces:
        cuts.append(small[at : at + piece.shape[1]])
        at += piece.shape[1]
    shape = (seqs, count, half)
    return (
        block_output.reshape(shape),
        input_grad.reshape(shape),
        cuts[0],
        sums_mixed[0][:, :channels],
        sums_mixed[1][:, :channels],
        jnp.concatenate([part[:, channels:] for part in sums_mixed], axis=1),
        out_joined[:, channels:],
        cuts[2].reshape(-1, heads),
        cuts[3].reshape(3, 4, heads, size // blocks),
        cuts[4],
        out_joined[:, :channels].T,
        cuts[1],
        sums_feed[0],
        sums_feed[1],
        jnp.concatenate(sums_down, axis=1).T,
    )


def solution(mesh):
    return jax.shard_map(
        local,
        mesh=mesh,
        in_specs=(
            P("dp", "seq", "head"),
            P("dp", "seq"),
            P(),
            P(None, "head"),
            P(None, "head"),
            P(None, "head"),
            P(None, "head"),
            P(None, "head"),
            P(None, None, "head", None),
            P(),
            P("head", None),
            P(),
            P(None, "head"),
            P(None, "head"),
            P("head", None),
            P("dp", "seq", "head"),
        ),
        out_specs=(
            P("dp", "seq", "head"),
            P("dp", "seq", "head"),
            P(("dp", "seq")),
            P(("dp", "seq"), "head"),
            P(("dp", "seq"), "head"),
            P(("dp", "seq"), "head"),
            P(("dp", "seq"), "head"),
            P(("dp", "seq"), "head"),
            P(None, None, "head", ("dp", "seq")),
            P(("dp", "seq")),
            P("head", ("dp", "seq")),
            P(("dp", "seq")),
            P(("dp", "seq"), "head"),
            P(("dp", "seq"), "head"),
            P("head", ("dp", "seq")),
        ),
        check_vma=False,
    )
```

```python
import functools
import math

import jax
import jax.numpy as jnp
from jax import lax
from jax.experimental import pallas as pl
from jax.experimental.pallas import tpu as pltpu
from jax.sharding import PartitionSpec as P

HALO = 16
LONGEST = 512

norm_eps = 1e-05
unit_eps = 1e-06
f32 = jnp.float32
bf16 = jnp.bfloat16
VMEM_LIMIT = 48 * 1024 * 1024


def cost(micros):
    return pl.CostEstimate(flops=int(micros * 1e9), bytes_accessed=1 << 20, transcendentals=0)


def nn(a, b):
    return lax.dot_general(a, b, (((1,), (0,)), ((), ())), preferred_element_type=f32)


def nt(a, b):
    return lax.dot_general(a, b, (((1,), (1,)), ((), ())), preferred_element_type=f32)


def tn(a, b):
    return lax.dot_general(a, b, (((0,), (0,)), ((), ())), preferred_element_type=f32)


def split(value):
    high = value.astype(bf16)
    return high, (value - high.astype(f32)).astype(bf16)


def nn3(a, b):
    a_high, a_low = a
    b_high, b_low = b
    return nn(a_high, b_high) + nn(a_high, b_low) + nn(a_low, b_high)


def sigmoid(value):
    return 1.0 / (1.0 + jnp.exp(-value))


def rms_scale(values):
    return lax.rsqrt(jnp.mean(values * values, axis=-1, keepdims=True) + norm_eps)


def norm_back(grad_rows, normed, row_scale, gain_vec):
    grad_hat = grad_rows * gain_vec
    return row_scale * (grad_hat - normed * jnp.mean(grad_hat * normed, axis=-1, keepdims=True))


def grid_of(size):
    row = lax.broadcasted_iota(jnp.int32, (size, size), 0)
    return row, lax.broadcasted_iota(jnp.int32, (size, size), 1)


def unit_inverses(lowers, size):
    row, col = grid_of(size)
    apart = row ^ col
    eye = jnp.where(apart == 0, 1.0, 0.0)
    inverses = [eye - jnp.where(apart == 1, lower, 0.0) for lower in lowers]
    lows = [lower.astype(bf16) for lower in lowers]
    level = 1
    while (1 << level) < size:
        here = (apart >> level) == 1
        rounded = [inverse.astype(bf16) for inverse in inverses]
        right = [nn(jnp.where(here, low, 0.0), near).astype(bf16) for low, near in zip(lows, rounded)]
        inverses = [inverse - nn(near, far) for inverse, near, far in zip(inverses, rounded, right)]
        level += 1
    parts = [split(inverse) for inverse in inverses]
    wholes = [split(lower) for lower in lowers]
    left = [
        (eye - inverse - nn3(whole, part)).astype(bf16)
        for inverse, whole, part in zip(inverses, wholes, parts)
    ]
    return [inverse + nn(part[0], rest) for inverse, part, rest in zip(inverses, parts, left)]


def conv_taps(proj, seq, taps, kind, info, count, lanes=slice(None)):
    rows = []
    for tap in range(4):
        moved = proj[seq, HALO - 3 + tap : HALO - 3 + tap + count, lanes]
        rows.append(moved if tap == 3 else moved * info[:, tap : tap + 1])
    mixed = rows[0] * taps[kind, 0:1, lanes]
    for tap in range(1, 4):
        mixed = mixed + rows[tap] * taps[kind, tap : tap + 1, lanes]
    return rows, mixed


def turned(info, seq):
    row, col = grid_of(8)
    return tn(info[seq].astype(bf16), jnp.where(row == col, 1.0, 0.0).astype(bf16))


def head_column(table, seq, head):
    lane = lax.broadcasted_iota(jnp.int32, table.shape[1:], 1)
    return jnp.sum(jnp.where(lane == head, table[seq], 0.0), axis=1, keepdims=True)


def forward_kernel(
    seqs, count, size, group,
    query_in, key_in, value_in, taps, info, beta,
    query_out, key_out, value_out, inverse_out, fresh_out, carry_out, local_out, reach_out, state_out, transit_out, both_out,
):
    row, col = grid_of(count)
    scale = 1.0 / math.sqrt(size)
    infos = [turned(info, seq) for seq in range(seqs)]
    sames = [infos[seq][:, 5:6] == info[seq, 5:6, :] for seq in range(seqs)]
    every = [(seq, part, slice(part * size, (part + 1) * size)) for part in range(group) for seq in range(seqs)]
    queries, keys, lowers, betas = [], [], [], []
    for seq, part, lanes in every:
        parts = []
        for kind, proj in enumerate((query_in, key_in, value_in)):
            mixed = conv_taps(proj, seq, taps, kind, infos[seq], count, lanes)[1]
            parts.append(mixed * sigmoid(mixed))
        query, key, value = parts
        query = query * (lax.rsqrt(jnp.sum(query * query, axis=1, keepdims=True) + unit_eps) * scale)
        key = key * lax.rsqrt(jnp.sum(key * key, axis=1, keepdims=True) + unit_eps)
        query, key, value = query.astype(bf16), key.astype(bf16), value.astype(bf16)
        query_out[seq, :, lanes], key_out[seq, :, lanes], value_out[seq, :, lanes] = query, key, value
        beta_col = head_column(beta, seq, pl.program_id(0) * group + part)
        queries.append(query)
        keys.append(key)
        betas.append(beta_col)
        lowers.append(jnp.where(sames[seq] & (row > col), nt(key, key) * beta_col, 0.0))
    inverses = unit_inverses(lowers, count)
    for (seq, part, lanes), query, key, beta_col, inverse in zip(every, queries, keys, betas, inverses):
        enter, last = infos[seq][:, 3:4], infos[seq][:, 4:5]
        key_full = key.astype(f32)
        inverse_parts = split(inverse)
        inverse_out[part, seq] = inverse_parts[0]
        right = jnp.concatenate(
            [key_full * (beta_col * enter), value_out[seq, :, lanes].astype(f32) * beta_col], axis=1
        )
        solved = nn3(inverse_parts, split(right))
        solved_high, solved_low = split(solved)
        key_last = (key_full * last).astype(bf16)
        ends = tn(key_last, solved_high) + tn(key_last, solved_low)
        transit_row, transit_col = grid_of(size)
        eye = jnp.where(transit_row == transit_col, 1.0, 0.0)
        transit = eye * info[seq, 3:4, count - 1 :] - ends[:, :size]
        state_out[seq, part] = ends[:, size:]
        transit_out[seq, part] = transit
        both_out[seq, part, 0] = ends[:, size:]
        both_out[seq, part, 1] = transit
        attend = jnp.where(sames[seq] & (row >= col), nt(query, key), 0.0).astype(bf16)
        reads = nn(attend, solved_high)
        local_out[seq, :, lanes] = reads[:, size:]
        reach_out[seq, :, lanes] = (query.astype(f32) * enter - reads[:, :size]).astype(bf16)
        carry_out[seq, :, lanes] = solved_high[:, :size]
        fresh_out[seq, :, lanes] = solved[:, size:]


def pl_forward(proj, taps, info, beta, group, heads, seqs, count, size, channels):
    def rows(dtype):
        return jax.ShapeDtypeStruct((seqs, count, heads * size), dtype)

    row_spec = pl.BlockSpec((seqs, count, group * size), lambda h: (0, 0, h))
    proj_spec = pl.BlockSpec((seqs, count + HALO, group * size), lambda h: (0, 0, h))
    state = jax.ShapeDtypeStruct((seqs, heads, size, size), f32)
    state_spec = pl.BlockSpec((seqs, group, size, size), lambda h: (0, h, 0, 0))
    return pl.pallas_call(
        functools.partial(forward_kernel, seqs, count, size, group),
        grid=(heads // group,),
        in_specs=[proj_spec] * 3
        + [
            pl.BlockSpec((3, 4, group * size), lambda h: (0, 0, h)),
            pl.BlockSpec(info.shape, lambda h: (0, 0, 0)),
            pl.BlockSpec(beta.shape, lambda h: (0, 0, 0)),
        ],
        out_specs=[row_spec] * 3
        + [pl.BlockSpec((group, seqs, count, count), lambda h: (h, 0, 0, 0))]
        + [row_spec] * 4
        + [state_spec] * 2
        + [pl.BlockSpec((seqs, group, 2, size, size), lambda h: (0, h, 0, 0, 0))],
        out_shape=[rows(bf16)] * 3
        + [jax.ShapeDtypeStruct((heads, seqs, count, count), bf16)]
        + [rows(f32), rows(bf16), rows(f32), rows(bf16)]
        + [state] * 2
        + [jax.ShapeDtypeStruct((seqs, heads, 2, size, size), f32)],
        compiler_params=pltpu.CompilerParams(vmem_limit_bytes=VMEM_LIMIT),
        cost_estimate=cost(17),
    )(*proj, taps, info, beta)


def arrived(boths, farthest, seq):
    total = farthest[seq, 0]
    for both in boths[::-1]:
        total = both[seq, 0, 0] + nn3(split(both[seq, 0, 1]), split(total))
    return total


def read_kernel(seqs, count, size, heads, hops, *refs):
    boths, farthest = refs[: hops - 1], refs[hops - 1]
    local, reach, gate, gain, out_weight, state_out, mix_out, gated_out, part_out, held = refs[hops:]
    head = pl.program_id(0)
    for seq in range(seqs):
        state = arrived(boths, farthest, seq)
        state_out[seq, 0] = state
        state_high, state_low = split(state)
        moved = reach[seq]
        mix = local[seq] + nn(moved, state_high) + nn(moved, state_low)
        mix_out[seq] = mix
        gate_now = gate[seq]
        gated = (mix * rms_scale(mix) * gain[...] * (gate_now * sigmoid(gate_now))).astype(bf16)
        gated_out[seq] = gated
        held[head, seq * count : (seq + 1) * count, :] = gated

    @pl.when(head == heads - 1)
    def _():
        rows = jnp.concatenate([held[h] for h in range(heads)], axis=1)
        part_out[...] = nn(rows, out_weight[...])


def pl_read(boths, farthest, local, reach, gate, gain, out_weight, heads, seqs, count, size, width):
    row_spec = pl.BlockSpec((seqs, count, size), lambda h: (0, 0, h))
    state_spec = pl.BlockSpec((seqs, 1, size, size), lambda h: (0, h, 0, 0))
    both_spec = pl.BlockSpec((seqs, 1, 2, size, size), lambda h: (0, h, 0, 0, 0))
    hops = len(boths) + 1
    return pl.pallas_call(
        functools.partial(read_kernel, seqs, count, size, heads, hops),
        grid=(heads,),
        in_specs=[both_spec] * (hops - 1)
        + [state_spec]
        + [row_spec] * 3
        + [pl.BlockSpec((1, size), lambda h: (0, 0)), pl.BlockSpec((heads * size, width), lambda h: (0, 0))],
        out_specs=[state_spec, row_spec, row_spec, pl.BlockSpec((seqs * count, width), lambda h: (0, 0))],
        out_shape=[
            jax.ShapeDtypeStruct((seqs, heads, size, size), f32),
            jax.ShapeDtypeStruct((seqs, count, heads * size), f32),
            jax.ShapeDtypeStruct((seqs, count, heads * size), bf16),
            jax.ShapeDtypeStruct((seqs * count, width), f32),
        ],
        scratch_shapes=[pltpu.VMEM((heads, seqs * count, size), bf16)],
        compiler_params=pltpu.CompilerParams(vmem_limit_bytes=VMEM_LIMIT),
        cost_estimate=cost(7),
    )(*boths, farthest, local, reach, gate, gain, out_weight)


def hidden_back_kernel(gate_grad, up_grad, feed_gate, feed_up, out):
    out[...] = nt(gate_grad[...], feed_gate[...]) + nt(up_grad[...], feed_up[...])


def pl_hidden_back(gate_grad, up_grad, feed_gate, feed_up):
    rows, hidden = gate_grad.shape
    width = feed_gate.shape[0]
    step = width // 4
    whole = pl.BlockSpec((rows, hidden), lambda i: (0, 0))
    weight = pl.BlockSpec((step, hidden), lambda i: (i, 0))
    return pl.pallas_call(
        hidden_back_kernel,
        grid=(4,),
        in_specs=[whole, whole, weight, weight],
        out_specs=pl.BlockSpec((rows, step), lambda i: (0, i)),
        out_shape=jax.ShapeDtypeStruct((rows, width), f32),
        compiler_params=pltpu.CompilerParams(vmem_limit_bytes=VMEM_LIMIT),
        cost_estimate=cost(6),
    )(gate_grad, up_grad, feed_gate, feed_up)


def gate_back_kernel(
    seqs, count, size,
    mid_part, mid_other, full_grad, middle, feed_gain, out_weight, mix, gate, gain, reach,
    middle_grad, mixer_grad, feed_gain_grad, mix_grad, gate_grad, gain_grad, pull,
):
    head = pl.program_id(0)

    @pl.when(head == 0)
    def _():
        gain_grad[...] = jnp.zeros_like(gain_grad)
        for seq in range(seqs):
            here = slice(seq * count, (seq + 1) * count)
            mid_grad = mid_part[here] + mid_other[here]
            scale = rms_scale(middle[here])
            normed = middle[here] * scale
            share = (mid_grad * normed).reshape(count // 8, 8, normed.shape[1])
            share = jnp.sum(share, axis=0)
            if seq == 0:
                feed_gain_grad[...] = share
            else:
                feed_gain_grad[...] += share
            whole = full_grad[here] + norm_back(mid_grad, normed, scale, feed_gain[...])
            middle_grad[here] = whole
            mixer_grad[here] = whole.astype(bf16)

    grads = nt(mixer_grad[...], out_weight[...])
    for seq in range(seqs):
        grad = grads[seq * count : (seq + 1) * count]
        mix_now, gate_now = mix[seq], gate[seq]
        scale = rms_scale(mix_now)
        normed = mix_now * scale
        sig = sigmoid(gate_now)
        gate_silu = gate_now * sig
        with_norm = grad * normed
        gain_grad[...] += jnp.sum((with_norm * gate_silu).reshape(count // 8, 8, size), axis=0)
        gate_grad[seq] = (with_norm * gain[...] * (sig * (1.0 + gate_now * (1.0 - sig)))).astype(bf16)
        normed_grad = grad * gain[...] * gate_silu
        mix_grad_now = scale * (normed_grad - normed * jnp.mean(normed_grad * normed, axis=1, keepdims=True))
        low = mix_grad_now.astype(bf16)
        mix_grad[seq] = low
        pull[seq, 0] = tn(reach[seq], low)


def pl_gate_back(
    mid_part, mid_other, full_grad, middle, feed_gain, out_weight, mix, gate, gain, reach, heads, seqs, count, size
):
    rows, width = middle.shape
    row_spec = pl.BlockSpec((seqs, count, size), lambda h: (0, 0, h))

    def fixed(*dims):
        return pl.BlockSpec(dims, lambda h: (0,) * len(dims))

    return pl.pallas_call(
        functools.partial(gate_back_kernel, seqs, count, size),
        grid=(heads,),
        in_specs=[fixed(rows, width)] * 4
        + [
            fixed(1, width),
            pl.BlockSpec((size, width), lambda h: (h, 0)),
            row_spec,
            row_spec,
            fixed(1, size),
            row_spec,
        ],
        out_specs=[
            fixed(rows, width),
            fixed(rows, width),
            fixed(8, width),
            row_spec,
            row_spec,
            fixed(8, size),
            pl.BlockSpec((seqs, 1, size, size), lambda h: (0, h, 0, 0)),
        ],
        out_shape=[
            jax.ShapeDtypeStruct((rows, width), f32),
            jax.ShapeDtypeStruct((rows, width), bf16),
            jax.ShapeDtypeStruct((8, width), f32),
            jax.ShapeDtypeStruct((seqs, count, heads * size), bf16),
            jax.ShapeDtypeStruct((seqs, count, heads * size), bf16),
            jax.ShapeDtypeStruct((8, size), f32),
            jax.ShapeDtypeStruct((seqs, heads, size, size), f32),
        ],
        compiler_params=pltpu.CompilerParams(vmem_limit_bytes=VMEM_LIMIT),
        cost_estimate=cost(9),
    )(mid_part, mid_other, full_grad, middle, feed_gain, out_weight, mix, gate, gain, reach)


def backward_kernel(seqs, count, size, hops, *refs):
    pulls, transits = refs[:hops], refs[hops : 2 * hops - 1]
    (
        query_in, key_in, value_in, taps, info_rows, beta,
        query_ref, key_ref, value_ref, inverse_ref, fresh_ref, carry_ref, mix_grad_ref, state_ref,
        query_grad_out, key_grad_out, value_grad_out, edge_out, taps_grad_out, logit_grad_out,
    ) = refs[2 * hops - 1 :]
    head = pl.program_id(0)
    row, col = grid_of(count)
    scale = 1.0 / math.sqrt(size)

    @pl.when(head == 0)
    def _():
        logit_grad_out[...] = jnp.zeros_like(logit_grad_out)

    taps_totals = None
    for seq in range(seqs):
        total = pulls[-1][seq, 0]
        for pull, transit in zip(pulls[-2::-1], transits[::-1]):
            transit_high, transit_low = split(transit[seq, 0])
            total_high, total_low = split(total)
            total = pull[seq, 0] + (
                tn(transit_high, total_high) + tn(transit_high, total_low) + tn(transit_low, total_high)
            )
        out_state_grad = total.astype(bf16)
        state = state_ref[seq, 0].astype(bf16)
        query, key, value = query_ref[seq], key_ref[seq], value_ref[seq]
        mix_grad = mix_grad_ref[seq]
        info = turned(info_rows, seq)
        enter, last = info[:, 3:4], info[:, 4:5]
        same = info[:, 5:6] == info_rows[seq, 5:6, :]
        causal = same & (row >= col)
        strict = same & (row > col)
        beta_col = head_column(beta, seq, head)
        key_full = key.astype(f32)
        key_last = (key_full * last).astype(bf16)
        update = (fresh_ref[seq] - nn(carry_ref[seq], state)).astype(bf16)
        attend = jnp.where(causal, nt(query, key), 0.0).astype(bf16)
        update_grad = tn(attend, mix_grad) + nn(key_last, out_state_grad)
        right_grad = tn(inverse_ref[0, seq], update_grad.astype(bf16))
        right_low = right_grad.astype(bf16)
        both = nt(jnp.concatenate([mix_grad, right_low], axis=0), update)
        attend_grad = jnp.where(causal, both[:count], 0.0).astype(bf16)
        lower_grad = jnp.where(strict, -both[count:], 0.0)
        gram = nt(key, key)
        surprise = value.astype(f32) - enter * nn(key, state)
        beta_grad = jnp.sum(right_grad * surprise, axis=1, keepdims=True) + jnp.sum(
            lower_grad * gram, axis=1, keepdims=True
        )
        logit_grad = beta_grad * beta_col * (1.0 - beta_col)
        lane = lax.broadcasted_iota(jnp.int32, logit_grad_out.shape[1:], 1)
        logit_grad_out[seq] += jnp.where(lane == head, logit_grad, 0.0)
        value_grad = right_grad * beta_col
        gram_grad = (lower_grad * beta_col).astype(bf16)
        stacked = jnp.concatenate([gram_grad, attend_grad], axis=0)
        forth = nn(stacked, key)
        back = tn(stacked, jnp.concatenate([key, query], axis=0))
        through = nt(
            jnp.concatenate([(value_grad * enter).astype(bf16), mix_grad], axis=0), state
        )
        key_grad = forth[:count] + back - through[:count] + last * nt(update, out_state_grad)
        query_grad = forth[count:] + enter * through[count:]
        for kind, (proj, grad, out) in enumerate(
            (
                (query_in, query_grad, query_grad_out),
                (key_in, key_grad, key_grad_out),
                (value_in, value_grad, value_grad_out),
            )
        ):
            rows, mixed = conv_taps(proj, seq, taps, kind, info, count)
            sig = sigmoid(mixed)
            if kind < 2:
                active = mixed * sig
                norm = lax.rsqrt(jnp.sum(active * active, axis=1, keepdims=True) + unit_eps)
                unit = active * norm
                grad = grad - unit * jnp.sum(grad * unit, axis=1, keepdims=True)
                grad = grad * (norm * scale if kind == 0 else norm)
            mixed_grad = grad * (sig * (1.0 + mixed * (1.0 - sig)))
            sums = [jnp.sum((mixed_grad * rows[tap]).reshape(count // 8, 8, size), axis=0) for tap in range(4)]
            blank = jnp.zeros((8, size), f32)
            proj_grad = mixed_grad * taps[kind, 3:4, :]
            edge = blank
            for tap in range(3):
                delay = 3 - tap
                masked = mixed_grad * (info[:, tap : tap + 1] * taps[kind, tap : tap + 1, :])
                moved = pltpu.roll(masked, count - delay, 0)
                at = lax.broadcasted_iota(jnp.int32, (count, size), 0)
                proj_grad = proj_grad + jnp.where(at < count - delay, moved, 0.0)
                first = pltpu.roll(masked[:8], 8 - delay, 0)
                at_edge = lax.broadcasted_iota(jnp.int32, (8, size), 0)
                edge = edge + jnp.where(at_edge >= 8 - delay, first, 0.0)
            out[seq] = proj_grad
            edge_out[kind, seq] = edge
            sums = jnp.stack([jnp.sum(part, axis=0) for part in sums])
            if seq == 0:
                taps_grad_out[kind] = sums
            else:
                taps_grad_out[kind] += sums


def pl_backward(pulls, transits, proj, taps, info, beta, saved, mix_grad, state, heads, seqs, count, size):
    hops = len(pulls)
    row_spec = pl.BlockSpec((seqs, count, size), lambda h: (0, 0, h))
    state_spec = pl.BlockSpec((seqs, 1, size, size), lambda h: (0, h, 0, 0))
    proj_spec = pl.BlockSpec((seqs, count + HALO, size), lambda h: (0, 0, h))
    return pl.pallas_call(
        functools.partial(backward_kernel, seqs, count, size, hops),
        grid=(heads,),
        in_specs=[state_spec] * (2 * hops - 1)
        + [proj_spec] * 3
        + [
            pl.BlockSpec((3, 4, size), lambda h: (0, 0, h)),
            pl.BlockSpec(info.shape, lambda h: (0, 0, 0)),
            pl.BlockSpec(beta.shape, lambda h: (0, 0, 0)),
        ]
        + [row_spec] * 3
        + [pl.BlockSpec((1, seqs, count, count), lambda h: (h, 0, 0, 0))]
        + [row_spec] * 3
        + [state_spec],
        out_specs=[row_spec] * 3
        + [
            pl.BlockSpec((3, seqs, 8, size), lambda h: (0, 0, 0, h)),
            pl.BlockSpec((3, 4, size), lambda h: (0, 0, h)),
            pl.BlockSpec((seqs, count, heads), lambda h: (0, 0, 0)),
        ],
        out_shape=[jax.ShapeDtypeStruct((seqs, count, heads * size), f32)] * 3
        + [
            jax.ShapeDtypeStruct((3, seqs, 8, heads * size), f32),
            jax.ShapeDtypeStruct((3, 4, heads * size), f32),
            jax.ShapeDtypeStruct((seqs, count, heads), f32),
        ],
        compiler_params=pltpu.CompilerParams(vmem_limit_bytes=VMEM_LIMIT),
        cost_estimate=cost(17),
    )(*pulls, *transits, *proj, taps, info, beta, *saved, mix_grad, state)


def input_back_kernel(first, second, gate_grad, beta_grad, query_w, key_w, value_w, gate_w, beta_w, out):
    channels = query_w.shape[1]
    third = channels // 2
    out[...] = (
        nt(first[:, :channels], query_w[...])
        + nt(second[:, :channels], key_w[...])
        + nt(first[:, channels:], value_w[:, :third])
        + nt(second[:, channels:], value_w[:, third:])
        + nt(gate_grad[...], gate_w[...])
        + nt(beta_grad[...], beta_w[...])
    )


def pl_input_back(grads, weights):
    rows = grads[0].shape[0]
    width = weights[0].shape[0]
    step = width // 4
    return pl.pallas_call(
        input_back_kernel,
        grid=(4,),
        in_specs=[pl.BlockSpec(grad.shape, lambda i: (0, 0)) for grad in grads]
        + [pl.BlockSpec((step, weight.shape[1]), lambda i: (i, 0)) for weight in weights],
        out_specs=pl.BlockSpec((rows, step), lambda i: (0, i)),
        out_shape=jax.ShapeDtypeStruct((rows, width), f32),
        compiler_params=pltpu.CompilerParams(vmem_limit_bytes=VMEM_LIMIT),
        cost_estimate=cost(1),
    )(*grads, *weights)


def input_norm_kernel(which, part, other, value, middle_grad, gain, out, gain_grad):
    grad = part[...] + other[...]
    scale = rms_scale(value[...])
    normed = value[...] * scale
    share = jnp.sum((grad * normed).reshape(grad.shape[0] // 8, 8, grad.shape[1]), axis=0)

    @pl.when(pl.program_id(0) == 0)
    def _():
        gain_grad[...] = share

    @pl.when(pl.program_id(0) > 0)
    def _():
        gain_grad[...] += share

    result = middle_grad[...] + norm_back(grad, normed, scale, gain[...])
    half = out.shape[1]
    out[...] = jnp.where(which[0] == 0, result[:, :half], result[:, half:])


def pl_input_norm(which, part, other, value, middle_grad, gain, steps):
    rows, width = value.shape
    tall = pl.BlockSpec((rows // steps, width), lambda i, which: (i, 0))
    return pl.pallas_call(
        input_norm_kernel,
        grid_spec=pltpu.PrefetchScalarGridSpec(
            num_scalar_prefetch=1,
            grid=(steps,),
            in_specs=[tall] * 4 + [pl.BlockSpec((1, width), lambda i, which: (0, 0))],
            out_specs=[
                pl.BlockSpec((rows // steps, width // 2), lambda i, which: (i, 0)),
                pl.BlockSpec((8, width), lambda i, which: (0, 0)),
            ],
        ),
        out_shape=[jax.ShapeDtypeStruct((rows, width // 2), f32), jax.ShapeDtypeStruct((8, width), f32)],
        compiler_params=pltpu.CompilerParams(vmem_limit_bytes=VMEM_LIMIT),
        cost_estimate=cost(1),
    )(which, part, other, value, middle_grad, gain)


def shifted(value, axis, steps):
    count = lax.axis_size(axis)
    initial, last = (max(0, -steps), min(count, count - steps))
    return lax.ppermute(value, axis, [(source, source + steps) for source in range(initial, last)])


def swapped(value):
    return lax.ppermute(value, "head", [(0, 1), (1, 0)])


def in_order(own, other, axis):
    mine = lax.axis_index("head") == 0
    return jnp.where(
        mine, jnp.concatenate([own, other], axis=axis), jnp.concatenate([other, own], axis=axis)
    )


def own_half(value, half):
    return lax.dynamic_slice_in_dim(value, lax.axis_index("head") * half, half, value.ndim - 1)


def pick(value, index, axis):
    return lax.dynamic_index_in_dim(value, index, axis, keepdims=False)


def together(*values):
    return lax.optimization_barrier(values)


def weight_kernel(block, first_window, second_window, bits, first_left, first_right, second_left, second_right, *refs):
    first_leaves, first_stays, second_leaves, second_stays, held, held_second = refs
    low, high = bits[0], bits[1]
    held[...] = tn(first_left[...], first_right[:, first_window])
    for part in range(2):
        base = part * 2 * block
        first_leaves[0, part] = held[pl.ds(pl.multiple_of(base + (1 - low) * block, 8), block), :]
        first_stays[0, part] = held[pl.ds(pl.multiple_of(base + low * block, 8), block), :]
    held_second[...] = tn(second_left[...], second_right[:, second_window])
    second_leaves[0] = held_second[pl.ds(pl.multiple_of((1 - high) * 2 * block, 8), 2 * block), :]
    second_stays[0] = held_second[pl.ds(pl.multiple_of(high * 2 * block, 8), 2 * block), :]


def fold_kernel(block, bits, first_stays, first_comes, second_stays, second_comes, *refs):
    first_leaves, first_keeps, second_leaves, second_keeps = refs
    low, high = bits[0], bits[1]
    first_leaves[0] = first_stays[0, 1 - high] + first_comes[0, 1 - high]
    first_keeps[0] = first_stays[0, high] + first_comes[0, high]
    away = pl.ds(pl.multiple_of((1 - low) * block, 8), block)
    here = pl.ds(pl.multiple_of(low * block, 8), block)
    second_leaves[0] = second_stays[0, away] + second_comes[0, away]
    second_keeps[0] = second_stays[0, here] + second_comes[0, here]


def join_kernel(pieces, bits, first_keeps, first_comes, second_keeps, second_comes, out):
    first, second = first_keeps.shape[-1] // pieces, second_keeps.shape[-1] // pieces
    at = 0
    for piece in range(pieces):
        lanes = slice(piece * first, (piece + 1) * first)
        out[:, at : at + first] = first_keeps[0, :, lanes] + first_comes[0, :, lanes]
        at += first
        lanes = slice(piece * second, (piece + 1) * second)
        out[:, at : at + second] = second_keeps[0, :, lanes] + second_comes[0, :, lanes]
        at += second


def per_block(kernel, bits, steps, args, in_specs, out_specs, out_shape, scratch=()):
    return pl.pallas_call(
        kernel,
        grid_spec=pltpu.PrefetchScalarGridSpec(
            num_scalar_prefetch=1, grid=(steps,), in_specs=in_specs, out_specs=out_specs, scratch_shapes=list(scratch)
        ),
        out_shape=out_shape,
        compiler_params=pltpu.CompilerParams(vmem_limit_bytes=VMEM_LIMIT),
        cost_estimate=cost(1),
    )(bits, *args)


def four_block(dims):
    return pl.BlockSpec((1,) + dims, lambda z, bits: (z,) + (0,) * len(dims))


def swap_bit(value, bit):
    return lax.ppermute(value, "seq", [(source, source ^ (1 << bit)) for source in range(4)])


def by_bits():
    return lax.axis_size("seq") == 4


def weight_grads(bits, first_left, first_right, second_left, second_right, first_window=None, second_window=None):
    first_window = first_window or slice(0, first_right.shape[1])
    second_window = second_window or slice(0, second_right.shape[1])
    if not by_bits():
        return tn(first_left, first_right[:, first_window]), tn(second_left, second_right[:, second_window])
    dp = lax.axis_size("dp")
    tokens, rows = first_left.shape
    first_cols = first_window.stop - first_window.start
    second_cols = second_window.stop - second_window.start
    block = rows // (4 * dp)
    left_spec = pl.BlockSpec((tokens, 4 * block), lambda z, bits: (0, z))

    def whole(cols):
        return pl.BlockSpec((tokens, cols), lambda z, bits: (0, 0))

    first, second = (2, block, first_cols), (2 * block, second_cols)
    return per_block(
        functools.partial(weight_kernel, block, first_window, second_window),
        bits,
        dp,
        (first_left, first_right, second_left, second_right),
        [left_spec, whole(first_right.shape[1]), left_spec, whole(second_right.shape[1])],
        [four_block(dims) for dims in (first, first, second, second)],
        [jax.ShapeDtypeStruct((dp,) + dims, f32) for dims in (first, first, second, second)],
        [pltpu.VMEM((4 * block, first_cols), f32), pltpu.VMEM((4 * block, second_cols), f32)],
    )


def paired_kernel(first_left, first_right, second_left, second_right, out):
    cut = first_right.shape[1]
    out[:, :cut] = tn(first_left[...], first_right[...])
    out[:, cut:] = tn(second_left[...], second_right[...])


def paired_grads(first_left, first_right, second_left, second_right):
    tokens, rows = first_left.shape
    cols = first_right.shape[1] + second_right.shape[1]
    step = rows // 4
    left_spec = pl.BlockSpec((tokens, step), lambda i: (0, i))
    whole = [pl.BlockSpec(right.shape, lambda i: (0, 0)) for right in (first_right, second_right)]
    return pl.pallas_call(
        paired_kernel,
        grid=(4,),
        in_specs=[left_spec, whole[0], left_spec, whole[1]],
        out_specs=pl.BlockSpec((step, cols), lambda i: (i, 0)),
        out_shape=jax.ShapeDtypeStruct((rows, cols), f32),
        compiler_params=pltpu.CompilerParams(vmem_limit_bytes=VMEM_LIMIT),
        cost_estimate=cost(4),
    )(first_left, first_right, second_left, second_right)


def first_swap(parts):
    if not by_bits():
        return parts
    first_leaves, first_stays, second_leaves, second_stays = parts
    return first_stays, swap_bit(first_leaves, 0), second_stays, swap_bit(second_leaves, 1)


def fold(bits, parts):
    if not by_bits():
        return parts
    dp = lax.axis_size("dp")
    block, first_cols, second_cols = parts[0].shape[2], parts[0].shape[3], parts[2].shape[2]
    ins = [(2, block, first_cols)] * 2 + [(2 * block, second_cols)] * 2
    outs = [(block, first_cols)] * 2 + [(block, second_cols)] * 2
    return per_block(
        functools.partial(fold_kernel, block),
        bits,
        dp,
        parts,
        [four_block(dims) for dims in ins],
        [four_block(dims) for dims in outs],
        [jax.ShapeDtypeStruct((dp,) + dims, f32) for dims in outs],
    )


def fold_two_kernel(block, bits, *refs):
    low, high = bits[0], bits[1]
    first_leaves, first_keeps, second_leaves, second_keeps = refs[8:]
    away = pl.ds(pl.multiple_of((1 - low) * block, 8), block)
    here = pl.ds(pl.multiple_of(low * block, 8), block)
    first_at = second_at = 0
    for first_stays, first_comes, second_stays, second_comes in (refs[:4], refs[4:8]):
        lanes = slice(first_at, first_at + first_stays.shape[-1])
        first_leaves[0, :, lanes] = first_stays[0, 1 - high] + first_comes[0, 1 - high]
        first_keeps[0, :, lanes] = first_stays[0, high] + first_comes[0, high]
        first_at = lanes.stop
        lanes = slice(second_at, second_at + second_stays.shape[-1])
        second_leaves[0, :, lanes] = second_stays[0, away] + second_comes[0, away]
        second_keeps[0, :, lanes] = second_stays[0, here] + second_comes[0, here]
        second_at = lanes.stop


def fold_two(bits, one, two):
    if not by_bits():
        return one + two
    dp = lax.axis_size("dp")
    block = one[0].shape[2]
    ins, outs = [], [0, 0]
    for part in (one, two):
        first_cols, second_cols = part[0].shape[3], part[2].shape[2]
        ins += [(2, block, first_cols)] * 2 + [(2 * block, second_cols)] * 2
        outs = [outs[0] + first_cols, outs[1] + second_cols]
    outs = [(block, outs[0])] * 2 + [(block, outs[1])] * 2
    return per_block(
        functools.partial(fold_two_kernel, block),
        bits,
        dp,
        tuple(one) + tuple(two),
        [four_block(dims) for dims in ins],
        [four_block(dims) for dims in outs],
        [jax.ShapeDtypeStruct((dp,) + dims, f32) for dims in outs],
    )


def second_swap(parts):
    if not by_bits():
        return parts
    first_leaves, first_keeps, second_leaves, second_keeps = parts
    return first_keeps, swap_bit(first_leaves, 1), second_keeps, swap_bit(second_leaves, 0)


def join(bits, parts, pieces=1):
    if not by_bits():
        return tuple(
            lax.psum_scatter(part, ("dp", "seq"), scatter_dimension=0, tiled=True) for part in parts
        )
    dp = lax.axis_size("dp")
    block, first_cols, second_cols = parts[0].shape[1], parts[0].shape[2], parts[2].shape[2]
    return per_block(
        functools.partial(join_kernel, pieces),
        bits,
        dp,
        parts,
        [four_block((block, cols)) for cols in (first_cols, first_cols, second_cols, second_cols)],
        pl.BlockSpec((block, first_cols + second_cols), lambda z, bits: (z, 0)),
        jax.ShapeDtypeStruct((dp * block, first_cols + second_cols), f32),
    )


def last_sum(joined):
    if not by_bits():
        return jnp.concatenate(joined, axis=1)
    return lax.psum_scatter(joined, "dp", scatter_dimension=0, tiled=True)


def swap_add(value, bit):
    if not by_bits():
        return value
    value = value.reshape(2 - bit, 2, -1, value.shape[-1])
    mine = (lax.axis_index("seq") >> bit) & 1
    return pick(value, mine, 1) + swap_bit(pick(value, 1 - mine, 1), bit)


def small_sum(value, names):
    if not by_bits():
        return lax.psum_scatter(value, names, scatter_dimension=0, tiled=True)
    if names == "dp" and lax.axis_size("dp") != 4:
        return lax.psum_scatter(value, "dp", scatter_dimension=0, tiled=True)
    value = value.reshape((2, 2) + (value.shape[0] // 4,) + value.shape[1:])
    for bit in range(2):
        mine = (lax.axis_index(names) >> bit) & 1
        perm = [(source, source ^ (1 << bit)) for source in range(4)]
        value = pick(value, mine, 1 - bit) + lax.ppermute(pick(value, 1 - mine, 1 - bit), names, perm)
    return value


def local(
    block_input,
    segment_ids,
    mixer_gain,
    query_weight,
    key_weight,
    value_weight,
    gate_weight,
    beta_weight,
    conv_weight,
    head_gain,
    out_weight,
    feed_gain,
    feed_gate,
    feed_up,
    feed_down,
    grad_output,
):
    seqs, count, half = block_input.shape
    rows = seqs * count
    size = head_gain.shape[0]
    heads = beta_weight.shape[1]
    channels = heads * size
    width = query_weight.shape[0]
    hops = -(-(LONGEST - 1) // count)
    hops = min(hops, lax.axis_size("seq") - 1)

    other_input = swapped(block_input)
    segments = segment_ids.astype(f32)
    before = shifted(
        jnp.concatenate([block_input[:, count - 3 :], segments[:, count - 3 :, None]], axis=2), "seq", 1
    )
    edge_ids = before[:, :, half]
    before = before[:, :, :half]
    other_before = swapped(before)
    full_input = in_order(block_input, other_input, 2)
    full_before = in_order(before, other_before, 2)
    other_grad = swapped(grad_output)

    extended = jnp.concatenate(
        [jnp.zeros((seqs, HALO - 3, width), f32), full_before, full_input], axis=1
    )
    extended_low = (extended * rms_scale(extended) * mixer_gain).astype(bf16)
    flat = extended_low.reshape(seqs * (count + HALO), width)
    proj = [
        nn(flat, weight).reshape(seqs, count + HALO, channels)
        for weight in (query_weight, key_weight, value_weight)
    ]
    normed_in = extended_low[:, HALO:].reshape(rows, width)
    beta = jax.nn.sigmoid(nn(normed_in, beta_weight)).reshape(seqs, count, heads)
    gate_proj = nn(normed_in, gate_weight).reshape(seqs, count, channels)

    extended_ids = jnp.concatenate([edge_ids, segments], axis=1)
    masks = [(extended_ids[:, tap : tap + count] == segments) for tap in range(3)]
    enter = segments == edge_ids[:, 2:3]
    last = segments == segments[:, count - 1 :]
    zero = jnp.zeros_like(segments)
    info = jnp.stack(
        [mask.astype(f32) for mask in masks] + [enter.astype(f32), last.astype(f32), segments, zero, zero], axis=1
    )
    taps = conv_weight.reshape(3, 4, channels)
    gain = head_gain[None, :]

    (query, key, value, inverse, fresh, carry, local_mix, reach, state_end, transit, both) = pl_forward(
        proj, taps, info, beta, 2 if heads % 2 == 0 else 1, heads, seqs, count, size, channels
    )
    boths = [shifted(both, "seq", hop) for hop in range(1, hops)]
    farthest = shifted(state_end, "seq", hops)
    back_transits = [shifted(transit, "seq", -hop) for hop in range(1, hops)]
    boths, farthest, back_transits = lax.optimization_barrier((boths, farthest, back_transits))
    state, mix, gated, part = pl_read(
        boths, farthest, local_mix, reach, gate_proj, gain, out_weight, heads, seqs, count, size, width
    )
    gated = gated.reshape(rows, channels)
    flat_input = full_input.reshape(rows, width)
    middle = flat_input + (part + swapped(part))
    middle_scale = rms_scale(middle)
    middle_normed = middle * middle_scale
    normed_mid = (middle_normed * feed_gain).astype(bf16)
    gate_act = nn(normed_mid, feed_gate)
    up_act = nn(normed_mid, feed_up)
    gate_sig = jax.nn.sigmoid(gate_act)
    gate_silu = gate_act * gate_sig
    inner = (gate_silu * up_act).astype(bf16)
    full_grad = in_order(grad_output, other_grad, 2).reshape(rows, width)
    down_grad = full_grad.astype(bf16)
    cut = feed_down.shape[0] // 256 * 128
    inner_grad = nt(down_grad, feed_down)
    gate_grad = (inner_grad * up_act * (gate_sig * (1.0 + gate_act * (1.0 - gate_sig)))).astype(bf16)
    up_grad = (inner_grad * gate_silu).astype(bf16)
    place = lax.axis_index("seq")
    bits = jnp.stack([place & 1, (place >> 1) & 1]).astype(jnp.int32)
    mid_part = pl_hidden_back(gate_grad, up_grad, feed_gate, feed_up)
    mid_part, late_inner = together(mid_part, inner)
    mid_other = swapped(mid_part)
    down_sums = weight_grads(
        bits, down_grad, late_inner, down_grad, late_inner, slice(0, cut), slice(cut, inner.shape[1])
    )
    down_sums, mid_part = together(down_sums, mid_part)
    down_sums = first_swap(down_sums)
    down_part = nn(inner, feed_down)
    mine = lax.axis_index("head")
    down_out = lax.dynamic_slice_in_dim(down_part, (1 - mine) * half, half, 1)
    block_output = own_half(middle, half) + (own_half(down_part, half) + swapped(down_out))

    middle_grad, mixer_grad, feed_gain_grad, mix_grad, gate_low, gain_grad, pull = pl_gate_back(
        mid_part, mid_other, full_grad, middle, feed_gain[None, :], out_weight, mix, gate_proj, gain, reach,
        heads, seqs, count, size,
    )
    grad_feed_gain = jnp.sum(feed_gain_grad, axis=0)
    gate_low = gate_low.reshape(rows, channels)
    pull, late_gate, late_up, late_gated, late_low = together(pull, gate_grad, up_grad, gated, gate_low)
    pulls = [shifted(pull, "seq", -hop) for hop in range(1, hops + 1)]
    halves = slice(0, cut), slice(cut, inner.shape[1])
    gate_sums = weight_grads(bits, normed_mid, late_gate, normed_mid, late_gate, *halves)
    out_joined = paired_grads(mixer_grad, late_gated, normed_in, late_low)
    down_sums, gate_sums, out_joined, late_up = together(down_sums, gate_sums, out_joined, late_up)
    if by_bits():
        out_joined = lax.psum_scatter(out_joined, "dp", scatter_dimension=0, tiled=True)
    down_half = list(fold(bits, down_sums))
    up_sums = weight_grads(bits, normed_mid, late_up, normed_mid, late_up, *halves)

    leaving = list(down_half)
    pulls, gate_sums, mix_grad, down_half[1], up_sums = together(pulls, gate_sums, mix_grad, down_half[1], up_sums)
    leaving[1] = down_half[1]
    down_sums = second_swap(leaving)
    gate_sums = first_swap(gate_sums)
    query_grad, key_grad, value_grad, edge, taps_grad, logit_grad = pl_backward(
        pulls, back_transits, proj, taps, info, beta,
        (query, key, value, inverse, fresh, carry), mix_grad, state, heads, seqs, count, size,
    )
    edge = shifted(edge, "seq", -1)

    gate_sums, edge, down_sums, up_sums, query_grad, key_grad, value_grad, logit_grad, taps_grad = together(
        gate_sums, edge, down_sums, up_sums, query_grad, key_grad, value_grad, logit_grad, taps_grad
    )
    up_sums = first_swap(up_sums)
    query_grad, key_grad, value_grad = (
        (grad + jnp.pad(edge[kind], ((0, 0), (count - 8, 0), (0, 0)))).astype(bf16).reshape(rows, channels)
        for kind, grad in enumerate((query_grad, key_grad, value_grad))
    )
    third = channels // 2
    first_grads = jnp.concatenate([query_grad, value_grad[:, :third]], axis=1)
    second_grads = jnp.concatenate([key_grad, value_grad[:, third:]], axis=1)
    mixed_sums = weight_grads(bits, normed_in, first_grads, normed_in, second_grads)
    beta_low = logit_grad.astype(bf16).reshape(rows, heads)
    in_part = pl_input_back(
        (first_grads, second_grads, gate_low, beta_low),
        (query_weight, key_weight, value_weight, gate_weight, beta_weight),
    )
    down_joined = join(bits, down_sums)
    mixed_sums, gate_sums, up_sums, down_joined, out_joined, in_part = together(
        mixed_sums, gate_sums, up_sums, down_joined, out_joined, in_part
    )
    sums_down = last_sum(down_joined)
    feed_half = fold_two(bits, tuple(gate_sums), tuple(up_sums))
    mixed_sums, feed_half = together(mixed_sums, feed_half)
    feed_sums = second_swap(feed_half)
    mixed_sums = first_swap(mixed_sums)
    feed_joined = join(bits, feed_sums, 2)
    sums_feed = last_sum(feed_joined)
    mixed_sums, sums_down = together(mixed_sums, sums_down, feed_joined)[:2]
    mixed_half = fold(bits, mixed_sums)
    mixed_sums = second_swap(mixed_half)
    mixed_joined = join(bits, mixed_sums)
    mixed_joined, out_joined, beta_low, in_part, sums_feed = together(
        mixed_joined, out_joined, beta_low, in_part, sums_feed
    )
    sums_mixed = last_sum(mixed_joined)
    input_grad, mixer_gain_grad = pl_input_norm(
        mine[None].astype(jnp.int32), in_part, swapped(in_part), flat_input, middle_grad, mixer_gain[None, :], seqs
    )

    out_joined = swap_add(swap_add(out_joined, 0), 1)
    grad_beta = tn(normed_in, beta_low)
    head_part = jnp.sum(gain_grad, axis=0)
    head_part = head_part + swapped(head_part)
    grad_mixer_gain = jnp.sum(mixer_gain_grad, axis=0)

    blocks = lax.axis_size("dp") * lax.axis_size("seq")
    pieces = [
        grad_mixer_gain.reshape(blocks, -1),
        grad_feed_gain.reshape(blocks, -1),
        grad_beta.reshape(blocks, -1),
        taps_grad.reshape(12 * heads, blocks, size // blocks).transpose(1, 0, 2).reshape(blocks, -1),
        head_part.reshape(blocks, -1),
    ]
    small = jnp.concatenate(pieces, axis=1)
    small = jnp.pad(small, ((0, 0), (0, -small.shape[1] % 1024)))
    small = small.reshape(blocks, -1, 128)
    if by_bits():
        small = small_sum(small_sum(small, "dp"), "seq")
    else:
        small = small_sum(small, ("dp", "seq"))
    small = small.reshape(-1)
    if by_bits():
        out_joined = out_joined.reshape(-1, out_joined.shape[-1])
    else:
        out_joined = lax.psum_scatter(out_joined, ("dp", "seq"), scatter_dimension=0, tiled=True)
    cuts, at = [], 0
    for piece in pieces:
        cuts.append(small[at : at + piece.shape[1]])
        at += piece.shape[1]
    shape = (seqs, count, half)
    hidden = feed_gate.shape[1]
    wide = channels + third
    return (
        block_output.reshape(shape),
        input_grad.reshape(shape),
        cuts[0],
        sums_mixed[:, :channels],
        sums_mixed[:, wide : wide + channels],
        jnp.concatenate([sums_mixed[:, channels:wide], sums_mixed[:, wide + channels :]], axis=1),
        out_joined[:, channels:],
        cuts[2].reshape(-1, heads),
        cuts[3].reshape(3, 4, heads, size // blocks),
        cuts[4],
        out_joined[:, :channels].T,
        cuts[1],
        sums_feed[:, :hidden],
        sums_feed[:, hidden:],
        sums_down.T,
    )


def solution(mesh):
    return jax.shard_map(
        local,
        mesh=mesh,
        in_specs=(
            P("dp", "seq", "head"),
            P("dp", "seq"),
            P(),
            P(None, "head"),
            P(None, "head"),
            P(None, "head"),
            P(None, "head"),
            P(None, "head"),
            P(None, None, "head", None),
            P(),
            P("head", None),
            P(),
            P(None, "head"),
            P(None, "head"),
            P("head", None),
            P("dp", "seq", "head"),
        ),
        out_specs=(
            P("dp", "seq", "head"),
            P("dp", "seq", "head"),
            P(("dp", "seq")),
            P(("dp", "seq"), "head"),
            P(("dp", "seq"), "head"),
            P(("dp", "seq"), "head"),
            P(("dp", "seq"), "head"),
            P(("dp", "seq"), "head"),
            P(None, None, "head", ("dp", "seq")),
            P(("dp", "seq")),
            P("head", ("dp", "seq")),
            P(("dp", "seq")),
            P(("dp", "seq"), "head"),
            P(("dp", "seq"), "head"),
            P("head", ("dp", "seq")),
        ),
        check_vma=False,
    )
```

```python
import functools
import math

import jax
import jax.numpy as jnp
from jax import lax
from jax.experimental import pallas as pl
from jax.experimental.pallas import tpu as pltpu
from jax.sharding import PartitionSpec as P

HALO = 16
LONGEST = 512

norm_eps = 1e-05
unit_eps = 1e-06
f32 = jnp.float32
bf16 = jnp.bfloat16
VMEM_LIMIT = 48 * 1024 * 1024


def cost(micros):
    return pl.CostEstimate(flops=int(micros * 1e9), bytes_accessed=1 << 20, transcendentals=0)


def nn(a, b):
    return lax.dot_general(a, b, (((1,), (0,)), ((), ())), preferred_element_type=f32)


def nt(a, b):
    return lax.dot_general(a, b, (((1,), (1,)), ((), ())), preferred_element_type=f32)


def tn(a, b):
    return lax.dot_general(a, b, (((0,), (0,)), ((), ())), preferred_element_type=f32)


def split(value):
    high = value.astype(bf16)
    return high, (value - high.astype(f32)).astype(bf16)


def nn3(a, b):
    a_high, a_low = a
    b_high, b_low = b
    return nn(a_high, b_high) + nn(a_high, b_low) + nn(a_low, b_high)


def sigmoid(value):
    return 1.0 / (1.0 + jnp.exp(-value))


def rms_scale(values):
    return lax.rsqrt(jnp.mean(values * values, axis=-1, keepdims=True) + norm_eps)


def norm_back(grad_rows, normed, row_scale, gain_vec):
    grad_hat = grad_rows * gain_vec
    return row_scale * (grad_hat - normed * jnp.mean(grad_hat * normed, axis=-1, keepdims=True))


def grid_of(size):
    row = lax.broadcasted_iota(jnp.int32, (size, size), 0)
    return row, lax.broadcasted_iota(jnp.int32, (size, size), 1)


def unit_inverses(lowers, size):
    row, col = grid_of(size)
    apart = row ^ col
    eye = jnp.where(apart == 0, 1.0, 0.0)
    inverses = [eye - jnp.where(apart == 1, lower, 0.0) for lower in lowers]
    lows = [lower.astype(bf16) for lower in lowers]
    level = 1
    while (1 << level) < size:
        here = (apart >> level) == 1
        rounded = [inverse.astype(bf16) for inverse in inverses]
        right = [nn(jnp.where(here, low, 0.0), near).astype(bf16) for low, near in zip(lows, rounded)]
        inverses = [inverse - nn(near, far) for inverse, near, far in zip(inverses, rounded, right)]
        level += 1
    parts = [split(inverse) for inverse in inverses]
    wholes = [split(lower) for lower in lowers]
    left = [
        (eye - inverse - nn3(whole, part)).astype(bf16)
        for inverse, whole, part in zip(inverses, wholes, parts)
    ]
    return [inverse + nn(part[0], rest) for inverse, part, rest in zip(inverses, parts, left)]


def conv_taps(proj, seq, taps, kind, info, count, lanes=slice(None)):
    rows = []
    for tap in range(4):
        moved = proj[seq, HALO - 3 + tap : HALO - 3 + tap + count, lanes]
        rows.append(moved if tap == 3 else moved * info[:, tap : tap + 1])
    mixed = rows[0] * taps[kind, 0:1, lanes]
    for tap in range(1, 4):
        mixed = mixed + rows[tap] * taps[kind, tap : tap + 1, lanes]
    return rows, mixed


def turned(info, seq):
    row, col = grid_of(8)
    return tn(info[seq].astype(bf16), jnp.where(row == col, 1.0, 0.0).astype(bf16))


def head_column(table, seq, head):
    lane = lax.broadcasted_iota(jnp.int32, table.shape[1:], 1)
    return jnp.sum(jnp.where(lane == head, table[seq], 0.0), axis=1, keepdims=True)


def forward_kernel(
    seqs, count, size, group,
    query_in, key_in, value_in, taps, info, beta,
    query_out, key_out, value_out, inverse_out, fresh_out, carry_out, local_out, reach_out, state_out, transit_out, both_out,
):
    row, col = grid_of(count)
    scale = 1.0 / math.sqrt(size)
    infos = [turned(info, seq) for seq in range(seqs)]
    sames = [infos[seq][:, 5:6] == info[seq, 5:6, :] for seq in range(seqs)]
    every = [(seq, part, slice(part * size, (part + 1) * size)) for part in range(group) for seq in range(seqs)]
    queries, keys, lowers, betas = [], [], [], []
    for seq, part, lanes in every:
        parts = []
        for kind, proj in enumerate((query_in, key_in, value_in)):
            mixed = conv_taps(proj, seq, taps, kind, infos[seq], count, lanes)[1]
            parts.append(mixed * sigmoid(mixed))
        query, key, value = parts
        query = query * (lax.rsqrt(jnp.sum(query * query, axis=1, keepdims=True) + unit_eps) * scale)
        key = key * lax.rsqrt(jnp.sum(key * key, axis=1, keepdims=True) + unit_eps)
        query, key, value = query.astype(bf16), key.astype(bf16), value.astype(bf16)
        query_out[seq, :, lanes], key_out[seq, :, lanes], value_out[seq, :, lanes] = query, key, value
        beta_col = head_column(beta, seq, pl.program_id(0) * group + part)
        queries.append(query)
        keys.append(key)
        betas.append(beta_col)
        lowers.append(jnp.where(sames[seq] & (row > col), nt(key, key) * beta_col, 0.0))
    inverses = unit_inverses(lowers, count)
    for (seq, part, lanes), query, key, beta_col, inverse in zip(every, queries, keys, betas, inverses):
        enter, last = infos[seq][:, 3:4], infos[seq][:, 4:5]
        key_full = key.astype(f32)
        inverse_parts = split(inverse)
        inverse_out[part, seq] = inverse_parts[0]
        right = jnp.concatenate(
            [key_full * (beta_col * enter), value_out[seq, :, lanes].astype(f32) * beta_col], axis=1
        )
        solved = nn3(inverse_parts, split(right))
        solved_high, solved_low = split(solved)
        key_last = (key_full * last).astype(bf16)
        ends = tn(key_last, solved_high) + tn(key_last, solved_low)
        transit_row, transit_col = grid_of(size)
        eye = jnp.where(transit_row == transit_col, 1.0, 0.0)
        transit = eye * info[seq, 3:4, count - 1 :] - ends[:, :size]
        state_out[seq, part] = ends[:, size:]
        transit_out[seq, part] = transit
        both_out[seq, part, 0] = ends[:, size:]
        both_out[seq, part, 1] = transit
        attend = jnp.where(sames[seq] & (row >= col), nt(query, key), 0.0).astype(bf16)
        reads = nn(attend, solved_high)
        local_out[seq, :, lanes] = reads[:, size:]
        reach_out[seq, :, lanes] = (query.astype(f32) * enter - reads[:, :size]).astype(bf16)
        carry_out[seq, :, lanes] = solved_high[:, :size]
        fresh_out[seq, :, lanes] = solved[:, size:]


def pl_forward(proj, taps, info, beta, group, heads, seqs, count, size, channels):
    def rows(dtype):
        return jax.ShapeDtypeStruct((seqs, count, heads * size), dtype)

    row_spec = pl.BlockSpec((seqs, count, group * size), lambda h: (0, 0, h))
    proj_spec = pl.BlockSpec((seqs, count + HALO, group * size), lambda h: (0, 0, h))
    state = jax.ShapeDtypeStruct((seqs, heads, size, size), f32)
    state_spec = pl.BlockSpec((seqs, group, size, size), lambda h: (0, h, 0, 0))
    return pl.pallas_call(
        functools.partial(forward_kernel, seqs, count, size, group),
        grid=(heads // group,),
        in_specs=[proj_spec] * 3
        + [
            pl.BlockSpec((3, 4, group * size), lambda h: (0, 0, h)),
            pl.BlockSpec(info.shape, lambda h: (0, 0, 0)),
            pl.BlockSpec(beta.shape, lambda h: (0, 0, 0)),
        ],
        out_specs=[row_spec] * 3
        + [pl.BlockSpec((group, seqs, count, count), lambda h: (h, 0, 0, 0))]
        + [row_spec] * 4
        + [state_spec] * 2
        + [pl.BlockSpec((seqs, group, 2, size, size), lambda h: (0, h, 0, 0, 0))],
        out_shape=[rows(bf16)] * 3
        + [jax.ShapeDtypeStruct((heads, seqs, count, count), bf16)]
        + [rows(f32), rows(bf16), rows(f32), rows(bf16)]
        + [state] * 2
        + [jax.ShapeDtypeStruct((seqs, heads, 2, size, size), f32)],
        compiler_params=pltpu.CompilerParams(vmem_limit_bytes=VMEM_LIMIT),
        cost_estimate=cost(17),
    )(*proj, taps, info, beta)


def arrived(boths, farthest, seq):
    total = farthest[seq, 0]
    for both in boths[::-1]:
        total = both[seq, 0, 0] + nn3(split(both[seq, 0, 1]), split(total))
    return total


def read_kernel(seqs, count, size, heads, hops, *refs):
    boths, farthest = refs[: hops - 1], refs[hops - 1]
    local, reach, gate, gain, out_weight, state_out, mix_out, gated_out, part_out, held = refs[hops:]
    head = pl.program_id(0)
    for seq in range(seqs):
        state = arrived(boths, farthest, seq)
        state_out[seq, 0] = state
        state_high, state_low = split(state)
        moved = reach[seq]
        mix = local[seq] + nn(moved, state_high) + nn(moved, state_low)
        mix_out[seq] = mix
        gate_now = gate[seq]
        gated = (mix * rms_scale(mix) * gain[...] * (gate_now * sigmoid(gate_now))).astype(bf16)
        gated_out[seq] = gated
        held[head, seq * count : (seq + 1) * count, :] = gated

    @pl.when(head == heads - 1)
    def _():
        rows = jnp.concatenate([held[h] for h in range(heads)], axis=1)
        part_out[...] = nn(rows, out_weight[...])


def pl_read(boths, farthest, local, reach, gate, gain, out_weight, heads, seqs, count, size, width):
    row_spec = pl.BlockSpec((seqs, count, size), lambda h: (0, 0, h))
    state_spec = pl.BlockSpec((seqs, 1, size, size), lambda h: (0, h, 0, 0))
    both_spec = pl.BlockSpec((seqs, 1, 2, size, size), lambda h: (0, h, 0, 0, 0))
    hops = len(boths) + 1
    return pl.pallas_call(
        functools.partial(read_kernel, seqs, count, size, heads, hops),
        grid=(heads,),
        in_specs=[both_spec] * (hops - 1)
        + [state_spec]
        + [row_spec] * 3
        + [pl.BlockSpec((1, size), lambda h: (0, 0)), pl.BlockSpec((heads * size, width), lambda h: (0, 0))],
        out_specs=[state_spec, row_spec, row_spec, pl.BlockSpec((seqs * count, width), lambda h: (0, 0))],
        out_shape=[
            jax.ShapeDtypeStruct((seqs, heads, size, size), f32),
            jax.ShapeDtypeStruct((seqs, count, heads * size), f32),
            jax.ShapeDtypeStruct((seqs, count, heads * size), bf16),
            jax.ShapeDtypeStruct((seqs * count, width), f32),
        ],
        scratch_shapes=[pltpu.VMEM((heads, seqs * count, size), bf16)],
        compiler_params=pltpu.CompilerParams(vmem_limit_bytes=VMEM_LIMIT),
        cost_estimate=cost(7),
    )(*boths, farthest, local, reach, gate, gain, out_weight)


def hidden_back_kernel(gate_grad, up_grad, feed_gate, feed_up, out):
    out[...] = nt(gate_grad[...], feed_gate[...]) + nt(up_grad[...], feed_up[...])


def pl_hidden_back(gate_grad, up_grad, feed_gate, feed_up):
    rows, hidden = gate_grad.shape
    width = feed_gate.shape[0]
    step = width // 4
    whole = pl.BlockSpec((rows, hidden), lambda i: (0, 0))
    weight = pl.BlockSpec((step, hidden), lambda i: (i, 0))
    return pl.pallas_call(
        hidden_back_kernel,
        grid=(4,),
        in_specs=[whole, whole, weight, weight],
        out_specs=pl.BlockSpec((rows, step), lambda i: (0, i)),
        out_shape=jax.ShapeDtypeStruct((rows, width), f32),
        compiler_params=pltpu.CompilerParams(vmem_limit_bytes=VMEM_LIMIT),
        cost_estimate=cost(6),
    )(gate_grad, up_grad, feed_gate, feed_up)


def gate_back_kernel(
    seqs, count, size,
    mid_part, mid_other, full_grad, middle, feed_gain, out_weight, mix, gate, gain, reach,
    middle_grad, mixer_grad, feed_gain_grad, mix_grad, gate_grad, gain_grad, pull,
):
    head = pl.program_id(0)

    @pl.when(head == 0)
    def _():
        gain_grad[...] = jnp.zeros_like(gain_grad)
        for seq in range(seqs):
            here = slice(seq * count, (seq + 1) * count)
            mid_grad = mid_part[here] + mid_other[here]
            scale = rms_scale(middle[here])
            normed = middle[here] * scale
            share = (mid_grad * normed).reshape(count // 8, 8, normed.shape[1])
            share = jnp.sum(share, axis=0)
            if seq == 0:
                feed_gain_grad[...] = share
            else:
                feed_gain_grad[...] += share
            whole = full_grad[here] + norm_back(mid_grad, normed, scale, feed_gain[...])
            middle_grad[here] = whole
            mixer_grad[here] = whole.astype(bf16)

    grads = nt(mixer_grad[...], out_weight[...])
    for seq in range(seqs):
        grad = grads[seq * count : (seq + 1) * count]
        mix_now, gate_now = mix[seq], gate[seq]
        scale = rms_scale(mix_now)
        normed = mix_now * scale
        sig = sigmoid(gate_now)
        gate_silu = gate_now * sig
        with_norm = grad * normed
        gain_grad[...] += jnp.sum((with_norm * gate_silu).reshape(count // 8, 8, size), axis=0)
        gate_grad[seq] = (with_norm * gain[...] * (sig * (1.0 + gate_now * (1.0 - sig)))).astype(bf16)
        normed_grad = grad * gain[...] * gate_silu
        mix_grad_now = scale * (normed_grad - normed * jnp.mean(normed_grad * normed, axis=1, keepdims=True))
        low = mix_grad_now.astype(bf16)
        mix_grad[seq] = low
        pull[seq, 0] = tn(reach[seq], low)


def pl_gate_back(
    mid_part, mid_other, full_grad, middle, feed_gain, out_weight, mix, gate, gain, reach, heads, seqs, count, size
):
    rows, width = middle.shape
    row_spec = pl.BlockSpec((seqs, count, size), lambda h: (0, 0, h))

    def fixed(*dims):
        return pl.BlockSpec(dims, lambda h: (0,) * len(dims))

    return pl.pallas_call(
        functools.partial(gate_back_kernel, seqs, count, size),
        grid=(heads,),
        in_specs=[fixed(rows, width)] * 4
        + [
            fixed(1, width),
            pl.BlockSpec((size, width), lambda h: (h, 0)),
            row_spec,
            row_spec,
            fixed(1, size),
            row_spec,
        ],
        out_specs=[
            fixed(rows, width),
            fixed(rows, width),
            fixed(8, width),
            row_spec,
            row_spec,
            fixed(8, size),
            pl.BlockSpec((seqs, 1, size, size), lambda h: (0, h, 0, 0)),
        ],
        out_shape=[
            jax.ShapeDtypeStruct((rows, width), f32),
            jax.ShapeDtypeStruct((rows, width), bf16),
            jax.ShapeDtypeStruct((8, width), f32),
            jax.ShapeDtypeStruct((seqs, count, heads * size), bf16),
            jax.ShapeDtypeStruct((seqs, count, heads * size), bf16),
            jax.ShapeDtypeStruct((8, size), f32),
            jax.ShapeDtypeStruct((seqs, heads, size, size), f32),
        ],
        compiler_params=pltpu.CompilerParams(vmem_limit_bytes=VMEM_LIMIT),
        cost_estimate=cost(9),
    )(mid_part, mid_other, full_grad, middle, feed_gain, out_weight, mix, gate, gain, reach)


def backward_kernel(seqs, count, size, hops, *refs):
    pulls, transits = refs[:hops], refs[hops : 2 * hops - 1]
    (
        query_in, key_in, value_in, taps, info_rows, beta,
        query_ref, key_ref, value_ref, inverse_ref, fresh_ref, carry_ref, mix_grad_ref, state_ref,
        query_grad_out, key_grad_out, value_grad_out, edge_out, taps_grad_out, logit_grad_out,
    ) = refs[2 * hops - 1 :]
    head = pl.program_id(0)
    row, col = grid_of(count)
    scale = 1.0 / math.sqrt(size)

    @pl.when(head == 0)
    def _():
        logit_grad_out[...] = jnp.zeros_like(logit_grad_out)

    taps_totals = None
    for seq in range(seqs):
        total = pulls[-1][seq, 0]
        for pull, transit in zip(pulls[-2::-1], transits[::-1]):
            transit_high, transit_low = split(transit[seq, 0])
            total_high, total_low = split(total)
            total = pull[seq, 0] + (
                tn(transit_high, total_high) + tn(transit_high, total_low) + tn(transit_low, total_high)
            )
        out_state_grad = total.astype(bf16)
        state = state_ref[seq, 0].astype(bf16)
        query, key, value = query_ref[seq], key_ref[seq], value_ref[seq]
        mix_grad = mix_grad_ref[seq]
        info = turned(info_rows, seq)
        enter, last = info[:, 3:4], info[:, 4:5]
        same = info[:, 5:6] == info_rows[seq, 5:6, :]
        causal = same & (row >= col)
        strict = same & (row > col)
        beta_col = head_column(beta, seq, head)
        key_full = key.astype(f32)
        key_last = (key_full * last).astype(bf16)
        update = (fresh_ref[seq] - nn(carry_ref[seq], state)).astype(bf16)
        attend = jnp.where(causal, nt(query, key), 0.0).astype(bf16)
        update_grad = tn(attend, mix_grad) + nn(key_last, out_state_grad)
        right_grad = tn(inverse_ref[0, seq], update_grad.astype(bf16))
        right_low = right_grad.astype(bf16)
        both = nt(jnp.concatenate([mix_grad, right_low], axis=0), update)
        attend_grad = jnp.where(causal, both[:count], 0.0).astype(bf16)
        lower_grad = jnp.where(strict, -both[count:], 0.0)
        gram = nt(key, key)
        surprise = value.astype(f32) - enter * nn(key, state)
        beta_grad = jnp.sum(right_grad * surprise, axis=1, keepdims=True) + jnp.sum(
            lower_grad * gram, axis=1, keepdims=True
        )
        logit_grad = beta_grad * beta_col * (1.0 - beta_col)
        lane = lax.broadcasted_iota(jnp.int32, logit_grad_out.shape[1:], 1)
        logit_grad_out[seq] += jnp.where(lane == head, logit_grad, 0.0)
        value_grad = right_grad * beta_col
        gram_grad = (lower_grad * beta_col).astype(bf16)
        stacked = jnp.concatenate([gram_grad, attend_grad], axis=0)
        forth = nn(stacked, key)
        back = tn(stacked, jnp.concatenate([key, query], axis=0))
        through = nt(
            jnp.concatenate([(value_grad * enter).astype(bf16), mix_grad], axis=0), state
        )
        key_grad = forth[:count] + back - through[:count] + last * nt(update, out_state_grad)
        query_grad = forth[count:] + enter * through[count:]
        for kind, (proj, grad, out) in enumerate(
            (
                (query_in, query_grad, query_grad_out),
                (key_in, key_grad, key_grad_out),
                (value_in, value_grad, value_grad_out),
            )
        ):
            rows, mixed = conv_taps(proj, seq, taps, kind, info, count)
            sig = sigmoid(mixed)
            if kind < 2:
                active = mixed * sig
                norm = lax.rsqrt(jnp.sum(active * active, axis=1, keepdims=True) + unit_eps)
                unit = active * norm
                grad = grad - unit * jnp.sum(grad * unit, axis=1, keepdims=True)
                grad = grad * (norm * scale if kind == 0 else norm)
            mixed_grad = grad * (sig * (1.0 + mixed * (1.0 - sig)))
            sums = [jnp.sum((mixed_grad * rows[tap]).reshape(count // 8, 8, size), axis=0) for tap in range(4)]
            blank = jnp.zeros((8, size), f32)
            proj_grad = mixed_grad * taps[kind, 3:4, :]
            edge = blank
            for tap in range(3):
                delay = 3 - tap
                masked = mixed_grad * (info[:, tap : tap + 1] * taps[kind, tap : tap + 1, :])
                moved = pltpu.roll(masked, count - delay, 0)
                at = lax.broadcasted_iota(jnp.int32, (count, size), 0)
                proj_grad = proj_grad + jnp.where(at < count - delay, moved, 0.0)
                first = pltpu.roll(masked[:8], 8 - delay, 0)
                at_edge = lax.broadcasted_iota(jnp.int32, (8, size), 0)
                edge = edge + jnp.where(at_edge >= 8 - delay, first, 0.0)
            out[seq] = proj_grad
            edge_out[kind, seq] = edge
            sums = jnp.stack([jnp.sum(part, axis=0) for part in sums])
            if seq == 0:
                taps_grad_out[kind] = sums
            else:
                taps_grad_out[kind] += sums


def pl_backward(pulls, transits, proj, taps, info, beta, saved, mix_grad, state, heads, seqs, count, size):
    hops = len(pulls)
    row_spec = pl.BlockSpec((seqs, count, size), lambda h: (0, 0, h))
    state_spec = pl.BlockSpec((seqs, 1, size, size), lambda h: (0, h, 0, 0))
    proj_spec = pl.BlockSpec((seqs, count + HALO, size), lambda h: (0, 0, h))
    return pl.pallas_call(
        functools.partial(backward_kernel, seqs, count, size, hops),
        grid=(heads,),
        in_specs=[state_spec] * (2 * hops - 1)
        + [proj_spec] * 3
        + [
            pl.BlockSpec((3, 4, size), lambda h: (0, 0, h)),
            pl.BlockSpec(info.shape, lambda h: (0, 0, 0)),
            pl.BlockSpec(beta.shape, lambda h: (0, 0, 0)),
        ]
        + [row_spec] * 3
        + [pl.BlockSpec((1, seqs, count, count), lambda h: (h, 0, 0, 0))]
        + [row_spec] * 3
        + [state_spec],
        out_specs=[row_spec] * 3
        + [
            pl.BlockSpec((3, seqs, 8, size), lambda h: (0, 0, 0, h)),
            pl.BlockSpec((3, 4, size), lambda h: (0, 0, h)),
            pl.BlockSpec((seqs, count, heads), lambda h: (0, 0, 0)),
        ],
        out_shape=[jax.ShapeDtypeStruct((seqs, count, heads * size), f32)] * 3
        + [
            jax.ShapeDtypeStruct((3, seqs, 8, heads * size), f32),
            jax.ShapeDtypeStruct((3, 4, heads * size), f32),
            jax.ShapeDtypeStruct((seqs, count, heads), f32),
        ],
        compiler_params=pltpu.CompilerParams(vmem_limit_bytes=VMEM_LIMIT),
        cost_estimate=cost(17),
    )(*pulls, *transits, *proj, taps, info, beta, *saved, mix_grad, state)


def input_back_kernel(first, second, gate_grad, beta_grad, query_w, key_w, value_w, gate_w, beta_w, out):
    channels = query_w.shape[1]
    third = channels // 2
    out[...] = (
        nt(first[:, :channels], query_w[...])
        + nt(second[:, :channels], key_w[...])
        + nt(first[:, channels:], value_w[:, :third])
        + nt(second[:, channels:], value_w[:, third:])
        + nt(gate_grad[...], gate_w[...])
        + nt(beta_grad[...], beta_w[...])
    )


def pl_input_back(grads, weights):
    rows = grads[0].shape[0]
    width = weights[0].shape[0]
    step = width // 4
    return pl.pallas_call(
        input_back_kernel,
        grid=(4,),
        in_specs=[pl.BlockSpec(grad.shape, lambda i: (0, 0)) for grad in grads]
        + [pl.BlockSpec((step, weight.shape[1]), lambda i: (i, 0)) for weight in weights],
        out_specs=pl.BlockSpec((rows, step), lambda i: (0, i)),
        out_shape=jax.ShapeDtypeStruct((rows, width), f32),
        compiler_params=pltpu.CompilerParams(vmem_limit_bytes=VMEM_LIMIT),
        cost_estimate=cost(1),
    )(*grads, *weights)


def input_norm_kernel(which, part, other, value, middle_grad, gain, out, gain_grad):
    grad = part[...] + other[...]
    scale = rms_scale(value[...])
    normed = value[...] * scale
    share = jnp.sum((grad * normed).reshape(grad.shape[0] // 8, 8, grad.shape[1]), axis=0)

    @pl.when(pl.program_id(0) == 0)
    def _():
        gain_grad[...] = share

    @pl.when(pl.program_id(0) > 0)
    def _():
        gain_grad[...] += share

    result = middle_grad[...] + norm_back(grad, normed, scale, gain[...])
    half = out.shape[1]
    out[...] = jnp.where(which[0] == 0, result[:, :half], result[:, half:])


def pl_input_norm(which, part, other, value, middle_grad, gain, steps):
    rows, width = value.shape
    tall = pl.BlockSpec((rows // steps, width), lambda i, which: (i, 0))
    return pl.pallas_call(
        input_norm_kernel,
        grid_spec=pltpu.PrefetchScalarGridSpec(
            num_scalar_prefetch=1,
            grid=(steps,),
            in_specs=[tall] * 4 + [pl.BlockSpec((1, width), lambda i, which: (0, 0))],
            out_specs=[
                pl.BlockSpec((rows // steps, width // 2), lambda i, which: (i, 0)),
                pl.BlockSpec((8, width), lambda i, which: (0, 0)),
            ],
        ),
        out_shape=[jax.ShapeDtypeStruct((rows, width // 2), f32), jax.ShapeDtypeStruct((8, width), f32)],
        compiler_params=pltpu.CompilerParams(vmem_limit_bytes=VMEM_LIMIT),
        cost_estimate=cost(1),
    )(which, part, other, value, middle_grad, gain)


def shifted(value, axis, steps):
    count = lax.axis_size(axis)
    initial, last = (max(0, -steps), min(count, count - steps))
    return lax.ppermute(value, axis, [(source, source + steps) for source in range(initial, last)])


def from_ahead(value, hops):
    if not relayed(hops):
        return [shifted(value, "seq", -hop) for hop in range(1, hops + 1)]
    return [lax.ppermute(value, "seq", pairs) for pairs in ([(1, 0), (3, 2)], [(2, 0), (3, 1)])]


def relayed(hops):
    return by_bits() and hops == 2


def swapped(value):
    return lax.ppermute(value, "head", [(0, 1), (1, 0)])


def in_order(own, other, axis):
    mine = lax.axis_index("head") == 0
    return jnp.where(
        mine, jnp.concatenate([own, other], axis=axis), jnp.concatenate([other, own], axis=axis)
    )


def own_half(value, half):
    return lax.dynamic_slice_in_dim(value, lax.axis_index("head") * half, half, value.ndim - 1)


def pick(value, index, axis):
    return lax.dynamic_index_in_dim(value, index, axis, keepdims=False)


def together(*values):
    return lax.optimization_barrier(values)


def weight_kernel(block, first_window, second_window, bits, first_left, first_right, second_left, second_right, *refs):
    first_leaves, first_stays, second_leaves, second_stays, held, held_second = refs
    low, high = bits[0], bits[1]
    held[...] = tn(first_left[...], first_right[:, first_window])
    for part in range(2):
        base = part * 2 * block
        first_leaves[0, part] = held[pl.ds(pl.multiple_of(base + (1 - low) * block, 8), block), :]
        first_stays[0, part] = held[pl.ds(pl.multiple_of(base + low * block, 8), block), :]
    held_second[...] = tn(second_left[...], second_right[:, second_window])
    second_leaves[0] = held_second[pl.ds(pl.multiple_of((1 - high) * 2 * block, 8), 2 * block), :]
    second_stays[0] = held_second[pl.ds(pl.multiple_of(high * 2 * block, 8), 2 * block), :]


def fold_kernel(block, bits, first_stays, first_comes, second_stays, second_comes, *refs):
    first_leaves, first_keeps, second_leaves, second_keeps = refs
    low, high = bits[0], bits[1]
    first_leaves[0] = first_stays[0, 1 - high] + first_comes[0, 1 - high]
    first_keeps[0] = first_stays[0, high] + first_comes[0, high]
    away = pl.ds(pl.multiple_of((1 - low) * block, 8), block)
    here = pl.ds(pl.multiple_of(low * block, 8), block)
    second_leaves[0] = second_stays[0, away] + second_comes[0, away]
    second_keeps[0] = second_stays[0, here] + second_comes[0, here]


def join_kernel(pieces, bits, first_keeps, first_comes, second_keeps, second_comes, out):
    first, second = first_keeps.shape[-1] // pieces, second_keeps.shape[-1] // pieces
    at = 0
    for piece in range(pieces):
        lanes = slice(piece * first, (piece + 1) * first)
        out[:, at : at + first] = first_keeps[0, :, lanes] + first_comes[0, :, lanes]
        at += first
        lanes = slice(piece * second, (piece + 1) * second)
        out[:, at : at + second] = second_keeps[0, :, lanes] + second_comes[0, :, lanes]
        at += second


def per_block(kernel, bits, steps, args, in_specs, out_specs, out_shape, scratch=()):
    return pl.pallas_call(
        kernel,
        grid_spec=pltpu.PrefetchScalarGridSpec(
            num_scalar_prefetch=1, grid=(steps,), in_specs=in_specs, out_specs=out_specs, scratch_shapes=list(scratch)
        ),
        out_shape=out_shape,
        compiler_params=pltpu.CompilerParams(vmem_limit_bytes=VMEM_LIMIT),
        cost_estimate=cost(1),
    )(bits, *args)


def four_block(dims):
    return pl.BlockSpec((1,) + dims, lambda z, bits: (z,) + (0,) * len(dims))


def swap_bit(value, bit):
    return lax.ppermute(value, "seq", [(source, source ^ (1 << bit)) for source in range(4)])


def by_bits():
    return lax.axis_size("seq") == 4


def weight_grads(bits, first_left, first_right, second_left, second_right, first_window=None, second_window=None):
    first_window = first_window or slice(0, first_right.shape[1])
    second_window = second_window or slice(0, second_right.shape[1])
    if not by_bits():
        return tn(first_left, first_right[:, first_window]), tn(second_left, second_right[:, second_window])
    dp = lax.axis_size("dp")
    tokens, rows = first_left.shape
    first_cols = first_window.stop - first_window.start
    second_cols = second_window.stop - second_window.start
    block = rows // (4 * dp)
    left_spec = pl.BlockSpec((tokens, 4 * block), lambda z, bits: (0, z))

    def whole(cols):
        return pl.BlockSpec((tokens, cols), lambda z, bits: (0, 0))

    first, second = (2, block, first_cols), (2 * block, second_cols)
    return per_block(
        functools.partial(weight_kernel, block, first_window, second_window),
        bits,
        dp,
        (first_left, first_right, second_left, second_right),
        [left_spec, whole(first_right.shape[1]), left_spec, whole(second_right.shape[1])],
        [four_block(dims) for dims in (first, first, second, second)],
        [jax.ShapeDtypeStruct((dp,) + dims, f32) for dims in (first, first, second, second)],
        [pltpu.VMEM((4 * block, first_cols), f32), pltpu.VMEM((4 * block, second_cols), f32)],
    )


def paired_kernel(first_left, first_right, second_left, second_right, out):
    cut = first_right.shape[1]
    out[:, :cut] = tn(first_left[...], first_right[...])
    out[:, cut:] = tn(second_left[...], second_right[...])


def paired_grads(first_left, first_right, second_left, second_right):
    tokens, rows = first_left.shape
    cols = first_right.shape[1] + second_right.shape[1]
    step = rows // 4
    left_spec = pl.BlockSpec((tokens, step), lambda i: (0, i))
    whole = [pl.BlockSpec(right.shape, lambda i: (0, 0)) for right in (first_right, second_right)]
    return pl.pallas_call(
        paired_kernel,
        grid=(4,),
        in_specs=[left_spec, whole[0], left_spec, whole[1]],
        out_specs=pl.BlockSpec((step, cols), lambda i: (i, 0)),
        out_shape=jax.ShapeDtypeStruct((rows, cols), f32),
        compiler_params=pltpu.CompilerParams(vmem_limit_bytes=VMEM_LIMIT),
        cost_estimate=cost(4),
    )(first_left, first_right, second_left, second_right)


def first_swap(parts):
    if not by_bits():
        return parts
    first_leaves, first_stays, second_leaves, second_stays = parts
    return first_stays, swap_bit(first_leaves, 0), second_stays, swap_bit(second_leaves, 1)


def fold(bits, parts):
    if not by_bits():
        return parts
    dp = lax.axis_size("dp")
    block, first_cols, second_cols = parts[0].shape[2], parts[0].shape[3], parts[2].shape[2]
    ins = [(2, block, first_cols)] * 2 + [(2 * block, second_cols)] * 2
    outs = [(block, first_cols)] * 2 + [(block, second_cols)] * 2
    return per_block(
        functools.partial(fold_kernel, block),
        bits,
        dp,
        parts,
        [four_block(dims) for dims in ins],
        [four_block(dims) for dims in outs],
        [jax.ShapeDtypeStruct((dp,) + dims, f32) for dims in outs],
    )


def fold_two_kernel(block, bits, *refs):
    low, high = bits[0], bits[1]
    first_leaves, first_keeps, second_leaves, second_keeps = refs[8:]
    away = pl.ds(pl.multiple_of((1 - low) * block, 8), block)
    here = pl.ds(pl.multiple_of(low * block, 8), block)
    first_at = second_at = 0
    for first_stays, first_comes, second_stays, second_comes in (refs[:4], refs[4:8]):
        lanes = slice(first_at, first_at + first_stays.shape[-1])
        first_leaves[0, :, lanes] = first_stays[0, 1 - high] + first_comes[0, 1 - high]
        first_keeps[0, :, lanes] = first_stays[0, high] + first_comes[0, high]
        first_at = lanes.stop
        lanes = slice(second_at, second_at + second_stays.shape[-1])
        second_leaves[0, :, lanes] = second_stays[0, away] + second_comes[0, away]
        second_keeps[0, :, lanes] = second_stays[0, here] + second_comes[0, here]
        second_at = lanes.stop


def fold_two(bits, one, two):
    if not by_bits():
        return one + two
    dp = lax.axis_size("dp")
    block = one[0].shape[2]
    ins, outs = [], [0, 0]
    for part in (one, two):
        first_cols, second_cols = part[0].shape[3], part[2].shape[2]
        ins += [(2, block, first_cols)] * 2 + [(2 * block, second_cols)] * 2
        outs = [outs[0] + first_cols, outs[1] + second_cols]
    outs = [(block, outs[0])] * 2 + [(block, outs[1])] * 2
    return per_block(
        functools.partial(fold_two_kernel, block),
        bits,
        dp,
        tuple(one) + tuple(two),
        [four_block(dims) for dims in ins],
        [four_block(dims) for dims in outs],
        [jax.ShapeDtypeStruct((dp,) + dims, f32) for dims in outs],
    )


def second_swap(parts):
    if not by_bits():
        return parts
    first_leaves, first_keeps, second_leaves, second_keeps = parts
    return first_keeps, swap_bit(first_leaves, 1), second_keeps, swap_bit(second_leaves, 0)


def join(bits, parts, pieces=1):
    if not by_bits():
        return tuple(
            lax.psum_scatter(part, ("dp", "seq"), scatter_dimension=0, tiled=True) for part in parts
        )
    dp = lax.axis_size("dp")
    block, first_cols, second_cols = parts[0].shape[1], parts[0].shape[2], parts[2].shape[2]
    return per_block(
        functools.partial(join_kernel, pieces),
        bits,
        dp,
        parts,
        [four_block((block, cols)) for cols in (first_cols, first_cols, second_cols, second_cols)],
        pl.BlockSpec((block, first_cols + second_cols), lambda z, bits: (z, 0)),
        jax.ShapeDtypeStruct((dp * block, first_cols + second_cols), f32),
    )


def last_sum(joined):
    if not by_bits():
        return jnp.concatenate(joined, axis=1)
    return lax.psum_scatter(joined, "dp", scatter_dimension=0, tiled=True)


def swap_add(value, bit):
    if not by_bits():
        return value
    value = value.reshape(2 - bit, 2, -1, value.shape[-1])
    mine = (lax.axis_index("seq") >> bit) & 1
    return pick(value, mine, 1) + swap_bit(pick(value, 1 - mine, 1), bit)


def small_sum(value, names):
    if not by_bits():
        return lax.psum_scatter(value, names, scatter_dimension=0, tiled=True)
    if names == "dp" and lax.axis_size("dp") != 4:
        return lax.psum_scatter(value, "dp", scatter_dimension=0, tiled=True)
    value = value.reshape((2, 2) + (value.shape[0] // 4,) + value.shape[1:])
    for bit in range(2):
        mine = (lax.axis_index(names) >> bit) & 1
        perm = [(source, source ^ (1 << bit)) for source in range(4)]
        value = pick(value, mine, 1 - bit) + lax.ppermute(pick(value, 1 - mine, 1 - bit), names, perm)
    return value


def local(
    block_input,
    segment_ids,
    mixer_gain,
    query_weight,
    key_weight,
    value_weight,
    gate_weight,
    beta_weight,
    conv_weight,
    head_gain,
    out_weight,
    feed_gain,
    feed_gate,
    feed_up,
    feed_down,
    grad_output,
):
    seqs, count, half = block_input.shape
    rows = seqs * count
    size = head_gain.shape[0]
    heads = beta_weight.shape[1]
    channels = heads * size
    width = query_weight.shape[0]
    hops = -(-(LONGEST - 1) // count)
    hops = min(hops, lax.axis_size("seq") - 1)

    other_input = swapped(block_input)
    segments = segment_ids.astype(f32)
    before = shifted(
        jnp.concatenate([block_input[:, count - 3 :], segments[:, count - 3 :, None]], axis=2), "seq", 1
    )
    edge_ids = before[:, :, half]
    before = before[:, :, :half]
    other_before = swapped(before)
    full_input = in_order(block_input, other_input, 2)
    full_before = in_order(before, other_before, 2)
    other_grad = swapped(grad_output)

    extended = jnp.concatenate(
        [jnp.zeros((seqs, HALO - 3, width), f32), full_before, full_input], axis=1
    )
    extended_low = (extended * rms_scale(extended) * mixer_gain).astype(bf16)
    flat = extended_low.reshape(seqs * (count + HALO), width)
    proj = [
        nn(flat, weight).reshape(seqs, count + HALO, channels)
        for weight in (query_weight, key_weight, value_weight)
    ]
    normed_in = extended_low[:, HALO:].reshape(rows, width)
    beta = jax.nn.sigmoid(nn(normed_in, beta_weight)).reshape(seqs, count, heads)
    gate_proj = nn(normed_in, gate_weight).reshape(seqs, count, channels)

    extended_ids = jnp.concatenate([edge_ids, segments], axis=1)
    masks = [(extended_ids[:, tap : tap + count] == segments) for tap in range(3)]
    enter = segments == edge_ids[:, 2:3]
    last = segments == segments[:, count - 1 :]
    zero = jnp.zeros_like(segments)
    info = jnp.stack(
        [mask.astype(f32) for mask in masks] + [enter.astype(f32), last.astype(f32), segments, zero, zero], axis=1
    )
    taps = conv_weight.reshape(3, 4, channels)
    gain = head_gain[None, :]

    (query, key, value, inverse, fresh, carry, local_mix, reach, state_end, transit, both) = pl_forward(
        proj, taps, info, beta, 2 if heads % 2 == 0 else 1, heads, seqs, count, size, channels
    )
    boths = [shifted(both, "seq", hop) for hop in range(1, hops)]
    farthest = shifted(state_end, "seq", hops)
    back_transits = [shifted(transit, "seq", -hop) for hop in range(1, hops)]
    boths, farthest, back_transits = lax.optimization_barrier((boths, farthest, back_transits))
    state, mix, gated, part = pl_read(
        boths, farthest, local_mix, reach, gate_proj, gain, out_weight, heads, seqs, count, size, width
    )
    gated = gated.reshape(rows, channels)
    flat_input = full_input.reshape(rows, width)
    middle = flat_input + (part + swapped(part))
    middle_scale = rms_scale(middle)
    middle_normed = middle * middle_scale
    normed_mid = (middle_normed * feed_gain).astype(bf16)
    gate_act = nn(normed_mid, feed_gate)
    up_act = nn(normed_mid, feed_up)
    gate_sig = jax.nn.sigmoid(gate_act)
    gate_silu = gate_act * gate_sig
    inner = (gate_silu * up_act).astype(bf16)
    full_grad = in_order(grad_output, other_grad, 2).reshape(rows, width)
    down_grad = full_grad.astype(bf16)
    cut = feed_down.shape[0] // 256 * 128
    inner_grad = nt(down_grad, feed_down)
    gate_grad = (inner_grad * up_act * (gate_sig * (1.0 + gate_act * (1.0 - gate_sig)))).astype(bf16)
    up_grad = (inner_grad * gate_silu).astype(bf16)
    place = lax.axis_index("seq")
    bits = jnp.stack([place & 1, (place >> 1) & 1]).astype(jnp.int32)
    mid_part = pl_hidden_back(gate_grad, up_grad, feed_gate, feed_up)
    mid_part, late_inner = together(mid_part, inner)
    mid_other = swapped(mid_part)
    down_sums = weight_grads(
        bits, down_grad, late_inner, down_grad, late_inner, slice(0, cut), slice(cut, inner.shape[1])
    )
    down_sums, mid_part = together(down_sums, mid_part)
    down_sums = first_swap(down_sums)
    mine = lax.axis_index("head")
    down_part = nn(inner, feed_down)
    down_out = lax.dynamic_slice_in_dim(down_part, (1 - mine) * half, half, 1)
    middle_grad, mixer_grad, feed_gain_grad, mix_grad, gate_low, gain_grad, pull = pl_gate_back(
        mid_part, mid_other, full_grad, middle, feed_gain[None, :], out_weight, mix, gate_proj, gain, reach,
        heads, seqs, count, size,
    )
    grad_feed_gain = jnp.sum(feed_gain_grad, axis=0)
    gate_low = gate_low.reshape(rows, channels)
    pull, late_gate, late_up, late_gated, late_low = together(pull, gate_grad, up_grad, gated, gate_low)
    pulls = from_ahead(pull, hops)
    halves = slice(0, cut), slice(cut, inner.shape[1])
    gate_sums = weight_grads(bits, normed_mid, late_gate, normed_mid, late_gate, *halves)
    out_joined = paired_grads(mixer_grad, late_gated, normed_in, late_low)
    down_sums, gate_sums, out_joined, late_up = together(down_sums, gate_sums, out_joined, late_up)
    if by_bits():
        out_joined = lax.psum_scatter(out_joined, "dp", scatter_dimension=0, tiled=True)
    down_half = list(fold(bits, down_sums))
    down_half[1], late_up = together(down_half[1], late_up)
    up_sums = weight_grads(bits, normed_mid, late_up, normed_mid, late_up, *halves)

    leaving = list(down_half)
    pulls, gate_sums, mix_grad, down_half[1], up_sums = together(pulls, gate_sums, mix_grad, down_half[1], up_sums)
    if relayed(hops):
        pulls = [pulls[0] + lax.ppermute(pulls[1], "seq", [(0, 1)]), pulls[1]]
    leaving[1] = down_half[1]
    down_sums = second_swap(leaving)
    gate_sums = first_swap(gate_sums)
    query_grad, key_grad, value_grad, edge, taps_grad, logit_grad = pl_backward(
        pulls, back_transits, proj, taps, info, beta,
        (query, key, value, inverse, fresh, carry), mix_grad, state, heads, seqs, count, size,
    )
    edge, up_sums = together(edge, up_sums)
    edge = shifted(edge, "seq", -1)
    up_sums = first_swap(up_sums)

    gate_sums, edge, down_sums, query_grad, key_grad, value_grad, logit_grad, taps_grad, down_part, down_out = together(
        gate_sums, edge, down_sums, query_grad, key_grad, value_grad, logit_grad, taps_grad, down_part, down_out
    )
    query_grad, key_grad, value_grad = (
        (grad + jnp.pad(edge[kind], ((0, 0), (count - 8, 0), (0, 0)))).astype(bf16).reshape(rows, channels)
        for kind, grad in enumerate((query_grad, key_grad, value_grad))
    )
    third = channels // 2
    first_grads = jnp.concatenate([query_grad, value_grad[:, :third]], axis=1)
    second_grads = jnp.concatenate([key_grad, value_grad[:, third:]], axis=1)
    mixed_sums = weight_grads(bits, normed_in, first_grads, normed_in, second_grads)
    beta_low = logit_grad.astype(bf16).reshape(rows, heads)
    down_joined = join(bits, down_sums)
    mixed_sums, gate_sums, up_sums, out_joined, down_joined = together(
        mixed_sums, gate_sums, up_sums, out_joined, down_joined
    )
    sums_down = last_sum(down_joined)
    feed_half = fold_two(bits, tuple(gate_sums), tuple(up_sums))
    mixed_sums, feed_half, first_grads, second_grads = together(mixed_sums, feed_half, first_grads, second_grads)
    in_part = pl_input_back(
        (first_grads, second_grads, gate_low, beta_low),
        (query_weight, key_weight, value_weight, gate_weight, beta_weight),
    )
    feed_sums = second_swap(feed_half)
    mixed_sums = first_swap(mixed_sums)
    block_output = own_half(middle, half) + (own_half(down_part, half) + swapped(down_out))
    grad_beta = tn(normed_in, beta_low)
    head_part = jnp.sum(gain_grad, axis=0)
    head_part = head_part + swapped(head_part)
    blocks = lax.axis_size("dp") * lax.axis_size("seq")
    taps_piece = taps_grad.reshape(12 * heads, blocks, size // blocks).transpose(1, 0, 2).reshape(blocks, -1)
    feed_sums, block_output, grad_beta, head_part, taps_piece, in_part = together(
        feed_sums, block_output, grad_beta, head_part, taps_piece, in_part
    )
    feed_joined = join(bits, feed_sums, 2)
    sums_feed = last_sum(feed_joined)
    mixed_sums, sums_down = together(mixed_sums, sums_down, feed_joined)[:2]
    mixed_half = fold(bits, mixed_sums)
    mixed_sums = second_swap(mixed_half)
    mixed_joined = join(bits, mixed_sums)
    mixed_joined, out_joined, in_part, sums_feed = together(mixed_joined, out_joined, in_part, sums_feed)
    sums_mixed = last_sum(mixed_joined)
    input_grad, mixer_gain_grad = pl_input_norm(
        mine[None].astype(jnp.int32), in_part, swapped(in_part), flat_input, middle_grad, mixer_gain[None, :], seqs
    )

    out_joined = swap_add(swap_add(out_joined, 0), 1)
    grad_mixer_gain = jnp.sum(mixer_gain_grad, axis=0)

    pieces = [
        grad_mixer_gain.reshape(blocks, -1),
        grad_feed_gain.reshape(blocks, -1),
        grad_beta.reshape(blocks, -1),
        taps_piece,
        head_part.reshape(blocks, -1),
    ]
    small = jnp.concatenate(pieces, axis=1)
    small = jnp.pad(small, ((0, 0), (0, -small.shape[1] % 1024)))
    small = small.reshape(blocks, -1, 128)
    if by_bits():
        small = small_sum(small_sum(small, "dp"), "seq")
    else:
        small = small_sum(small, ("dp", "seq"))
    small = small.reshape(-1)
    if by_bits():
        out_joined = out_joined.reshape(-1, out_joined.shape[-1])
    else:
        out_joined = lax.psum_scatter(out_joined, ("dp", "seq"), scatter_dimension=0, tiled=True)
    cuts, at = [], 0
    for piece in pieces:
        cuts.append(small[at : at + piece.shape[1]])
        at += piece.shape[1]
    shape = (seqs, count, half)
    hidden = feed_gate.shape[1]
    wide = channels + third
    return (
        block_output.reshape(shape),
        input_grad.reshape(shape),
        cuts[0],
        sums_mixed[:, :channels],
        sums_mixed[:, wide : wide + channels],
        jnp.concatenate([sums_mixed[:, channels:wide], sums_mixed[:, wide + channels :]], axis=1),
        out_joined[:, channels:],
        cuts[2].reshape(-1, heads),
        cuts[3].reshape(3, 4, heads, size // blocks),
        cuts[4],
        out_joined[:, :channels].T,
        cuts[1],
        sums_feed[:, :hidden],
        sums_feed[:, hidden:],
        sums_down.T,
    )


def solution(mesh):
    return jax.shard_map(
        local,
        mesh=mesh,
        in_specs=(
            P("dp", "seq", "head"),
            P("dp", "seq"),
            P(),
            P(None, "head"),
            P(None, "head"),
            P(None, "head"),
            P(None, "head"),
            P(None, "head"),
            P(None, None, "head", None),
            P(),
            P("head", None),
            P(),
            P(None, "head"),
            P(None, "head"),
            P("head", None),
            P("dp", "seq", "head"),
        ),
        out_specs=(
            P("dp", "seq", "head"),
            P("dp", "seq", "head"),
            P(("dp", "seq")),
            P(("dp", "seq"), "head"),
            P(("dp", "seq"), "head"),
            P(("dp", "seq"), "head"),
            P(("dp", "seq"), "head"),
            P(("dp", "seq"), "head"),
            P(None, None, "head", ("dp", "seq")),
            P(("dp", "seq")),
            P("head", ("dp", "seq")),
            P(("dp", "seq")),
            P(("dp", "seq"), "head"),
            P(("dp", "seq"), "head"),
            P("head", ("dp", "seq")),
        ),
        check_vma=False,
    )
```

```python
import functools
import math

import jax
import jax.numpy as jnp
from jax import lax
from jax.experimental import pallas as pl
from jax.experimental.pallas import tpu as pltpu
from jax.sharding import PartitionSpec as P

HALO = 16
LONGEST = 512

norm_eps = 1e-05
unit_eps = 1e-06
f32 = jnp.float32
bf16 = jnp.bfloat16
VMEM_LIMIT = 48 * 1024 * 1024


def cost(micros):
    return pl.CostEstimate(flops=int(micros * 1e9), bytes_accessed=1 << 20, transcendentals=0)


def nn(a, b):
    return lax.dot_general(a, b, (((1,), (0,)), ((), ())), preferred_element_type=f32)


def nt(a, b):
    return lax.dot_general(a, b, (((1,), (1,)), ((), ())), preferred_element_type=f32)


def tn(a, b):
    return lax.dot_general(a, b, (((0,), (0,)), ((), ())), preferred_element_type=f32)


def split(value):
    high = value.astype(bf16)
    return high, (value - high.astype(f32)).astype(bf16)


def nn3(a, b):
    a_high, a_low = a
    b_high, b_low = b
    return nn(a_high, b_high) + nn(a_high, b_low) + nn(a_low, b_high)


def sigmoid(value):
    return 1.0 / (1.0 + jnp.exp(-value))


def rms_scale(values):
    return lax.rsqrt(jnp.mean(values * values, axis=-1, keepdims=True) + norm_eps)


def norm_back(grad_rows, normed, row_scale, gain_vec):
    grad_hat = grad_rows * gain_vec
    return row_scale * (grad_hat - normed * jnp.mean(grad_hat * normed, axis=-1, keepdims=True))


def grid_of(size):
    row = lax.broadcasted_iota(jnp.int32, (size, size), 0)
    return row, lax.broadcasted_iota(jnp.int32, (size, size), 1)


def unit_inverses(lowers, size):
    row, col = grid_of(size)
    apart = row ^ col
    eye = jnp.where(apart == 0, 1.0, 0.0)
    inverses = [eye - jnp.where(apart == 1, lower, 0.0) for lower in lowers]
    lows = [lower.astype(bf16) for lower in lowers]
    level = 1
    while (1 << level) < size:
        here = (apart >> level) == 1
        rounded = [inverse.astype(bf16) for inverse in inverses]
        right = [nn(jnp.where(here, low, 0.0), near).astype(bf16) for low, near in zip(lows, rounded)]
        inverses = [inverse - nn(near, far) for inverse, near, far in zip(inverses, rounded, right)]
        level += 1
    parts = [split(inverse) for inverse in inverses]
    wholes = [split(lower) for lower in lowers]
    left = [
        (eye - inverse - nn3(whole, part)).astype(bf16)
        for inverse, whole, part in zip(inverses, wholes, parts)
    ]
    return [inverse + nn(part[0], rest) for inverse, part, rest in zip(inverses, parts, left)]


def conv_taps(proj, seq, taps, kind, info, count, lanes=slice(None)):
    rows = []
    for tap in range(4):
        moved = proj[seq, HALO - 3 + tap : HALO - 3 + tap + count, lanes]
        rows.append(moved if tap == 3 else moved * info[:, tap : tap + 1])
    mixed = rows[0] * taps[kind, 0:1, lanes]
    for tap in range(1, 4):
        mixed = mixed + rows[tap] * taps[kind, tap : tap + 1, lanes]
    return rows, mixed


def turned(info, seq):
    row, col = grid_of(8)
    return tn(info[seq].astype(bf16), jnp.where(row == col, 1.0, 0.0).astype(bf16))


def head_column(table, seq, head):
    lane = lax.broadcasted_iota(jnp.int32, table.shape[1:], 1)
    return jnp.sum(jnp.where(lane == head, table[seq], 0.0), axis=1, keepdims=True)


def forward_kernel(
    seqs, count, size, group,
    query_in, key_in, value_in, taps, info, beta,
    query_out, key_out, value_out, inverse_out, fresh_out, carry_out, local_out, reach_out, state_out, transit_out, both_out,
):
    row, col = grid_of(count)
    scale = 1.0 / math.sqrt(size)
    infos = [turned(info, seq) for seq in range(seqs)]
    sames = [infos[seq][:, 5:6] == info[seq, 5:6, :] for seq in range(seqs)]
    every = [(seq, part, slice(part * size, (part + 1) * size)) for part in range(group) for seq in range(seqs)]
    queries, keys, lowers, betas = [], [], [], []
    for seq, part, lanes in every:
        parts = []
        for kind, proj in enumerate((query_in, key_in, value_in)):
            mixed = conv_taps(proj, seq, taps, kind, infos[seq], count, lanes)[1]
            parts.append(mixed * sigmoid(mixed))
        query, key, value = parts
        query = query * (lax.rsqrt(jnp.sum(query * query, axis=1, keepdims=True) + unit_eps) * scale)
        key = key * lax.rsqrt(jnp.sum(key * key, axis=1, keepdims=True) + unit_eps)
        query, key, value = query.astype(bf16), key.astype(bf16), value.astype(bf16)
        query_out[seq, :, lanes], key_out[seq, :, lanes], value_out[seq, :, lanes] = query, key, value
        beta_col = head_column(beta, seq, pl.program_id(0) * group + part)
        queries.append(query)
        keys.append(key)
        betas.append(beta_col)
        lowers.append(jnp.where(sames[seq] & (row > col), nt(key, key) * beta_col, 0.0))
    inverses = unit_inverses(lowers, count)
    for (seq, part, lanes), query, key, beta_col, inverse in zip(every, queries, keys, betas, inverses):
        enter, last = infos[seq][:, 3:4], infos[seq][:, 4:5]
        key_full = key.astype(f32)
        inverse_parts = split(inverse)
        inverse_out[part, seq] = inverse_parts[0]
        right = jnp.concatenate(
            [key_full * (beta_col * enter), value_out[seq, :, lanes].astype(f32) * beta_col], axis=1
        )
        solved = nn3(inverse_parts, split(right))
        solved_high, solved_low = split(solved)
        key_last = (key_full * last).astype(bf16)
        ends = tn(key_last, solved_high) + tn(key_last, solved_low)
        transit_row, transit_col = grid_of(size)
        eye = jnp.where(transit_row == transit_col, 1.0, 0.0)
        transit = eye * info[seq, 3:4, count - 1 :] - ends[:, :size]
        state_out[seq, part] = ends[:, size:]
        transit_out[seq, part] = transit
        both_out[seq, part, 0] = ends[:, size:]
        both_out[seq, part, 1] = transit
        attend = jnp.where(sames[seq] & (row >= col), nt(query, key), 0.0).astype(bf16)
        reads = nn(attend, solved_high)
        local_out[seq, :, lanes] = reads[:, size:]
        reach_out[seq, :, lanes] = (query.astype(f32) * enter - reads[:, :size]).astype(bf16)
        carry_out[seq, :, lanes] = solved_high[:, :size]
        fresh_out[seq, :, lanes] = solved[:, size:]


def pl_forward(proj, taps, info, beta, group, heads, seqs, count, size, channels):
    def rows(dtype):
        return jax.ShapeDtypeStruct((seqs, count, heads * size), dtype)

    row_spec = pl.BlockSpec((seqs, count, group * size), lambda h: (0, 0, h))
    proj_spec = pl.BlockSpec((seqs, count + HALO, group * size), lambda h: (0, 0, h))
    state = jax.ShapeDtypeStruct((seqs, heads, size, size), f32)
    state_spec = pl.BlockSpec((seqs, group, size, size), lambda h: (0, h, 0, 0))
    return pl.pallas_call(
        functools.partial(forward_kernel, seqs, count, size, group),
        grid=(heads // group,),
        in_specs=[proj_spec] * 3
        + [
            pl.BlockSpec((3, 4, group * size), lambda h: (0, 0, h)),
            pl.BlockSpec(info.shape, lambda h: (0, 0, 0)),
            pl.BlockSpec(beta.shape, lambda h: (0, 0, 0)),
        ],
        out_specs=[row_spec] * 3
        + [pl.BlockSpec((group, seqs, count, count), lambda h: (h, 0, 0, 0))]
        + [row_spec] * 4
        + [state_spec] * 2
        + [pl.BlockSpec((seqs, group, 2, size, size), lambda h: (0, h, 0, 0, 0))],
        out_shape=[rows(bf16)] * 3
        + [jax.ShapeDtypeStruct((heads, seqs, count, count), bf16)]
        + [rows(f32), rows(bf16), rows(f32), rows(bf16)]
        + [state] * 2
        + [jax.ShapeDtypeStruct((seqs, heads, 2, size, size), f32)],
        compiler_params=pltpu.CompilerParams(vmem_limit_bytes=VMEM_LIMIT),
        cost_estimate=cost(17),
    )(*proj, taps, info, beta)


def arrived(boths, farthest, seq):
    total = farthest[seq, 0]
    for both in boths[::-1]:
        total = both[seq, 0, 0] + nn3(split(both[seq, 0, 1]), split(total))
    return total


def read_kernel(seqs, count, size, heads, hops, *refs):
    boths, farthest = refs[: hops - 1], refs[hops - 1]
    local, reach, gate, gain, out_weight, state_out, mix_out, gated_out, part_out, held = refs[hops:]
    head = pl.program_id(0)
    for seq in range(seqs):
        state = arrived(boths, farthest, seq)
        state_out[seq, 0] = state
        state_high, state_low = split(state)
        moved = reach[seq]
        mix = local[seq] + nn(moved, state_high) + nn(moved, state_low)
        mix_out[seq] = mix
        gate_now = gate[seq]
        gated = (mix * rms_scale(mix) * gain[...] * (gate_now * sigmoid(gate_now))).astype(bf16)
        gated_out[seq] = gated
        held[head, seq * count : (seq + 1) * count, :] = gated

    @pl.when(head == heads - 1)
    def _():
        rows = jnp.concatenate([held[h] for h in range(heads)], axis=1)
        part_out[...] = nn(rows, out_weight[...])


def pl_read(boths, farthest, local, reach, gate, gain, out_weight, heads, seqs, count, size, width):
    row_spec = pl.BlockSpec((seqs, count, size), lambda h: (0, 0, h))
    state_spec = pl.BlockSpec((seqs, 1, size, size), lambda h: (0, h, 0, 0))
    both_spec = pl.BlockSpec((seqs, 1, 2, size, size), lambda h: (0, h, 0, 0, 0))
    hops = len(boths) + 1
    return pl.pallas_call(
        functools.partial(read_kernel, seqs, count, size, heads, hops),
        grid=(heads,),
        in_specs=[both_spec] * (hops - 1)
        + [state_spec]
        + [row_spec] * 3
        + [pl.BlockSpec((1, size), lambda h: (0, 0)), pl.BlockSpec((heads * size, width), lambda h: (0, 0))],
        out_specs=[state_spec, row_spec, row_spec, pl.BlockSpec((seqs * count, width), lambda h: (0, 0))],
        out_shape=[
            jax.ShapeDtypeStruct((seqs, heads, size, size), f32),
            jax.ShapeDtypeStruct((seqs, count, heads * size), f32),
            jax.ShapeDtypeStruct((seqs, count, heads * size), bf16),
            jax.ShapeDtypeStruct((seqs * count, width), f32),
        ],
        scratch_shapes=[pltpu.VMEM((heads, seqs * count, size), bf16)],
        compiler_params=pltpu.CompilerParams(vmem_limit_bytes=VMEM_LIMIT),
        cost_estimate=cost(7),
    )(*boths, farthest, local, reach, gate, gain, out_weight)


def hidden_back_kernel(gate_grad, up_grad, feed_gate, feed_up, out):
    out[...] = nt(gate_grad[...], feed_gate[...]) + nt(up_grad[...], feed_up[...])


def pl_hidden_back(gate_grad, up_grad, feed_gate, feed_up):
    rows, hidden = gate_grad.shape
    width = feed_gate.shape[0]
    step = width // 4
    whole = pl.BlockSpec((rows, hidden), lambda i: (0, 0))
    weight = pl.BlockSpec((step, hidden), lambda i: (i, 0))
    return pl.pallas_call(
        hidden_back_kernel,
        grid=(4,),
        in_specs=[whole, whole, weight, weight],
        out_specs=pl.BlockSpec((rows, step), lambda i: (0, i)),
        out_shape=jax.ShapeDtypeStruct((rows, width), f32),
        compiler_params=pltpu.CompilerParams(vmem_limit_bytes=VMEM_LIMIT),
        cost_estimate=cost(6),
    )(gate_grad, up_grad, feed_gate, feed_up)


def gate_back_kernel(
    seqs, count, size,
    mid_part, mid_other, full_grad, middle, feed_gain, out_weight, mix, gate, gain, reach,
    middle_grad, mixer_grad, feed_gain_grad, mix_grad, gate_grad, gain_grad, pull,
):
    head = pl.program_id(0)

    @pl.when(head == 0)
    def _():
        gain_grad[...] = jnp.zeros_like(gain_grad)
        feed_gain_grad[...] = jnp.zeros_like(feed_gain_grad)
        tall = 64

        def some_rows(index, carried):
            here = pl.ds(pl.multiple_of(index * tall, tall), tall)
            mid_grad = mid_part[here, :] + mid_other[here, :]
            scale = rms_scale(middle[here, :])
            normed = middle[here, :] * scale
            feed_gain_grad[...] += jnp.sum((mid_grad * normed).reshape(tall // 8, 8, normed.shape[1]), axis=0)
            whole = full_grad[here, :] + norm_back(mid_grad, normed, scale, feed_gain[...])
            middle_grad[here, :] = whole
            mixer_grad[here, :] = whole.astype(bf16)
            return carried

        lax.fori_loop(0, seqs * count // tall, some_rows, 0)

    grads = nt(mixer_grad[...], out_weight[...])
    for seq in range(seqs):
        grad = grads[seq * count : (seq + 1) * count]
        mix_now, gate_now = mix[seq], gate[seq]
        scale = rms_scale(mix_now)
        normed = mix_now * scale
        sig = sigmoid(gate_now)
        gate_silu = gate_now * sig
        with_norm = grad * normed
        gain_grad[...] += jnp.sum((with_norm * gate_silu).reshape(count // 8, 8, size), axis=0)
        gate_grad[seq] = (with_norm * gain[...] * (sig * (1.0 + gate_now * (1.0 - sig)))).astype(bf16)
        normed_grad = grad * gain[...] * gate_silu
        mix_grad_now = scale * (normed_grad - normed * jnp.mean(normed_grad * normed, axis=1, keepdims=True))
        low = mix_grad_now.astype(bf16)
        mix_grad[seq] = low
        pull[seq, 0] = tn(reach[seq], low)


def pl_gate_back(
    mid_part, mid_other, full_grad, middle, feed_gain, out_weight, mix, gate, gain, reach, heads, seqs, count, size
):
    rows, width = middle.shape
    row_spec = pl.BlockSpec((seqs, count, size), lambda h: (0, 0, h))

    def fixed(*dims):
        return pl.BlockSpec(dims, lambda h: (0,) * len(dims))

    return pl.pallas_call(
        functools.partial(gate_back_kernel, seqs, count, size),
        grid=(heads,),
        in_specs=[fixed(rows, width)] * 4
        + [
            fixed(1, width),
            pl.BlockSpec((size, width), lambda h: (h, 0)),
            row_spec,
            row_spec,
            fixed(1, size),
            row_spec,
        ],
        out_specs=[
            fixed(rows, width),
            fixed(rows, width),
            fixed(8, width),
            row_spec,
            row_spec,
            fixed(8, size),
            pl.BlockSpec((seqs, 1, size, size), lambda h: (0, h, 0, 0)),
        ],
        out_shape=[
            jax.ShapeDtypeStruct((rows, width), f32),
            jax.ShapeDtypeStruct((rows, width), bf16),
            jax.ShapeDtypeStruct((8, width), f32),
            jax.ShapeDtypeStruct((seqs, count, heads * size), bf16),
            jax.ShapeDtypeStruct((seqs, count, heads * size), bf16),
            jax.ShapeDtypeStruct((8, size), f32),
            jax.ShapeDtypeStruct((seqs, heads, size, size), f32),
        ],
        compiler_params=pltpu.CompilerParams(vmem_limit_bytes=VMEM_LIMIT),
        cost_estimate=cost(9),
    )(mid_part, mid_other, full_grad, middle, feed_gain, out_weight, mix, gate, gain, reach)


def backward_kernel(seqs, count, size, hops, *refs):
    pulls, transits = refs[:hops], refs[hops : 2 * hops - 1]
    (
        query_in, key_in, value_in, taps, info_rows, beta,
        query_ref, key_ref, value_ref, inverse_ref, fresh_ref, carry_ref, mix_grad_ref, state_ref,
        query_grad_out, key_grad_out, value_grad_out, edge_out, taps_grad_out, logit_grad_out,
    ) = refs[2 * hops - 1 :]
    head = pl.program_id(0)
    row, col = grid_of(count)
    scale = 1.0 / math.sqrt(size)

    @pl.when(head == 0)
    def _():
        logit_grad_out[...] = jnp.zeros_like(logit_grad_out)

    taps_totals = None
    for seq in range(seqs):
        total = pulls[-1][seq, 0]
        for pull, transit in zip(pulls[-2::-1], transits[::-1]):
            transit_high, transit_low = split(transit[seq, 0])
            total_high, total_low = split(total)
            total = pull[seq, 0] + (
                tn(transit_high, total_high) + tn(transit_high, total_low) + tn(transit_low, total_high)
            )
        out_state_grad = total.astype(bf16)
        state = state_ref[seq, 0].astype(bf16)
        query, key, value = query_ref[seq], key_ref[seq], value_ref[seq]
        mix_grad = mix_grad_ref[seq]
        info = turned(info_rows, seq)
        enter, last = info[:, 3:4], info[:, 4:5]
        same = info[:, 5:6] == info_rows[seq, 5:6, :]
        causal = same & (row >= col)
        strict = same & (row > col)
        beta_col = head_column(beta, seq, head)
        key_full = key.astype(f32)
        key_last = (key_full * last).astype(bf16)
        update = (fresh_ref[seq] - nn(carry_ref[seq], state)).astype(bf16)
        attend = jnp.where(causal, nt(query, key), 0.0).astype(bf16)
        update_grad = tn(attend, mix_grad) + nn(key_last, out_state_grad)
        right_grad = tn(inverse_ref[0, seq], update_grad.astype(bf16))
        right_low = right_grad.astype(bf16)
        both = nt(jnp.concatenate([mix_grad, right_low], axis=0), update)
        attend_grad = jnp.where(causal, both[:count], 0.0).astype(bf16)
        lower_grad = jnp.where(strict, -both[count:], 0.0)
        gram = nt(key, key)
        surprise = value.astype(f32) - enter * nn(key, state)
        beta_grad = jnp.sum(right_grad * surprise, axis=1, keepdims=True) + jnp.sum(
            lower_grad * gram, axis=1, keepdims=True
        )
        logit_grad = beta_grad * beta_col * (1.0 - beta_col)
        lane = lax.broadcasted_iota(jnp.int32, logit_grad_out.shape[1:], 1)
        logit_grad_out[seq] += jnp.where(lane == head, logit_grad, 0.0)
        value_grad = right_grad * beta_col
        gram_grad = (lower_grad * beta_col).astype(bf16)
        stacked = jnp.concatenate([gram_grad, attend_grad], axis=0)
        forth = nn(stacked, key)
        back = tn(stacked, jnp.concatenate([key, query], axis=0))
        through = nt(
            jnp.concatenate([(value_grad * enter).astype(bf16), mix_grad], axis=0), state
        )
        key_grad = forth[:count] + back - through[:count] + last * nt(update, out_state_grad)
        query_grad = forth[count:] + enter * through[count:]
        for kind, (proj, grad, out) in enumerate(
            (
                (query_in, query_grad, query_grad_out),
                (key_in, key_grad, key_grad_out),
                (value_in, value_grad, value_grad_out),
            )
        ):
            rows, mixed = conv_taps(proj, seq, taps, kind, info, count)
            sig = sigmoid(mixed)
            if kind < 2:
                active = mixed * sig
                norm = lax.rsqrt(jnp.sum(active * active, axis=1, keepdims=True) + unit_eps)
                unit = active * norm
                grad = grad - unit * jnp.sum(grad * unit, axis=1, keepdims=True)
                grad = grad * (norm * scale if kind == 0 else norm)
            mixed_grad = grad * (sig * (1.0 + mixed * (1.0 - sig)))
            sums = [jnp.sum((mixed_grad * rows[tap]).reshape(count // 8, 8, size), axis=0) for tap in range(4)]
            blank = jnp.zeros((8, size), f32)
            proj_grad = mixed_grad * taps[kind, 3:4, :]
            edge = blank
            for tap in range(3):
                delay = 3 - tap
                masked = mixed_grad * (info[:, tap : tap + 1] * taps[kind, tap : tap + 1, :])
                moved = pltpu.roll(masked, count - delay, 0)
                at = lax.broadcasted_iota(jnp.int32, (count, size), 0)
                proj_grad = proj_grad + jnp.where(at < count - delay, moved, 0.0)
                first = pltpu.roll(masked[:8], 8 - delay, 0)
                at_edge = lax.broadcasted_iota(jnp.int32, (8, size), 0)
                edge = edge + jnp.where(at_edge >= 8 - delay, first, 0.0)
            out[seq] = proj_grad
            edge_out[kind, seq] = edge
            sums = jnp.stack([jnp.sum(part, axis=0) for part in sums])
            if seq == 0:
                taps_grad_out[kind] = sums
            else:
                taps_grad_out[kind] += sums


def pl_backward(pulls, transits, proj, taps, info, beta, saved, mix_grad, state, heads, seqs, count, size):
    hops = len(pulls)
    row_spec = pl.BlockSpec((seqs, count, size), lambda h: (0, 0, h))
    state_spec = pl.BlockSpec((seqs, 1, size, size), lambda h: (0, h, 0, 0))
    proj_spec = pl.BlockSpec((seqs, count + HALO, size), lambda h: (0, 0, h))
    return pl.pallas_call(
        functools.partial(backward_kernel, seqs, count, size, hops),
        grid=(heads,),
        in_specs=[state_spec] * (2 * hops - 1)
        + [proj_spec] * 3
        + [
            pl.BlockSpec((3, 4, size), lambda h: (0, 0, h)),
            pl.BlockSpec(info.shape, lambda h: (0, 0, 0)),
            pl.BlockSpec(beta.shape, lambda h: (0, 0, 0)),
        ]
        + [row_spec] * 3
        + [pl.BlockSpec((1, seqs, count, count), lambda h: (h, 0, 0, 0))]
        + [row_spec] * 3
        + [state_spec],
        out_specs=[row_spec] * 3
        + [
            pl.BlockSpec((3, seqs, 8, size), lambda h: (0, 0, 0, h)),
            pl.BlockSpec((3, 4, size), lambda h: (0, 0, h)),
            pl.BlockSpec((seqs, count, heads), lambda h: (0, 0, 0)),
        ],
        out_shape=[jax.ShapeDtypeStruct((seqs, count, heads * size), f32)] * 3
        + [
            jax.ShapeDtypeStruct((3, seqs, 8, heads * size), f32),
            jax.ShapeDtypeStruct((3, 4, heads * size), f32),
            jax.ShapeDtypeStruct((seqs, count, heads), f32),
        ],
        compiler_params=pltpu.CompilerParams(vmem_limit_bytes=VMEM_LIMIT),
        cost_estimate=cost(17),
    )(*pulls, *transits, *proj, taps, info, beta, *saved, mix_grad, state)


def input_back_kernel(first, second, gate_grad, beta_grad, query_w, key_w, value_w, gate_w, beta_w, out):
    channels = query_w.shape[1]
    third = channels // 2
    out[...] = (
        nt(first[:, :channels], query_w[...])
        + nt(second[:, :channels], key_w[...])
        + nt(first[:, channels:], value_w[:, :third])
        + nt(second[:, channels:], value_w[:, third:])
        + nt(gate_grad[...], gate_w[...])
        + nt(beta_grad[...], beta_w[...])
    )


def pl_input_back(grads, weights):
    rows = grads[0].shape[0]
    width = weights[0].shape[0]
    step = width // 4
    return pl.pallas_call(
        input_back_kernel,
        grid=(4,),
        in_specs=[pl.BlockSpec(grad.shape, lambda i: (0, 0)) for grad in grads]
        + [pl.BlockSpec((step, weight.shape[1]), lambda i: (i, 0)) for weight in weights],
        out_specs=pl.BlockSpec((rows, step), lambda i: (0, i)),
        out_shape=jax.ShapeDtypeStruct((rows, width), f32),
        compiler_params=pltpu.CompilerParams(vmem_limit_bytes=VMEM_LIMIT),
        cost_estimate=cost(1),
    )(*grads, *weights)


def input_norm_kernel(which, part, other, value, middle_grad, gain, out, gain_grad):
    grad = part[...] + other[...]
    scale = rms_scale(value[...])
    normed = value[...] * scale
    share = jnp.sum((grad * normed).reshape(grad.shape[0] // 8, 8, grad.shape[1]), axis=0)

    @pl.when(pl.program_id(0) == 0)
    def _():
        gain_grad[...] = share

    @pl.when(pl.program_id(0) > 0)
    def _():
        gain_grad[...] += share

    result = middle_grad[...] + norm_back(grad, normed, scale, gain[...])
    half = out.shape[1]
    out[...] = jnp.where(which[0] == 0, result[:, :half], result[:, half:])


def pl_input_norm(which, part, other, value, middle_grad, gain, steps):
    rows, width = value.shape
    tall = pl.BlockSpec((rows // steps, width), lambda i, which: (i, 0))
    return pl.pallas_call(
        input_norm_kernel,
        grid_spec=pltpu.PrefetchScalarGridSpec(
            num_scalar_prefetch=1,
            grid=(steps,),
            in_specs=[tall] * 4 + [pl.BlockSpec((1, width), lambda i, which: (0, 0))],
            out_specs=[
                pl.BlockSpec((rows // steps, width // 2), lambda i, which: (i, 0)),
                pl.BlockSpec((8, width), lambda i, which: (0, 0)),
            ],
        ),
        out_shape=[jax.ShapeDtypeStruct((rows, width // 2), f32), jax.ShapeDtypeStruct((8, width), f32)],
        compiler_params=pltpu.CompilerParams(vmem_limit_bytes=VMEM_LIMIT),
        cost_estimate=cost(1),
    )(which, part, other, value, middle_grad, gain)


def shifted(value, axis, steps):
    count = lax.axis_size(axis)
    initial, last = (max(0, -steps), min(count, count - steps))
    return lax.ppermute(value, axis, [(source, source + steps) for source in range(initial, last)])


def from_ahead(value, hops):
    if not relayed(hops):
        return [shifted(value, "seq", -hop) for hop in range(1, hops + 1)]
    return [lax.ppermute(value, "seq", pairs) for pairs in ([(1, 0), (3, 2)], [(2, 0), (3, 1)])]


def relayed(hops):
    return by_bits() and hops == 2


def swapped(value):
    return lax.ppermute(value, "head", [(0, 1), (1, 0)])


def in_order(own, other, axis):
    mine = lax.axis_index("head") == 0
    return jnp.where(
        mine, jnp.concatenate([own, other], axis=axis), jnp.concatenate([other, own], axis=axis)
    )


def own_half(value, half):
    return lax.dynamic_slice_in_dim(value, lax.axis_index("head") * half, half, value.ndim - 1)


def pick(value, index, axis):
    return lax.dynamic_index_in_dim(value, index, axis, keepdims=False)


def together(*values):
    return lax.optimization_barrier(values)


def weight_kernel(block, first_window, second_window, bits, first_left, first_right, second_left, second_right, *refs):
    first_leaves, first_stays, second_leaves, second_stays, held, held_second = refs
    low, high = bits[0], bits[1]
    held[...] = tn(first_left[...], first_right[:, first_window])
    for part in range(2):
        base = part * 2 * block
        first_leaves[0, part] = held[pl.ds(pl.multiple_of(base + (1 - low) * block, 8), block), :]
        first_stays[0, part] = held[pl.ds(pl.multiple_of(base + low * block, 8), block), :]
    held_second[...] = tn(second_left[...], second_right[:, second_window])
    second_leaves[0] = held_second[pl.ds(pl.multiple_of((1 - high) * 2 * block, 8), 2 * block), :]
    second_stays[0] = held_second[pl.ds(pl.multiple_of(high * 2 * block, 8), 2 * block), :]


def fold_kernel(block, bits, first_stays, first_comes, second_stays, second_comes, *refs):
    first_leaves, first_keeps, second_leaves, second_keeps = refs
    low, high = bits[0], bits[1]
    first_leaves[0] = first_stays[0, 1 - high] + first_comes[0, 1 - high]
    first_keeps[0] = first_stays[0, high] + first_comes[0, high]
    away = pl.ds(pl.multiple_of((1 - low) * block, 8), block)
    here = pl.ds(pl.multiple_of(low * block, 8), block)
    second_leaves[0] = second_stays[0, away] + second_comes[0, away]
    second_keeps[0] = second_stays[0, here] + second_comes[0, here]


def join_kernel(pieces, bits, first_keeps, first_comes, second_keeps, second_comes, out):
    first, second = first_keeps.shape[-1] // pieces, second_keeps.shape[-1] // pieces
    at = 0
    for piece in range(pieces):
        lanes = slice(piece * first, (piece + 1) * first)
        out[:, at : at + first] = first_keeps[0, :, lanes] + first_comes[0, :, lanes]
        at += first
        lanes = slice(piece * second, (piece + 1) * second)
        out[:, at : at + second] = second_keeps[0, :, lanes] + second_comes[0, :, lanes]
        at += second


def per_block(kernel, bits, steps, args, in_specs, out_specs, out_shape, scratch=()):
    return pl.pallas_call(
        kernel,
        grid_spec=pltpu.PrefetchScalarGridSpec(
            num_scalar_prefetch=1, grid=(steps,), in_specs=in_specs, out_specs=out_specs, scratch_shapes=list(scratch)
        ),
        out_shape=out_shape,
        compiler_params=pltpu.CompilerParams(vmem_limit_bytes=VMEM_LIMIT),
        cost_estimate=cost(1),
    )(bits, *args)


def four_block(dims):
    return pl.BlockSpec((1,) + dims, lambda z, bits: (z,) + (0,) * len(dims))


def swap_bit(value, bit):
    return lax.ppermute(value, "seq", [(source, source ^ (1 << bit)) for source in range(4)])


def by_bits():
    return lax.axis_size("seq") == 4


def weight_grads(bits, first_left, first_right, second_left, second_right, first_window=None, second_window=None):
    first_window = first_window or slice(0, first_right.shape[1])
    second_window = second_window or slice(0, second_right.shape[1])
    if not by_bits():
        return tn(first_left, first_right[:, first_window]), tn(second_left, second_right[:, second_window])
    dp = lax.axis_size("dp")
    tokens, rows = first_left.shape
    first_cols = first_window.stop - first_window.start
    second_cols = second_window.stop - second_window.start
    block = rows // (4 * dp)
    left_spec = pl.BlockSpec((tokens, 4 * block), lambda z, bits: (0, z))

    def whole(cols):
        return pl.BlockSpec((tokens, cols), lambda z, bits: (0, 0))

    first, second = (2, block, first_cols), (2 * block, second_cols)
    return per_block(
        functools.partial(weight_kernel, block, first_window, second_window),
        bits,
        dp,
        (first_left, first_right, second_left, second_right),
        [left_spec, whole(first_right.shape[1]), left_spec, whole(second_right.shape[1])],
        [four_block(dims) for dims in (first, first, second, second)],
        [jax.ShapeDtypeStruct((dp,) + dims, f32) for dims in (first, first, second, second)],
        [pltpu.VMEM((4 * block, first_cols), f32), pltpu.VMEM((4 * block, second_cols), f32)],
    )


def paired_kernel(first_left, first_right, second_left, second_right, out):
    cut = first_right.shape[1]
    out[:, :cut] = tn(first_left[...], first_right[...])
    out[:, cut:] = tn(second_left[...], second_right[...])


def paired_grads(first_left, first_right, second_left, second_right):
    tokens, rows = first_left.shape
    cols = first_right.shape[1] + second_right.shape[1]
    step = rows // 4
    left_spec = pl.BlockSpec((tokens, step), lambda i: (0, i))
    whole = [pl.BlockSpec(right.shape, lambda i: (0, 0)) for right in (first_right, second_right)]
    return pl.pallas_call(
        paired_kernel,
        grid=(4,),
        in_specs=[left_spec, whole[0], left_spec, whole[1]],
        out_specs=pl.BlockSpec((step, cols), lambda i: (i, 0)),
        out_shape=jax.ShapeDtypeStruct((rows, cols), f32),
        compiler_params=pltpu.CompilerParams(vmem_limit_bytes=VMEM_LIMIT),
        cost_estimate=cost(4),
    )(first_left, first_right, second_left, second_right)


def first_swap(parts):
    if not by_bits():
        return parts
    first_leaves, first_stays, second_leaves, second_stays = parts
    return first_stays, swap_bit(first_leaves, 0), second_stays, swap_bit(second_leaves, 1)


def fold(bits, parts):
    if not by_bits():
        return parts
    dp = lax.axis_size("dp")
    block, first_cols, second_cols = parts[0].shape[2], parts[0].shape[3], parts[2].shape[2]
    ins = [(2, block, first_cols)] * 2 + [(2 * block, second_cols)] * 2
    outs = [(block, first_cols)] * 2 + [(block, second_cols)] * 2
    return per_block(
        functools.partial(fold_kernel, block),
        bits,
        dp,
        parts,
        [four_block(dims) for dims in ins],
        [four_block(dims) for dims in outs],
        [jax.ShapeDtypeStruct((dp,) + dims, f32) for dims in outs],
    )


def fold_two_kernel(block, bits, *refs):
    low, high = bits[0], bits[1]
    first_leaves, first_keeps, second_leaves, second_keeps = refs[8:]
    away = pl.ds(pl.multiple_of((1 - low) * block, 8), block)
    here = pl.ds(pl.multiple_of(low * block, 8), block)
    first_at = second_at = 0
    for first_stays, first_comes, second_stays, second_comes in (refs[:4], refs[4:8]):
        lanes = slice(first_at, first_at + first_stays.shape[-1])
        first_leaves[0, :, lanes] = first_stays[0, 1 - high] + first_comes[0, 1 - high]
        first_keeps[0, :, lanes] = first_stays[0, high] + first_comes[0, high]
        first_at = lanes.stop
        lanes = slice(second_at, second_at + second_stays.shape[-1])
        second_leaves[0, :, lanes] = second_stays[0, away] + second_comes[0, away]
        second_keeps[0, :, lanes] = second_stays[0, here] + second_comes[0, here]
        second_at = lanes.stop


def fold_two(bits, one, two):
    if not by_bits():
        return one + two
    dp = lax.axis_size("dp")
    block = one[0].shape[2]
    ins, outs = [], [0, 0]
    for part in (one, two):
        first_cols, second_cols = part[0].shape[3], part[2].shape[2]
        ins += [(2, block, first_cols)] * 2 + [(2 * block, second_cols)] * 2
        outs = [outs[0] + first_cols, outs[1] + second_cols]
    outs = [(block, outs[0])] * 2 + [(block, outs[1])] * 2
    return per_block(
        functools.partial(fold_two_kernel, block),
        bits,
        dp,
        tuple(one) + tuple(two),
        [four_block(dims) for dims in ins],
        [four_block(dims) for dims in outs],
        [jax.ShapeDtypeStruct((dp,) + dims, f32) for dims in outs],
    )


def second_swap(parts):
    if not by_bits():
        return parts
    first_leaves, first_keeps, second_leaves, second_keeps = parts
    return first_keeps, swap_bit(first_leaves, 1), second_keeps, swap_bit(second_leaves, 0)


def join(bits, parts, pieces=1):
    if not by_bits():
        return tuple(
            lax.psum_scatter(part, ("dp", "seq"), scatter_dimension=0, tiled=True) for part in parts
        )
    dp = lax.axis_size("dp")
    block, first_cols, second_cols = parts[0].shape[1], parts[0].shape[2], parts[2].shape[2]
    return per_block(
        functools.partial(join_kernel, pieces),
        bits,
        dp,
        parts,
        [four_block((block, cols)) for cols in (first_cols, first_cols, second_cols, second_cols)],
        pl.BlockSpec((block, first_cols + second_cols), lambda z, bits: (z, 0)),
        jax.ShapeDtypeStruct((dp * block, first_cols + second_cols), f32),
    )


def last_sum(joined):
    if not by_bits():
        return jnp.concatenate(joined, axis=1)
    return lax.psum_scatter(joined, "dp", scatter_dimension=0, tiled=True)


def swap_add(value, bit):
    if not by_bits():
        return value
    value = value.reshape(2 - bit, 2, -1, value.shape[-1])
    mine = (lax.axis_index("seq") >> bit) & 1
    return pick(value, mine, 1) + swap_bit(pick(value, 1 - mine, 1), bit)


def small_sum(value, names):
    if not by_bits():
        return lax.psum_scatter(value, names, scatter_dimension=0, tiled=True)
    if names == "dp" and lax.axis_size("dp") != 4:
        return lax.psum_scatter(value, "dp", scatter_dimension=0, tiled=True)
    value = value.reshape((2, 2) + (value.shape[0] // 4,) + value.shape[1:])
    for bit in range(2):
        mine = (lax.axis_index(names) >> bit) & 1
        perm = [(source, source ^ (1 << bit)) for source in range(4)]
        value = pick(value, mine, 1 - bit) + lax.ppermute(pick(value, 1 - mine, 1 - bit), names, perm)
    return value


def local(
    block_input,
    segment_ids,
    mixer_gain,
    query_weight,
    key_weight,
    value_weight,
    gate_weight,
    beta_weight,
    conv_weight,
    head_gain,
    out_weight,
    feed_gain,
    feed_gate,
    feed_up,
    feed_down,
    grad_output,
):
    seqs, count, half = block_input.shape
    rows = seqs * count
    size = head_gain.shape[0]
    heads = beta_weight.shape[1]
    channels = heads * size
    width = query_weight.shape[0]
    hops = -(-(LONGEST - 1) // count)
    hops = min(hops, lax.axis_size("seq") - 1)

    other_input = swapped(block_input)
    segments = segment_ids.astype(f32)
    before = shifted(
        jnp.concatenate([block_input[:, count - 3 :], segments[:, count - 3 :, None]], axis=2), "seq", 1
    )
    edge_ids = before[:, :, half]
    before = before[:, :, :half]
    other_before = swapped(before)
    full_input = in_order(block_input, other_input, 2)
    full_before = in_order(before, other_before, 2)
    other_grad = swapped(grad_output)

    extended = jnp.concatenate(
        [jnp.zeros((seqs, HALO - 3, width), f32), full_before, full_input], axis=1
    )
    extended_low = (extended * rms_scale(extended) * mixer_gain).astype(bf16)
    flat = extended_low.reshape(seqs * (count + HALO), width)
    proj = [
        nn(flat, weight).reshape(seqs, count + HALO, channels)
        for weight in (query_weight, key_weight, value_weight)
    ]
    normed_in = extended_low[:, HALO:].reshape(rows, width)
    beta = jax.nn.sigmoid(nn(normed_in, beta_weight)).reshape(seqs, count, heads)
    gate_proj = nn(normed_in, gate_weight).reshape(seqs, count, channels)

    extended_ids = jnp.concatenate([edge_ids, segments], axis=1)
    masks = [(extended_ids[:, tap : tap + count] == segments) for tap in range(3)]
    enter = segments == edge_ids[:, 2:3]
    last = segments == segments[:, count - 1 :]
    zero = jnp.zeros_like(segments)
    info = jnp.stack(
        [mask.astype(f32) for mask in masks] + [enter.astype(f32), last.astype(f32), segments, zero, zero], axis=1
    )
    taps = conv_weight.reshape(3, 4, channels)
    gain = head_gain[None, :]

    (query, key, value, inverse, fresh, carry, local_mix, reach, state_end, transit, both) = pl_forward(
        proj, taps, info, beta, 2 if heads % 2 == 0 else 1, heads, seqs, count, size, channels
    )
    boths = [shifted(both, "seq", hop) for hop in range(1, hops)]
    farthest = shifted(state_end, "seq", hops)
    back_transits = [shifted(transit, "seq", -hop) for hop in range(1, hops)]
    full_grad = in_order(grad_output, other_grad, 2).reshape(rows, width)
    down_grad = full_grad.astype(bf16)
    inner_grad = nt(down_grad, feed_down)
    boths, farthest, back_transits, full_grad, down_grad, inner_grad = together(
        boths, farthest, back_transits, full_grad, down_grad, inner_grad
    )
    state, mix, gated, part = pl_read(
        boths, farthest, local_mix, reach, gate_proj, gain, out_weight, heads, seqs, count, size, width
    )
    gated = gated.reshape(rows, channels)
    flat_input = full_input.reshape(rows, width)
    middle = flat_input + (part + swapped(part))
    middle_scale = rms_scale(middle)
    middle_normed = middle * middle_scale
    normed_mid = (middle_normed * feed_gain).astype(bf16)
    gate_act = nn(normed_mid, feed_gate)
    up_act = nn(normed_mid, feed_up)
    gate_sig = jax.nn.sigmoid(gate_act)
    gate_silu = gate_act * gate_sig
    inner = (gate_silu * up_act).astype(bf16)
    cut = feed_down.shape[0] // 256 * 128
    gate_grad = (inner_grad * up_act * (gate_sig * (1.0 + gate_act * (1.0 - gate_sig)))).astype(bf16)
    up_grad = (inner_grad * gate_silu).astype(bf16)
    place = lax.axis_index("seq")
    bits = jnp.stack([place & 1, (place >> 1) & 1]).astype(jnp.int32)
    mid_part = nt(gate_grad, feed_gate) + nt(up_grad, feed_up)
    mid_part, late_inner = together(mid_part, inner)
    mid_other = swapped(mid_part)
    down_sums = weight_grads(
        bits, down_grad, late_inner, down_grad, late_inner, slice(0, cut), slice(cut, inner.shape[1])
    )
    down_sums, mid_part = together(down_sums, mid_part)
    down_sums = first_swap(down_sums)
    mine = lax.axis_index("head")
    down_part = nn(inner, feed_down)
    down_out = lax.dynamic_slice_in_dim(down_part, (1 - mine) * half, half, 1)
    middle_grad, mixer_grad, feed_gain_grad, mix_grad, gate_low, gain_grad, pull = pl_gate_back(
        mid_part, mid_other, full_grad, middle, feed_gain[None, :], out_weight, mix, gate_proj, gain, reach,
        heads, seqs, count, size,
    )
    grad_feed_gain = jnp.sum(feed_gain_grad, axis=0)
    gate_low = gate_low.reshape(rows, channels)
    pull, late_gate, late_up, late_gated, late_low = together(pull, gate_grad, up_grad, gated, gate_low)
    pulls = from_ahead(pull, hops)
    halves = slice(0, cut), slice(cut, inner.shape[1])
    gate_sums = weight_grads(bits, normed_mid, late_gate, normed_mid, late_gate, *halves)
    out_joined = paired_grads(mixer_grad, late_gated, normed_in, late_low)
    down_sums, gate_sums, out_joined, late_up = together(down_sums, gate_sums, out_joined, late_up)
    if by_bits():
        out_joined = lax.psum_scatter(out_joined, "dp", scatter_dimension=0, tiled=True)
    down_half = list(fold(bits, down_sums))
    down_half[1], late_up = together(down_half[1], late_up)
    up_sums = weight_grads(bits, normed_mid, late_up, normed_mid, late_up, *halves)

    leaving = list(down_half)
    pulls, gate_sums, mix_grad, down_half[1], up_sums = together(pulls, gate_sums, mix_grad, down_half[1], up_sums)
    if relayed(hops):
        pulls = [pulls[0] + lax.ppermute(pulls[1], "seq", [(0, 1)]), pulls[1]]
    leaving[1] = down_half[1]
    down_sums = second_swap(leaving)
    gate_sums = first_swap(gate_sums)
    query_grad, key_grad, value_grad, edge, taps_grad, logit_grad = pl_backward(
        pulls, back_transits, proj, taps, info, beta,
        (query, key, value, inverse, fresh, carry), mix_grad, state, heads, seqs, count, size,
    )
    edge, up_sums = together(edge, up_sums)
    edge = shifted(edge, "seq", -1)
    up_sums = first_swap(up_sums)

    gate_sums, edge, down_sums, query_grad, key_grad, value_grad, logit_grad, taps_grad, down_part, down_out = together(
        gate_sums, edge, down_sums, query_grad, key_grad, value_grad, logit_grad, taps_grad, down_part, down_out
    )
    query_grad, key_grad, value_grad = (
        (grad + jnp.pad(edge[kind], ((0, 0), (count - 8, 0), (0, 0)))).astype(bf16).reshape(rows, channels)
        for kind, grad in enumerate((query_grad, key_grad, value_grad))
    )
    third = channels // 2
    first_grads = jnp.concatenate([query_grad, value_grad[:, :third]], axis=1)
    second_grads = jnp.concatenate([key_grad, value_grad[:, third:]], axis=1)
    mixed_sums = weight_grads(bits, normed_in, first_grads, normed_in, second_grads)
    beta_low = logit_grad.astype(bf16).reshape(rows, heads)
    down_joined = join(bits, down_sums)
    mixed_sums, gate_sums, up_sums, out_joined, down_joined = together(
        mixed_sums, gate_sums, up_sums, out_joined, down_joined
    )
    sums_down = last_sum(down_joined)
    feed_half = fold_two(bits, tuple(gate_sums), tuple(up_sums))
    mixed_sums, feed_half, first_grads, second_grads = together(mixed_sums, feed_half, first_grads, second_grads)
    in_part = pl_input_back(
        (first_grads, second_grads, gate_low, beta_low),
        (query_weight, key_weight, value_weight, gate_weight, beta_weight),
    )
    feed_sums = second_swap(feed_half)
    mixed_sums = first_swap(mixed_sums)
    block_output = own_half(middle, half) + (own_half(down_part, half) + swapped(down_out))
    grad_beta = tn(normed_in, beta_low)
    head_part = jnp.sum(gain_grad, axis=0)
    head_part = head_part + swapped(head_part)
    blocks = lax.axis_size("dp") * lax.axis_size("seq")
    taps_piece = taps_grad.reshape(12 * heads, blocks, size // blocks).transpose(1, 0, 2).reshape(blocks, -1)
    feed_sums, block_output, grad_beta, head_part, taps_piece, in_part = together(
        feed_sums, block_output, grad_beta, head_part, taps_piece, in_part
    )
    feed_joined = join(bits, feed_sums, 2)
    sums_feed = last_sum(feed_joined)
    mixed_sums, sums_down = together(mixed_sums, sums_down, feed_joined)[:2]
    mixed_half = fold(bits, mixed_sums)
    mixed_sums = second_swap(mixed_half)
    mixed_joined = join(bits, mixed_sums)
    mixed_joined, out_joined, in_part, sums_feed = together(mixed_joined, out_joined, in_part, sums_feed)
    sums_mixed = last_sum(mixed_joined)
    input_grad, mixer_gain_grad = pl_input_norm(
        mine[None].astype(jnp.int32), in_part, swapped(in_part), flat_input, middle_grad, mixer_gain[None, :], rows // 64
    )

    out_joined = swap_add(swap_add(out_joined, 0), 1)
    grad_mixer_gain = jnp.sum(mixer_gain_grad, axis=0)

    pieces = [
        grad_mixer_gain.reshape(blocks, -1),
        grad_feed_gain.reshape(blocks, -1),
        grad_beta.reshape(blocks, -1),
        taps_piece,
        head_part.reshape(blocks, -1),
    ]
    small = jnp.concatenate(pieces, axis=1)
    small = jnp.pad(small, ((0, 0), (0, -small.shape[1] % 1024)))
    small = small.reshape(blocks, -1, 128)
    if by_bits():
        small = small_sum(small_sum(small, "dp"), "seq")
    else:
        small = small_sum(small, ("dp", "seq"))
    small = small.reshape(-1)
    if by_bits():
        out_joined = out_joined.reshape(-1, out_joined.shape[-1])
    else:
        out_joined = lax.psum_scatter(out_joined, ("dp", "seq"), scatter_dimension=0, tiled=True)
    cuts, at = [], 0
    for piece in pieces:
        cuts.append(small[at : at + piece.shape[1]])
        at += piece.shape[1]
    shape = (seqs, count, half)
    hidden = feed_gate.shape[1]
    wide = channels + third
    return (
        block_output.reshape(shape),
        input_grad.reshape(shape),
        cuts[0],
        sums_mixed[:, :channels],
        sums_mixed[:, wide : wide + channels],
        jnp.concatenate([sums_mixed[:, channels:wide], sums_mixed[:, wide + channels :]], axis=1),
        out_joined[:, channels:],
        cuts[2].reshape(-1, heads),
        cuts[3].reshape(3, 4, heads, size // blocks),
        cuts[4],
        out_joined[:, :channels].T,
        cuts[1],
        sums_feed[:, :hidden],
        sums_feed[:, hidden:],
        sums_down.T,
    )


def solution(mesh):
    return jax.shard_map(
        local,
        mesh=mesh,
        in_specs=(
            P("dp", "seq", "head"),
            P("dp", "seq"),
            P(),
            P(None, "head"),
            P(None, "head"),
            P(None, "head"),
            P(None, "head"),
            P(None, "head"),
            P(None, None, "head", None),
            P(),
            P("head", None),
            P(),
            P(None, "head"),
            P(None, "head"),
            P("head", None),
            P("dp", "seq", "head"),
        ),
        out_specs=(
            P("dp", "seq", "head"),
            P("dp", "seq", "head"),
            P(("dp", "seq")),
            P(("dp", "seq"), "head"),
            P(("dp", "seq"), "head"),
            P(("dp", "seq"), "head"),
            P(("dp", "seq"), "head"),
            P(("dp", "seq"), "head"),
            P(None, None, "head", ("dp", "seq")),
            P(("dp", "seq")),
            P("head", ("dp", "seq")),
            P(("dp", "seq")),
            P(("dp", "seq"), "head"),
            P(("dp", "seq"), "head"),
            P("head", ("dp", "seq")),
        ),
        check_vma=False,
    )
```

```python
import functools
import math

import jax
import jax.numpy as jnp
from jax import lax
from jax.experimental import pallas as pl
from jax.experimental.pallas import tpu as pltpu
from jax.sharding import PartitionSpec as P

HALO = 16
LONGEST = 512

norm_eps = 1e-05
unit_eps = 1e-06
f32 = jnp.float32
bf16 = jnp.bfloat16
VMEM_LIMIT = 48 * 1024 * 1024


def cost(micros):
    return pl.CostEstimate(flops=int(micros * 1e9), bytes_accessed=1 << 20, transcendentals=0)


def nn(a, b):
    return lax.dot_general(a, b, (((1,), (0,)), ((), ())), preferred_element_type=f32)


def nt(a, b):
    return lax.dot_general(a, b, (((1,), (1,)), ((), ())), preferred_element_type=f32)


def tn(a, b):
    return lax.dot_general(a, b, (((0,), (0,)), ((), ())), preferred_element_type=f32)


def split(value):
    high = value.astype(bf16)
    return high, (value - high.astype(f32)).astype(bf16)


def nn3(a, b):
    a_high, a_low = a
    b_high, b_low = b
    return nn(a_high, b_high) + nn(a_high, b_low) + nn(a_low, b_high)


def sigmoid(value):
    return 1.0 / (1.0 + jnp.exp(-value))


def rms_scale(values):
    return lax.rsqrt(jnp.mean(values * values, axis=-1, keepdims=True) + norm_eps)


def norm_back(grad_rows, normed, row_scale, gain_vec):
    grad_hat = grad_rows * gain_vec
    return row_scale * (grad_hat - normed * jnp.mean(grad_hat * normed, axis=-1, keepdims=True))


def grid_of(size):
    row = lax.broadcasted_iota(jnp.int32, (size, size), 0)
    return row, lax.broadcasted_iota(jnp.int32, (size, size), 1)


def unit_inverses(lowers, size):
    row, col = grid_of(size)
    apart = row ^ col
    eye = jnp.where(apart == 0, 1.0, 0.0)
    inverses = [eye - jnp.where(apart == 1, lower, 0.0) for lower in lowers]
    lows = [lower.astype(bf16) for lower in lowers]
    level = 1
    while (1 << level) < size:
        here = (apart >> level) == 1
        rounded = [inverse.astype(bf16) for inverse in inverses]
        right = [nn(jnp.where(here, low, 0.0), near).astype(bf16) for low, near in zip(lows, rounded)]
        inverses = [inverse - nn(near, far) for inverse, near, far in zip(inverses, rounded, right)]
        level += 1
    parts = [split(inverse) for inverse in inverses]
    wholes = [split(lower) for lower in lowers]
    left = [
        (eye - inverse - nn3(whole, part)).astype(bf16)
        for inverse, whole, part in zip(inverses, wholes, parts)
    ]
    return [inverse + nn(part[0], rest) for inverse, part, rest in zip(inverses, parts, left)]


def conv_taps(proj, seq, taps, kind, info, count, lanes=slice(None)):
    rows = []
    for tap in range(4):
        moved = proj[seq, HALO - 3 + tap : HALO - 3 + tap + count, lanes]
        rows.append(moved if tap == 3 else moved * info[:, tap : tap + 1])
    mixed = rows[0] * taps[kind, 0:1, lanes]
    for tap in range(1, 4):
        mixed = mixed + rows[tap] * taps[kind, tap : tap + 1, lanes]
    return rows, mixed


def turned(info, seq):
    row, col = grid_of(8)
    return tn(info[seq].astype(bf16), jnp.where(row == col, 1.0, 0.0).astype(bf16))


def head_column(table, seq, head):
    lane = lax.broadcasted_iota(jnp.int32, table.shape[1:], 1)
    return jnp.sum(jnp.where(lane == head, table[seq], 0.0), axis=1, keepdims=True)


def forward_kernel(
    seqs, count, size, group,
    query_in, key_in, value_in, taps, info, beta,
    query_out, key_out, value_out, inverse_out, fresh_out, carry_out, local_out, reach_out, state_out, transit_out, both_out,
):
    row, col = grid_of(count)
    scale = 1.0 / math.sqrt(size)
    infos = [turned(info, seq) for seq in range(seqs)]
    sames = [infos[seq][:, 5:6] == info[seq, 5:6, :] for seq in range(seqs)]
    every = [(seq, part, slice(part * size, (part + 1) * size)) for part in range(group) for seq in range(seqs)]
    queries, keys, lowers, betas = [], [], [], []
    for seq, part, lanes in every:
        parts = []
        for kind, proj in enumerate((query_in, key_in, value_in)):
            mixed = conv_taps(proj, seq, taps, kind, infos[seq], count, lanes)[1]
            parts.append(mixed * sigmoid(mixed))
        query, key, value = parts
        query = query * (lax.rsqrt(jnp.sum(query * query, axis=1, keepdims=True) + unit_eps) * scale)
        key = key * lax.rsqrt(jnp.sum(key * key, axis=1, keepdims=True) + unit_eps)
        query, key, value = query.astype(bf16), key.astype(bf16), value.astype(bf16)
        query_out[seq, :, lanes], key_out[seq, :, lanes], value_out[seq, :, lanes] = query, key, value
        beta_col = head_column(beta, seq, pl.program_id(0) * group + part)
        queries.append(query)
        keys.append(key)
        betas.append(beta_col)
        lowers.append(jnp.where(sames[seq] & (row > col), nt(key, key) * beta_col, 0.0))
    inverses = unit_inverses(lowers, count)
    for (seq, part, lanes), query, key, beta_col, inverse in zip(every, queries, keys, betas, inverses):
        enter, last = infos[seq][:, 3:4], infos[seq][:, 4:5]
        key_full = key.astype(f32)
        inverse_parts = split(inverse)
        inverse_out[part, seq] = inverse_parts[0]
        right = jnp.concatenate(
            [key_full * (beta_col * enter), value_out[seq, :, lanes].astype(f32) * beta_col], axis=1
        )
        solved = nn3(inverse_parts, split(right))
        solved_high, solved_low = split(solved)
        key_last = (key_full * last).astype(bf16)
        ends = tn(key_last, solved_high) + tn(key_last, solved_low)
        transit_row, transit_col = grid_of(size)
        eye = jnp.where(transit_row == transit_col, 1.0, 0.0)
        transit = eye * info[seq, 3:4, count - 1 :] - ends[:, :size]
        state_out[seq, part] = ends[:, size:]
        transit_out[seq, part] = transit
        both_out[seq, part, 0] = ends[:, size:]
        both_out[seq, part, 1] = transit
        attend = jnp.where(sames[seq] & (row >= col), nt(query, key), 0.0).astype(bf16)
        reads = nn(attend, solved_high)
        local_out[seq, :, lanes] = reads[:, size:]
        reach_out[seq, :, lanes] = (query.astype(f32) * enter - reads[:, :size]).astype(bf16)
        carry_out[seq, :, lanes] = solved_high[:, :size]
        fresh_out[seq, :, lanes] = solved[:, size:]


def pl_forward(proj, taps, info, beta, group, heads, seqs, count, size, channels):
    def rows(dtype):
        return jax.ShapeDtypeStruct((seqs, count, heads * size), dtype)

    row_spec = pl.BlockSpec((seqs, count, group * size), lambda h: (0, 0, h))
    proj_spec = pl.BlockSpec((seqs, count + HALO, group * size), lambda h: (0, 0, h))
    state = jax.ShapeDtypeStruct((seqs, heads, size, size), f32)
    state_spec = pl.BlockSpec((seqs, group, size, size), lambda h: (0, h, 0, 0))
    return pl.pallas_call(
        functools.partial(forward_kernel, seqs, count, size, group),
        grid=(heads // group,),
        in_specs=[proj_spec] * 3
        + [
            pl.BlockSpec((3, 4, group * size), lambda h: (0, 0, h)),
            pl.BlockSpec(info.shape, lambda h: (0, 0, 0)),
            pl.BlockSpec(beta.shape, lambda h: (0, 0, 0)),
        ],
        out_specs=[row_spec] * 3
        + [pl.BlockSpec((group, seqs, count, count), lambda h: (h, 0, 0, 0))]
        + [row_spec] * 4
        + [state_spec] * 2
        + [pl.BlockSpec((seqs, group, 2, size, size), lambda h: (0, h, 0, 0, 0))],
        out_shape=[rows(bf16)] * 3
        + [jax.ShapeDtypeStruct((heads, seqs, count, count), bf16)]
        + [rows(f32), rows(bf16), rows(f32), rows(bf16)]
        + [state] * 2
        + [jax.ShapeDtypeStruct((seqs, heads, 2, size, size), f32)],
        compiler_params=pltpu.CompilerParams(vmem_limit_bytes=VMEM_LIMIT),
        cost_estimate=cost(17),
    )(*proj, taps, info, beta)


def arrived(boths, farthest, seq):
    total = farthest[seq, 0]
    for both in boths[::-1]:
        total = both[seq, 0, 0] + nn3(split(both[seq, 0, 1]), split(total))
    return total


def read_kernel(seqs, count, size, heads, hops, *refs):
    boths, farthest = refs[: hops - 1], refs[hops - 1]
    local, reach, gate, gain, out_weight, state_out, mix_out, gated_out, part_out, held = refs[hops:]
    head = pl.program_id(0)
    for seq in range(seqs):
        state = arrived(boths, farthest, seq)
        state_out[seq, 0] = state
        state_high, state_low = split(state)
        moved = reach[seq]
        mix = local[seq] + nn(moved, state_high) + nn(moved, state_low)
        mix_out[seq] = mix
        gate_now = gate[seq]
        gated = (mix * rms_scale(mix) * gain[...] * (gate_now * sigmoid(gate_now))).astype(bf16)
        gated_out[seq] = gated
        held[head, seq * count : (seq + 1) * count, :] = gated

    @pl.when(head == heads - 1)
    def _():
        rows = jnp.concatenate([held[h] for h in range(heads)], axis=1)
        part_out[...] = nn(rows, out_weight[...])


def pl_read(boths, farthest, local, reach, gate, gain, out_weight, heads, seqs, count, size, width):
    row_spec = pl.BlockSpec((seqs, count, size), lambda h: (0, 0, h))
    state_spec = pl.BlockSpec((seqs, 1, size, size), lambda h: (0, h, 0, 0))
    both_spec = pl.BlockSpec((seqs, 1, 2, size, size), lambda h: (0, h, 0, 0, 0))
    hops = len(boths) + 1
    return pl.pallas_call(
        functools.partial(read_kernel, seqs, count, size, heads, hops),
        grid=(heads,),
        in_specs=[both_spec] * (hops - 1)
        + [state_spec]
        + [row_spec] * 3
        + [pl.BlockSpec((1, size), lambda h: (0, 0)), pl.BlockSpec((heads * size, width), lambda h: (0, 0))],
        out_specs=[state_spec, row_spec, row_spec, pl.BlockSpec((seqs * count, width), lambda h: (0, 0))],
        out_shape=[
            jax.ShapeDtypeStruct((seqs, heads, size, size), f32),
            jax.ShapeDtypeStruct((seqs, count, heads * size), f32),
            jax.ShapeDtypeStruct((seqs, count, heads * size), bf16),
            jax.ShapeDtypeStruct((seqs * count, width), f32),
        ],
        scratch_shapes=[pltpu.VMEM((heads, seqs * count, size), bf16)],
        compiler_params=pltpu.CompilerParams(vmem_limit_bytes=VMEM_LIMIT),
        cost_estimate=cost(7),
    )(*boths, farthest, local, reach, gate, gain, out_weight)


def hidden_back_kernel(gate_grad, up_grad, feed_gate, feed_up, out):
    out[...] = nt(gate_grad[...], feed_gate[...]) + nt(up_grad[...], feed_up[...])


def pl_hidden_back(gate_grad, up_grad, feed_gate, feed_up):
    rows, hidden = gate_grad.shape
    width = feed_gate.shape[0]
    step = width // 4
    whole = pl.BlockSpec((rows, hidden), lambda i: (0, 0))
    weight = pl.BlockSpec((step, hidden), lambda i: (i, 0))
    return pl.pallas_call(
        hidden_back_kernel,
        grid=(4,),
        in_specs=[whole, whole, weight, weight],
        out_specs=pl.BlockSpec((rows, step), lambda i: (0, i)),
        out_shape=jax.ShapeDtypeStruct((rows, width), f32),
        compiler_params=pltpu.CompilerParams(vmem_limit_bytes=VMEM_LIMIT),
        cost_estimate=cost(6),
    )(gate_grad, up_grad, feed_gate, feed_up)


def gate_back_kernel(
    seqs, count, size,
    mid_part, mid_other, full_grad, middle, feed_gain, out_weight, mix, gate, gain, reach,
    middle_grad, mixer_grad, feed_gain_grad, mix_grad, gate_grad, gain_grad, pull,
):
    head = pl.program_id(0)

    @pl.when(head == 0)
    def _():
        gain_grad[...] = jnp.zeros_like(gain_grad)
        feed_gain_grad[...] = jnp.zeros_like(feed_gain_grad)
        tall = 64

        def some_rows(index, carried):
            here = pl.ds(pl.multiple_of(index * tall, tall), tall)
            mid_grad = mid_part[here, :] + mid_other[here, :]
            scale = rms_scale(middle[here, :])
            normed = middle[here, :] * scale
            feed_gain_grad[...] += jnp.sum((mid_grad * normed).reshape(tall // 8, 8, normed.shape[1]), axis=0)
            whole = full_grad[here, :] + norm_back(mid_grad, normed, scale, feed_gain[...])
            middle_grad[here, :] = whole
            mixer_grad[here, :] = whole.astype(bf16)
            return carried

        lax.fori_loop(0, seqs * count // tall, some_rows, 0)

    grads = nt(mixer_grad[...], out_weight[...])
    for seq in range(seqs):
        grad = grads[seq * count : (seq + 1) * count]
        mix_now, gate_now = mix[seq], gate[seq]
        scale = rms_scale(mix_now)
        normed = mix_now * scale
        sig = sigmoid(gate_now)
        gate_silu = gate_now * sig
        with_norm = grad * normed
        gain_grad[...] += jnp.sum((with_norm * gate_silu).reshape(count // 8, 8, size), axis=0)
        gate_grad[seq] = (with_norm * gain[...] * (sig * (1.0 + gate_now * (1.0 - sig)))).astype(bf16)
        normed_grad = grad * gain[...] * gate_silu
        mix_grad_now = scale * (normed_grad - normed * jnp.mean(normed_grad * normed, axis=1, keepdims=True))
        low = mix_grad_now.astype(bf16)
        mix_grad[seq] = low
        pull[seq, 0] = tn(reach[seq], low)


def pl_gate_back(
    mid_part, mid_other, full_grad, middle, feed_gain, out_weight, mix, gate, gain, reach, heads, seqs, count, size
):
    rows, width = middle.shape
    row_spec = pl.BlockSpec((seqs, count, size), lambda h: (0, 0, h))

    def fixed(*dims):
        return pl.BlockSpec(dims, lambda h: (0,) * len(dims))

    return pl.pallas_call(
        functools.partial(gate_back_kernel, seqs, count, size),
        grid=(heads,),
        in_specs=[fixed(rows, width)] * 4
        + [
            fixed(1, width),
            pl.BlockSpec((size, width), lambda h: (h, 0)),
            row_spec,
            row_spec,
            fixed(1, size),
            row_spec,
        ],
        out_specs=[
            fixed(rows, width),
            fixed(rows, width),
            fixed(8, width),
            row_spec,
            row_spec,
            fixed(8, size),
            pl.BlockSpec((seqs, 1, size, size), lambda h: (0, h, 0, 0)),
        ],
        out_shape=[
            jax.ShapeDtypeStruct((rows, width), f32),
            jax.ShapeDtypeStruct((rows, width), bf16),
            jax.ShapeDtypeStruct((8, width), f32),
            jax.ShapeDtypeStruct((seqs, count, heads * size), bf16),
            jax.ShapeDtypeStruct((seqs, count, heads * size), bf16),
            jax.ShapeDtypeStruct((8, size), f32),
            jax.ShapeDtypeStruct((seqs, heads, size, size), f32),
        ],
        compiler_params=pltpu.CompilerParams(vmem_limit_bytes=VMEM_LIMIT),
        cost_estimate=cost(9),
    )(mid_part, mid_other, full_grad, middle, feed_gain, out_weight, mix, gate, gain, reach)


def backward_kernel(seqs, count, size, hops, *refs):
    pulls, transits = refs[:hops], refs[hops : 2 * hops - 1]
    (
        query_in, key_in, value_in, taps, info_rows, beta,
        query_ref, key_ref, value_ref, inverse_ref, fresh_ref, carry_ref, mix_grad_ref, state_ref,
        query_grad_out, key_grad_out, value_grad_out, edge_out, taps_grad_out, logit_grad_out,
    ) = refs[2 * hops - 1 :]
    head = pl.program_id(0)
    row, col = grid_of(count)
    scale = 1.0 / math.sqrt(size)

    @pl.when(head == 0)
    def _():
        logit_grad_out[...] = jnp.zeros_like(logit_grad_out)

    taps_totals = None
    for seq in range(seqs):
        total = pulls[-1][seq, 0]
        for pull, transit in zip(pulls[-2::-1], transits[::-1]):
            transit_high, transit_low = split(transit[seq, 0])
            total_high, total_low = split(total)
            total = pull[seq, 0] + (
                tn(transit_high, total_high) + tn(transit_high, total_low) + tn(transit_low, total_high)
            )
        out_state_grad = total.astype(bf16)
        state = state_ref[seq, 0].astype(bf16)
        query, key, value = query_ref[seq], key_ref[seq], value_ref[seq]
        mix_grad = mix_grad_ref[seq]
        info = turned(info_rows, seq)
        enter, last = info[:, 3:4], info[:, 4:5]
        same = info[:, 5:6] == info_rows[seq, 5:6, :]
        causal = same & (row >= col)
        strict = same & (row > col)
        beta_col = head_column(beta, seq, head)
        key_full = key.astype(f32)
        key_last = (key_full * last).astype(bf16)
        update = (fresh_ref[seq] - nn(carry_ref[seq], state)).astype(bf16)
        attend = jnp.where(causal, nt(query, key), 0.0).astype(bf16)
        update_grad = tn(attend, mix_grad) + nn(key_last, out_state_grad)
        right_grad = tn(inverse_ref[0, seq], update_grad.astype(bf16))
        right_low = right_grad.astype(bf16)
        both = nt(jnp.concatenate([mix_grad, right_low], axis=0), update)
        attend_grad = jnp.where(causal, both[:count], 0.0).astype(bf16)
        lower_grad = jnp.where(strict, -both[count:], 0.0)
        gram = nt(key, key)
        surprise = value.astype(f32) - enter * nn(key, state)
        beta_grad = jnp.sum(right_grad * surprise, axis=1, keepdims=True) + jnp.sum(
            lower_grad * gram, axis=1, keepdims=True
        )
        logit_grad = beta_grad * beta_col * (1.0 - beta_col)
        lane = lax.broadcasted_iota(jnp.int32, logit_grad_out.shape[1:], 1)
        logit_grad_out[seq] += jnp.where(lane == head, logit_grad, 0.0)
        value_grad = right_grad * beta_col
        gram_grad = (lower_grad * beta_col).astype(bf16)
        stacked = jnp.concatenate([gram_grad, attend_grad], axis=0)
        forth = nn(stacked, key)
        back = tn(stacked, jnp.concatenate([key, query], axis=0))
        through = nt(
            jnp.concatenate([(value_grad * enter).astype(bf16), mix_grad], axis=0), state
        )
        key_grad = forth[:count] + back - through[:count] + last * nt(update, out_state_grad)
        query_grad = forth[count:] + enter * through[count:]
        for kind, (proj, grad, out) in enumerate(
            (
                (query_in, query_grad, query_grad_out),
                (key_in, key_grad, key_grad_out),
                (value_in, value_grad, value_grad_out),
            )
        ):
            rows, mixed = conv_taps(proj, seq, taps, kind, info, count)
            sig = sigmoid(mixed)
            if kind < 2:
                active = mixed * sig
                norm = lax.rsqrt(jnp.sum(active * active, axis=1, keepdims=True) + unit_eps)
                unit = active * norm
                grad = grad - unit * jnp.sum(grad * unit, axis=1, keepdims=True)
                grad = grad * (norm * scale if kind == 0 else norm)
            mixed_grad = grad * (sig * (1.0 + mixed * (1.0 - sig)))
            sums = [jnp.sum((mixed_grad * rows[tap]).reshape(count // 8, 8, size), axis=0) for tap in range(4)]
            blank = jnp.zeros((8, size), f32)
            proj_grad = mixed_grad * taps[kind, 3:4, :]
            edge = blank
            for tap in range(3):
                delay = 3 - tap
                masked = mixed_grad * (info[:, tap : tap + 1] * taps[kind, tap : tap + 1, :])
                moved = pltpu.roll(masked, count - delay, 0)
                at = lax.broadcasted_iota(jnp.int32, (count, size), 0)
                proj_grad = proj_grad + jnp.where(at < count - delay, moved, 0.0)
                first = pltpu.roll(masked[:8], 8 - delay, 0)
                at_edge = lax.broadcasted_iota(jnp.int32, (8, size), 0)
                edge = edge + jnp.where(at_edge >= 8 - delay, first, 0.0)
            out[seq] = proj_grad
            edge_out[kind, seq] = edge
            sums = jnp.stack([jnp.sum(part, axis=0) for part in sums])
            if seq == 0:
                taps_grad_out[kind] = sums
            else:
                taps_grad_out[kind] += sums


def pl_backward(pulls, transits, proj, taps, info, beta, saved, mix_grad, state, heads, seqs, count, size):
    hops = len(pulls)
    row_spec = pl.BlockSpec((seqs, count, size), lambda h: (0, 0, h))
    state_spec = pl.BlockSpec((seqs, 1, size, size), lambda h: (0, h, 0, 0))
    proj_spec = pl.BlockSpec((seqs, count + HALO, size), lambda h: (0, 0, h))
    return pl.pallas_call(
        functools.partial(backward_kernel, seqs, count, size, hops),
        grid=(heads,),
        in_specs=[state_spec] * (2 * hops - 1)
        + [proj_spec] * 3
        + [
            pl.BlockSpec((3, 4, size), lambda h: (0, 0, h)),
            pl.BlockSpec(info.shape, lambda h: (0, 0, 0)),
            pl.BlockSpec(beta.shape, lambda h: (0, 0, 0)),
        ]
        + [row_spec] * 3
        + [pl.BlockSpec((1, seqs, count, count), lambda h: (h, 0, 0, 0))]
        + [row_spec] * 3
        + [state_spec],
        out_specs=[row_spec] * 3
        + [
            pl.BlockSpec((3, seqs, 8, size), lambda h: (0, 0, 0, h)),
            pl.BlockSpec((3, 4, size), lambda h: (0, 0, h)),
            pl.BlockSpec((seqs, count, heads), lambda h: (0, 0, 0)),
        ],
        out_shape=[jax.ShapeDtypeStruct((seqs, count, heads * size), f32)] * 3
        + [
            jax.ShapeDtypeStruct((3, seqs, 8, heads * size), f32),
            jax.ShapeDtypeStruct((3, 4, heads * size), f32),
            jax.ShapeDtypeStruct((seqs, count, heads), f32),
        ],
        compiler_params=pltpu.CompilerParams(vmem_limit_bytes=VMEM_LIMIT),
        cost_estimate=cost(17),
    )(*pulls, *transits, *proj, taps, info, beta, *saved, mix_grad, state)


def input_back_kernel(first, second, gate_grad, beta_grad, query_w, key_w, value_w, gate_w, beta_w, out):
    channels = query_w.shape[1]
    third = channels // 2
    out[...] = (
        nt(first[:, :channels], query_w[...])
        + nt(second[:, :channels], key_w[...])
        + nt(first[:, channels:], value_w[:, :third])
        + nt(second[:, channels:], value_w[:, third:])
        + nt(gate_grad[...], gate_w[...])
        + nt(beta_grad[...], beta_w[...])
    )


def pl_input_back(grads, weights):
    rows = grads[0].shape[0]
    width = weights[0].shape[0]
    step = width // 4
    return pl.pallas_call(
        input_back_kernel,
        grid=(4,),
        in_specs=[pl.BlockSpec(grad.shape, lambda i: (0, 0)) for grad in grads]
        + [pl.BlockSpec((step, weight.shape[1]), lambda i: (i, 0)) for weight in weights],
        out_specs=pl.BlockSpec((rows, step), lambda i: (0, i)),
        out_shape=jax.ShapeDtypeStruct((rows, width), f32),
        compiler_params=pltpu.CompilerParams(vmem_limit_bytes=VMEM_LIMIT),
        cost_estimate=cost(1),
    )(*grads, *weights)


def input_norm_kernel(which, part, other, value, middle_grad, gain, out, gain_grad):
    grad = part[...] + other[...]
    scale = rms_scale(value[...])
    normed = value[...] * scale
    share = jnp.sum((grad * normed).reshape(grad.shape[0] // 8, 8, grad.shape[1]), axis=0)

    @pl.when(pl.program_id(0) == 0)
    def _():
        gain_grad[...] = share

    @pl.when(pl.program_id(0) > 0)
    def _():
        gain_grad[...] += share

    result = middle_grad[...] + norm_back(grad, normed, scale, gain[...])
    half = out.shape[1]
    out[...] = jnp.where(which[0] == 0, result[:, :half], result[:, half:])


def pl_input_norm(which, part, other, value, middle_grad, gain, steps):
    rows, width = value.shape
    tall = pl.BlockSpec((rows // steps, width), lambda i, which: (i, 0))
    return pl.pallas_call(
        input_norm_kernel,
        grid_spec=pltpu.PrefetchScalarGridSpec(
            num_scalar_prefetch=1,
            grid=(steps,),
            in_specs=[tall] * 4 + [pl.BlockSpec((1, width), lambda i, which: (0, 0))],
            out_specs=[
                pl.BlockSpec((rows // steps, width // 2), lambda i, which: (i, 0)),
                pl.BlockSpec((8, width), lambda i, which: (0, 0)),
            ],
        ),
        out_shape=[jax.ShapeDtypeStruct((rows, width // 2), f32), jax.ShapeDtypeStruct((8, width), f32)],
        compiler_params=pltpu.CompilerParams(vmem_limit_bytes=VMEM_LIMIT),
        cost_estimate=cost(1),
    )(which, part, other, value, middle_grad, gain)


def shifted(value, axis, steps):
    count = lax.axis_size(axis)
    initial, last = (max(0, -steps), min(count, count - steps))
    return lax.ppermute(value, axis, [(source, source + steps) for source in range(initial, last)])


def from_ahead(value, hops):
    if not relayed(hops):
        return [shifted(value, "seq", -hop) for hop in range(1, hops + 1)]
    return [lax.ppermute(value, "seq", pairs) for pairs in ([(1, 0), (3, 2)], [(2, 0), (3, 1)])]


def relayed(hops):
    return by_bits() and hops == 2


def swapped(value):
    return lax.ppermute(value, "head", [(0, 1), (1, 0)])


def in_order(own, other, axis):
    mine = lax.axis_index("head") == 0
    return jnp.where(
        mine, jnp.concatenate([own, other], axis=axis), jnp.concatenate([other, own], axis=axis)
    )


def own_half(value, half):
    return lax.dynamic_slice_in_dim(value, lax.axis_index("head") * half, half, value.ndim - 1)


def pick(value, index, axis):
    return lax.dynamic_index_in_dim(value, index, axis, keepdims=False)


def together(*values):
    return lax.optimization_barrier(values)


def weight_kernel(block, first_window, second_window, bits, first_left, first_right, second_left, second_right, *refs):
    first_leaves, first_stays, second_leaves, second_stays, held, held_second = refs
    low, high = bits[0], bits[1]
    held[...] = tn(first_left[...], first_right[:, first_window])
    for part in range(2):
        base = part * 2 * block
        first_leaves[0, part] = held[pl.ds(pl.multiple_of(base + (1 - low) * block, 8), block), :]
        first_stays[0, part] = held[pl.ds(pl.multiple_of(base + low * block, 8), block), :]
    held_second[...] = tn(second_left[...], second_right[:, second_window])
    second_leaves[0] = held_second[pl.ds(pl.multiple_of((1 - high) * 2 * block, 8), 2 * block), :]
    second_stays[0] = held_second[pl.ds(pl.multiple_of(high * 2 * block, 8), 2 * block), :]


def fold_kernel(block, bits, first_stays, first_comes, second_stays, second_comes, *refs):
    first_leaves, first_keeps, second_leaves, second_keeps = refs
    low, high = bits[0], bits[1]
    first_leaves[0] = first_stays[0, 1 - high] + first_comes[0, 1 - high]
    first_keeps[0] = first_stays[0, high] + first_comes[0, high]
    away = pl.ds(pl.multiple_of((1 - low) * block, 8), block)
    here = pl.ds(pl.multiple_of(low * block, 8), block)
    second_leaves[0] = second_stays[0, away] + second_comes[0, away]
    second_keeps[0] = second_stays[0, here] + second_comes[0, here]


def join_kernel(pieces, bits, first_keeps, first_comes, second_keeps, second_comes, out):
    first, second = first_keeps.shape[-1] // pieces, second_keeps.shape[-1] // pieces
    at = 0
    for piece in range(pieces):
        lanes = slice(piece * first, (piece + 1) * first)
        out[:, at : at + first] = first_keeps[0, :, lanes] + first_comes[0, :, lanes]
        at += first
        lanes = slice(piece * second, (piece + 1) * second)
        out[:, at : at + second] = second_keeps[0, :, lanes] + second_comes[0, :, lanes]
        at += second


def per_block(kernel, bits, steps, args, in_specs, out_specs, out_shape, scratch=()):
    return pl.pallas_call(
        kernel,
        grid_spec=pltpu.PrefetchScalarGridSpec(
            num_scalar_prefetch=1, grid=(steps,), in_specs=in_specs, out_specs=out_specs, scratch_shapes=list(scratch)
        ),
        out_shape=out_shape,
        compiler_params=pltpu.CompilerParams(vmem_limit_bytes=VMEM_LIMIT),
        cost_estimate=cost(1),
    )(bits, *args)


def four_block(dims):
    return pl.BlockSpec((1,) + dims, lambda z, bits: (z,) + (0,) * len(dims))


def swap_bit(value, bit):
    return lax.ppermute(value, "seq", [(source, source ^ (1 << bit)) for source in range(4)])


def by_bits():
    return lax.axis_size("seq") == 4


def weight_grads(bits, first_left, first_right, second_left, second_right, first_window=None, second_window=None):
    first_window = first_window or slice(0, first_right.shape[1])
    second_window = second_window or slice(0, second_right.shape[1])
    if not by_bits():
        return tn(first_left, first_right[:, first_window]), tn(second_left, second_right[:, second_window])
    dp = lax.axis_size("dp")
    tokens, rows = first_left.shape
    first_cols = first_window.stop - first_window.start
    second_cols = second_window.stop - second_window.start
    block = rows // (4 * dp)
    left_spec = pl.BlockSpec((tokens, 4 * block), lambda z, bits: (0, z))

    def whole(cols):
        return pl.BlockSpec((tokens, cols), lambda z, bits: (0, 0))

    first, second = (2, block, first_cols), (2 * block, second_cols)
    return per_block(
        functools.partial(weight_kernel, block, first_window, second_window),
        bits,
        dp,
        (first_left, first_right, second_left, second_right),
        [left_spec, whole(first_right.shape[1]), left_spec, whole(second_right.shape[1])],
        [four_block(dims) for dims in (first, first, second, second)],
        [jax.ShapeDtypeStruct((dp,) + dims, f32) for dims in (first, first, second, second)],
        [pltpu.VMEM((4 * block, first_cols), f32), pltpu.VMEM((4 * block, second_cols), f32)],
    )


def paired_kernel(first_left, first_right, second_left, second_right, out):
    cut = first_right.shape[1]
    out[:, :cut] = tn(first_left[...], first_right[...])
    out[:, cut:] = tn(second_left[...], second_right[...])


def paired_grads(first_left, first_right, second_left, second_right):
    tokens, rows = first_left.shape
    cols = first_right.shape[1] + second_right.shape[1]
    step = rows // 4
    left_spec = pl.BlockSpec((tokens, step), lambda i: (0, i))
    whole = [pl.BlockSpec(right.shape, lambda i: (0, 0)) for right in (first_right, second_right)]
    return pl.pallas_call(
        paired_kernel,
        grid=(4,),
        in_specs=[left_spec, whole[0], left_spec, whole[1]],
        out_specs=pl.BlockSpec((step, cols), lambda i: (i, 0)),
        out_shape=jax.ShapeDtypeStruct((rows, cols), f32),
        compiler_params=pltpu.CompilerParams(vmem_limit_bytes=VMEM_LIMIT),
        cost_estimate=cost(4),
    )(first_left, first_right, second_left, second_right)


def first_swap(parts):
    if not by_bits():
        return parts
    first_leaves, first_stays, second_leaves, second_stays = parts
    return first_stays, swap_bit(first_leaves, 0), second_stays, swap_bit(second_leaves, 1)


def fold(bits, parts):
    if not by_bits():
        return parts
    dp = lax.axis_size("dp")
    block, first_cols, second_cols = parts[0].shape[2], parts[0].shape[3], parts[2].shape[2]
    ins = [(2, block, first_cols)] * 2 + [(2 * block, second_cols)] * 2
    outs = [(block, first_cols)] * 2 + [(block, second_cols)] * 2
    return per_block(
        functools.partial(fold_kernel, block),
        bits,
        dp,
        parts,
        [four_block(dims) for dims in ins],
        [four_block(dims) for dims in outs],
        [jax.ShapeDtypeStruct((dp,) + dims, f32) for dims in outs],
    )


def fold_two_kernel(block, bits, *refs):
    low, high = bits[0], bits[1]
    first_leaves, first_keeps, second_leaves, second_keeps = refs[8:]
    away = pl.ds(pl.multiple_of((1 - low) * block, 8), block)
    here = pl.ds(pl.multiple_of(low * block, 8), block)
    first_at = second_at = 0
    for first_stays, first_comes, second_stays, second_comes in (refs[:4], refs[4:8]):
        lanes = slice(first_at, first_at + first_stays.shape[-1])
        first_leaves[0, :, lanes] = first_stays[0, 1 - high] + first_comes[0, 1 - high]
        first_keeps[0, :, lanes] = first_stays[0, high] + first_comes[0, high]
        first_at = lanes.stop
        lanes = slice(second_at, second_at + second_stays.shape[-1])
        second_leaves[0, :, lanes] = second_stays[0, away] + second_comes[0, away]
        second_keeps[0, :, lanes] = second_stays[0, here] + second_comes[0, here]
        second_at = lanes.stop


def fold_two(bits, one, two):
    if not by_bits():
        return one + two
    dp = lax.axis_size("dp")
    block = one[0].shape[2]
    ins, outs = [], [0, 0]
    for part in (one, two):
        first_cols, second_cols = part[0].shape[3], part[2].shape[2]
        ins += [(2, block, first_cols)] * 2 + [(2 * block, second_cols)] * 2
        outs = [outs[0] + first_cols, outs[1] + second_cols]
    outs = [(block, outs[0])] * 2 + [(block, outs[1])] * 2
    return per_block(
        functools.partial(fold_two_kernel, block),
        bits,
        dp,
        tuple(one) + tuple(two),
        [four_block(dims) for dims in ins],
        [four_block(dims) for dims in outs],
        [jax.ShapeDtypeStruct((dp,) + dims, f32) for dims in outs],
    )


def second_swap(parts):
    if not by_bits():
        return parts
    first_leaves, first_keeps, second_leaves, second_keeps = parts
    return first_keeps, swap_bit(first_leaves, 1), second_keeps, swap_bit(second_leaves, 0)


def join(bits, parts, pieces=1):
    if not by_bits():
        return tuple(
            lax.psum_scatter(part, ("dp", "seq"), scatter_dimension=0, tiled=True) for part in parts
        )
    dp = lax.axis_size("dp")
    block, first_cols, second_cols = parts[0].shape[1], parts[0].shape[2], parts[2].shape[2]
    return per_block(
        functools.partial(join_kernel, pieces),
        bits,
        dp,
        parts,
        [four_block((block, cols)) for cols in (first_cols, first_cols, second_cols, second_cols)],
        pl.BlockSpec((block, first_cols + second_cols), lambda z, bits: (z, 0)),
        jax.ShapeDtypeStruct((dp * block, first_cols + second_cols), f32),
    )


def last_sum(joined):
    if not by_bits():
        return jnp.concatenate(joined, axis=1)
    return lax.psum_scatter(joined, "dp", scatter_dimension=0, tiled=True)


def swap_add(value, bit):
    if not by_bits():
        return value
    value = value.reshape(2 - bit, 2, -1, value.shape[-1])
    mine = (lax.axis_index("seq") >> bit) & 1
    return pick(value, mine, 1) + swap_bit(pick(value, 1 - mine, 1), bit)


def small_sum(value, names):
    if not by_bits():
        return lax.psum_scatter(value, names, scatter_dimension=0, tiled=True)
    if names == "dp" and lax.axis_size("dp") != 4:
        return lax.psum_scatter(value, "dp", scatter_dimension=0, tiled=True)
    value = value.reshape((2, 2) + (value.shape[0] // 4,) + value.shape[1:])
    for bit in range(2):
        mine = (lax.axis_index(names) >> bit) & 1
        perm = [(source, source ^ (1 << bit)) for source in range(4)]
        value = pick(value, mine, 1 - bit) + lax.ppermute(pick(value, 1 - mine, 1 - bit), names, perm)
    return value


def local(
    block_input,
    segment_ids,
    mixer_gain,
    query_weight,
    key_weight,
    value_weight,
    gate_weight,
    beta_weight,
    conv_weight,
    head_gain,
    out_weight,
    feed_gain,
    feed_gate,
    feed_up,
    feed_down,
    grad_output,
):
    seqs, count, half = block_input.shape
    rows = seqs * count
    size = head_gain.shape[0]
    heads = beta_weight.shape[1]
    channels = heads * size
    width = query_weight.shape[0]
    hops = -(-(LONGEST - 1) // count)
    hops = min(hops, lax.axis_size("seq") - 1)

    other_input = swapped(block_input)
    segments = segment_ids.astype(f32)
    before = shifted(
        jnp.concatenate([block_input[:, count - 3 :], segments[:, count - 3 :, None]], axis=2), "seq", 1
    )
    edge_ids = before[:, :, half]
    before = before[:, :, :half]
    other_before = swapped(before)
    full_input = in_order(block_input, other_input, 2)
    full_before = in_order(before, other_before, 2)
    other_grad = swapped(grad_output)

    extended = jnp.concatenate(
        [jnp.zeros((seqs, HALO - 3, width), f32), full_before, full_input], axis=1
    )
    extended_low = (extended * rms_scale(extended) * mixer_gain).astype(bf16)
    flat = extended_low.reshape(seqs * (count + HALO), width)
    proj = [
        nn(flat, weight).reshape(seqs, count + HALO, channels)
        for weight in (query_weight, key_weight, value_weight)
    ]
    normed_in = extended_low[:, HALO:].reshape(rows, width)
    beta = jax.nn.sigmoid(nn(normed_in, beta_weight)).reshape(seqs, count, heads)
    gate_proj = nn(normed_in, gate_weight).reshape(seqs, count, channels)

    extended_ids = jnp.concatenate([edge_ids, segments], axis=1)
    masks = [(extended_ids[:, tap : tap + count] == segments) for tap in range(3)]
    enter = segments == edge_ids[:, 2:3]
    last = segments == segments[:, count - 1 :]
    zero = jnp.zeros_like(segments)
    info = jnp.stack(
        [mask.astype(f32) for mask in masks] + [enter.astype(f32), last.astype(f32), segments, zero, zero], axis=1
    )
    taps = conv_weight.reshape(3, 4, channels)
    gain = head_gain[None, :]

    (query, key, value, inverse, fresh, carry, local_mix, reach, state_end, transit, both) = pl_forward(
        proj, taps, info, beta, 2 if heads % 2 == 0 else 1, heads, seqs, count, size, channels
    )
    boths = [shifted(both, "seq", hop) for hop in range(1, hops)]
    farthest = shifted(state_end, "seq", hops)
    back_transits = [shifted(transit, "seq", -hop) for hop in range(1, hops)]
    full_grad = in_order(grad_output, other_grad, 2).reshape(rows, width)
    down_grad = full_grad.astype(bf16)
    inner_grad = nt(down_grad, feed_down)
    boths, farthest, back_transits, full_grad, down_grad, inner_grad = together(
        boths, farthest, back_transits, full_grad, down_grad, inner_grad
    )
    state, mix, gated, part = pl_read(
        boths, farthest, local_mix, reach, gate_proj, gain, out_weight, heads, seqs, count, size, width
    )
    gated = gated.reshape(rows, channels)
    flat_input = full_input.reshape(rows, width)
    middle = flat_input + (part + swapped(part))
    middle_scale = rms_scale(middle)
    middle_normed = middle * middle_scale
    normed_mid = (middle_normed * feed_gain).astype(bf16)
    gate_act = nn(normed_mid, feed_gate)
    up_act = nn(normed_mid, feed_up)
    gate_sig = jax.nn.sigmoid(gate_act)
    gate_silu = gate_act * gate_sig
    inner = (gate_silu * up_act).astype(bf16)
    cut = feed_down.shape[0] // 256 * 128
    gate_grad = (inner_grad * up_act * (gate_sig * (1.0 + gate_act * (1.0 - gate_sig)))).astype(bf16)
    up_grad = (inner_grad * gate_silu).astype(bf16)
    place = lax.axis_index("seq")
    bits = jnp.stack([place & 1, (place >> 1) & 1]).astype(jnp.int32)
    mid_part = nt(gate_grad, feed_gate) + nt(up_grad, feed_up)
    mid_part, late_inner = together(mid_part, inner)
    mid_other = swapped(mid_part)
    down_sums = weight_grads(
        bits, down_grad, late_inner, down_grad, late_inner, slice(0, cut), slice(cut, inner.shape[1])
    )
    down_sums, mid_part = together(down_sums, mid_part)
    down_sums = first_swap(down_sums)
    mine = lax.axis_index("head")
    middle_grad, mixer_grad, feed_gain_grad, mix_grad, gate_low, gain_grad, pull = pl_gate_back(
        mid_part, mid_other, full_grad, middle, feed_gain[None, :], out_weight, mix, gate_proj, gain, reach,
        heads, seqs, count, size,
    )
    grad_feed_gain = jnp.sum(feed_gain_grad, axis=0)
    gate_low = gate_low.reshape(rows, channels)
    pull, late_gate, late_up, late_gated, late_low = together(pull, gate_grad, up_grad, gated, gate_low)
    pulls = from_ahead(pull, hops)
    halves = slice(0, cut), slice(cut, inner.shape[1])
    gate_sums = weight_grads(bits, normed_mid, late_gate, normed_mid, late_gate, *halves)
    out_joined = paired_grads(mixer_grad, late_gated, normed_in, late_low)
    down_sums, gate_sums, out_joined, late_up = together(down_sums, gate_sums, out_joined, late_up)
    if by_bits():
        out_joined = lax.psum_scatter(out_joined, "dp", scatter_dimension=0, tiled=True)
    down_half = list(fold(bits, down_sums))
    down_half[1], late_up = together(down_half[1], late_up)
    up_sums = weight_grads(bits, normed_mid, late_up, normed_mid, late_up, *halves)

    leaving = list(down_half)
    pulls, gate_sums, mix_grad, down_half[1], up_sums = together(pulls, gate_sums, mix_grad, down_half[1], up_sums)
    if relayed(hops):
        pulls = [pulls[0] + lax.ppermute(pulls[1], "seq", [(0, 1)]), pulls[1]]
    leaving[1] = down_half[1]
    down_sums = second_swap(leaving)
    gate_sums = first_swap(gate_sums)
    query_grad, key_grad, value_grad, edge, taps_grad, logit_grad = pl_backward(
        pulls, back_transits, proj, taps, info, beta,
        (query, key, value, inverse, fresh, carry), mix_grad, state, heads, seqs, count, size,
    )
    edge, up_sums, late_inner = together(edge, up_sums, inner)
    down_part = nn(late_inner, feed_down)
    down_out = lax.dynamic_slice_in_dim(down_part, (1 - mine) * half, half, 1)
    edge = shifted(edge, "seq", -1)
    up_sums = first_swap(up_sums)

    gate_sums, edge, down_sums, query_grad, key_grad, value_grad, logit_grad, taps_grad = together(
        gate_sums, edge, down_sums, query_grad, key_grad, value_grad, logit_grad, taps_grad
    )
    query_grad, key_grad, value_grad = (
        (grad + jnp.pad(edge[kind], ((0, 0), (count - 8, 0), (0, 0)))).astype(bf16).reshape(rows, channels)
        for kind, grad in enumerate((query_grad, key_grad, value_grad))
    )
    third = channels // 2
    first_grads = jnp.concatenate([query_grad, value_grad[:, :third]], axis=1)
    second_grads = jnp.concatenate([key_grad, value_grad[:, third:]], axis=1)
    mixed_sums = weight_grads(bits, normed_in, first_grads, normed_in, second_grads)
    beta_low = logit_grad.astype(bf16).reshape(rows, heads)
    down_joined = join(bits, down_sums)
    mixed_sums, gate_sums, up_sums, out_joined, down_joined, down_part, down_out = together(
        mixed_sums, gate_sums, up_sums, out_joined, down_joined, down_part, down_out
    )
    sums_down = last_sum(down_joined)
    feed_half = fold_two(bits, tuple(gate_sums), tuple(up_sums))
    mixed_sums, feed_half, first_grads, second_grads = together(mixed_sums, feed_half, first_grads, second_grads)
    in_part = pl_input_back(
        (first_grads, second_grads, gate_low, beta_low),
        (query_weight, key_weight, value_weight, gate_weight, beta_weight),
    )
    feed_sums = second_swap(feed_half)
    mixed_sums = first_swap(mixed_sums)
    block_output = own_half(middle, half) + (own_half(down_part, half) + swapped(down_out))
    grad_beta = tn(normed_in, beta_low)
    head_part = jnp.sum(gain_grad, axis=0)
    head_part = head_part + swapped(head_part)
    blocks = lax.axis_size("dp") * lax.axis_size("seq")
    taps_piece = taps_grad.reshape(12 * heads, blocks, size // blocks).transpose(1, 0, 2).reshape(blocks, -1)
    feed_sums, block_output, grad_beta, head_part, taps_piece, in_part = together(
        feed_sums, block_output, grad_beta, head_part, taps_piece, in_part
    )
    feed_joined = join(bits, feed_sums, 2)
    sums_feed = last_sum(feed_joined)
    mixed_sums, sums_down = together(mixed_sums, sums_down, feed_joined)[:2]
    mixed_half = fold(bits, mixed_sums)
    mixed_sums = second_swap(mixed_half)
    mixed_joined = join(bits, mixed_sums)
    mixed_joined, out_joined, in_part, sums_feed = together(mixed_joined, out_joined, in_part, sums_feed)
    sums_mixed = last_sum(mixed_joined)
    input_grad, mixer_gain_grad = pl_input_norm(
        mine[None].astype(jnp.int32), in_part, swapped(in_part), flat_input, middle_grad, mixer_gain[None, :], rows // 64
    )

    out_joined = swap_add(swap_add(out_joined, 0), 1)
    grad_mixer_gain = jnp.sum(mixer_gain_grad, axis=0)

    pieces = [
        grad_mixer_gain.reshape(blocks, -1),
        grad_feed_gain.reshape(blocks, -1),
        grad_beta.reshape(blocks, -1),
        taps_piece,
        head_part.reshape(blocks, -1),
    ]
    small = jnp.concatenate(pieces, axis=1)
    small = jnp.pad(small, ((0, 0), (0, -small.shape[1] % 1024)))
    small = small.reshape(blocks, -1, 128)
    if by_bits():
        small = small_sum(small_sum(small, "dp"), "seq")
    else:
        small = small_sum(small, ("dp", "seq"))
    small = small.reshape(-1)
    if by_bits():
        out_joined = out_joined.reshape(-1, out_joined.shape[-1])
    else:
        out_joined = lax.psum_scatter(out_joined, ("dp", "seq"), scatter_dimension=0, tiled=True)
    cuts, at = [], 0
    for piece in pieces:
        cuts.append(small[at : at + piece.shape[1]])
        at += piece.shape[1]
    shape = (seqs, count, half)
    hidden = feed_gate.shape[1]
    wide = channels + third
    return (
        block_output.reshape(shape),
        input_grad.reshape(shape),
        cuts[0],
        sums_mixed[:, :channels],
        sums_mixed[:, wide : wide + channels],
        jnp.concatenate([sums_mixed[:, channels:wide], sums_mixed[:, wide + channels :]], axis=1),
        out_joined[:, channels:],
        cuts[2].reshape(-1, heads),
        cuts[3].reshape(3, 4, heads, size // blocks),
        cuts[4],
        out_joined[:, :channels].T,
        cuts[1],
        sums_feed[:, :hidden],
        sums_feed[:, hidden:],
        sums_down.T,
    )


def solution(mesh):
    return jax.shard_map(
        local,
        mesh=mesh,
        in_specs=(
            P("dp", "seq", "head"),
            P("dp", "seq"),
            P(),
            P(None, "head"),
            P(None, "head"),
            P(None, "head"),
            P(None, "head"),
            P(None, "head"),
            P(None, None, "head", None),
            P(),
            P("head", None),
            P(),
            P(None, "head"),
            P(None, "head"),
            P("head", None),
            P("dp", "seq", "head"),
        ),
        out_specs=(
            P("dp", "seq", "head"),
            P("dp", "seq", "head"),
            P(("dp", "seq")),
            P(("dp", "seq"), "head"),
            P(("dp", "seq"), "head"),
            P(("dp", "seq"), "head"),
            P(("dp", "seq"), "head"),
            P(("dp", "seq"), "head"),
            P(None, None, "head", ("dp", "seq")),
            P(("dp", "seq")),
            P("head", ("dp", "seq")),
            P(("dp", "seq")),
            P(("dp", "seq"), "head"),
            P(("dp", "seq"), "head"),
            P("head", ("dp", "seq")),
        ),
        check_vma=False,
    )
```
